32 devices in a mesh: win: 2 (over y), gz: 4 (over z), gy: 2 (over x), gx: 2 (over core).
Axes of the slice: x: 2, y: 2, z: 4, core: 2. Of those that a mesh axis runs over, the one named last changes fastest.
Arguments:
- noisy: float32 [32, 16, 256], P(('win', 'gz'), 'gy', 'gx'), parts along dimension 0, may hold values from -6 to 6
- first_weight: float32 [32, 1, 27], replicated, may hold values from -1.25 to 1.25
- first_bias: float32 [16], replicated, may hold values from -8 to -3
- second_weight: float32 [32, 16, 27], replicated, may hold values from -0.3125 to 0.3125
- second_bias: float32 [16], replicated, may hold values from -8 to -3
- head_weight: float32 [16], replicated, may hold values from -18 to 18
- seg_weight_in: float32 [16, 1, 27], replicated, may hold values from -1.25 to 1.25
- seg_bias_in: float32 [16], replicated, may hold values from -3 to 3
- seg_weight_out: float32 [16, 16, 27], replicated, may hold values from -0.3125 to 0.3125
- seg_bias_out: float32 [16], replicated, may hold values from -3 to 3
Outputs:
- denoised: float32 [32, 16, 256], P(('win', 'gz'), 'gy', 'gx'), parts along dimension 0
- segmented: float32 [16, 32, 16, 256], P(None, ('win', 'gz'), 'gy', 'gx'), parts along dimension 1
The draws below stay inside these ranges and needn't reach their ends.
There are 2 independent parts, one for each index of `win`. The reference program is written for one: setup_inputs(seed, part) draws one part's arguments, and reference() takes and returns one part's arrays. A program takes and returns all parts, laid end to end along the dimension named above; an argument that names none is the same for every part. Nothing has to cross between parts.
All inputs are finite; a program needn't handle non-finite values.
Results may differ from the reference program's by a relative error of at most 0.00029.
Values sent between devices are 32-bit elements; how exact they have to be, the bound alone decides.
A program may use at most 64 MiB of HBM per device.

```python
import jax
import jax.numpy as jnp
from jax import lax

C = 16
TAPS = 27
NZ = 16
NY = 16
NX = 256


def level_of(key, shape, pieces, low, high):
    level = 1.0
    for dim, shards_of in pieces:
        steps = jax.random.uniform(jax.random.fold_in(jax.random.fold_in(key, 6), dim), (shards_of,), jnp.float32, low / len(pieces), high / len(pieces))
        level = level * jnp.repeat(jnp.exp(steps), shape[dim] // shards_of).reshape((-1,) + (1,) * (len(shape) - 1 - dim))
    return level


def noise(stream_key, extent, width, limit, cuts=(), kind=jnp.bfloat16):
    drawn = jax.random.normal(stream_key, extent, jnp.float32) * width
    if len(cuts) > 0:
        drawn = level_of(stream_key, extent, cuts, -0.22, 0.18) * drawn
    return jnp.clip(drawn, min=-limit, max=limit).astype(kind)


def setup_inputs(seed: int = 0, part: int = 0) -> dict:
    key_of = jax.random.split(jax.random.key(seed), 11)
    part_splits = jax.random.split(jax.random.fold_in(key_of[10], part), 11)
    noisy = noise(part_splits[0], (NZ, NY, NX), 1.0, 6.0, ((0, 4), (1, 2), (2, 2)), jnp.float32)
    first_weight = noise(key_of[1], (2 * C, 1, TAPS), TAPS ** -0.5, 1.25, (), jnp.float32)
    first_bias = jnp.clip(jax.random.uniform(key_of[2], (C,), jnp.float32, -8.0, -3.0), -8.0, -3.0)
    second_weight = noise(key_of[3], (2 * C, C, TAPS), (C * TAPS) ** -0.5, 0.3125, (), jnp.float32)
    second_bias = jnp.clip(jax.random.uniform(key_of[4], (C,), jnp.float32, -8.0, -3.0), -8.0, -3.0)
    head_weight = noise(key_of[5], (C,), 3.0, 18.0, (), jnp.float32)
    seg_weight_in = noise(key_of[6], (C, 1, TAPS), TAPS ** -0.5, 1.25, (), jnp.float32)
    seg_bias_in = noise(key_of[7], (C,), 0.5, 3.0, (), jnp.float32)
    seg_weight_out = noise(key_of[8], (C, C, TAPS), (C * TAPS) ** -0.5, 0.3125, (), jnp.float32)
    seg_bias_out = noise(key_of[9], (C,), 0.5, 3.0, (), jnp.float32)
    return dict(noisy=noisy, first_weight=first_weight, first_bias=first_bias, second_weight=second_weight, second_bias=second_bias, head_weight=head_weight, seg_weight_in=seg_weight_in, seg_bias_in=seg_bias_in, seg_weight_out=seg_weight_out, seg_bias_out=seg_bias_out)


def convolve(field, weight):
    kernel = weight.reshape(weight.shape[0], weight.shape[1], 3, 3, 3)
    result = lax.conv_general_dilated(field[None], kernel, (1, 1, 1), ((1, 1), (1, 1), (1, 1)), dimension_numbers=("NCDHW", "OIDHW", "NCDHW"), precision=lax.Precision.HIGHEST)
    return result[0]


def recurrent(field, weight, bias, backward):
    channels = bias.shape[0]
    pre = convolve(field, weight)
    cand = jnp.tanh(pre[:channels])
    keep = jax.nn.sigmoid(-(pre[channels:] + bias[:, None, None, None]))
    inject = (1.0 - keep) * cand

    def advance(state, inputs):
        state = inputs[0] * state + inputs[1]
        return state, state

    start = jnp.zeros((channels, field.shape[2], field.shape[3]), jnp.float32)
    _, states = lax.scan(advance, start, (jnp.moveaxis(keep, 1, 0), jnp.moveaxis(inject, 1, 0)), reverse=backward)
    return jnp.moveaxis(states, 0, 1)


def reference(noisy, first_weight, first_bias, second_weight, second_bias, head_weight, seg_weight_in, seg_bias_in, seg_weight_out, seg_bias_out):
    first_hidden = recurrent(noisy[None], first_weight, first_bias, False)
    second_hidden = recurrent(first_hidden, second_weight, second_bias, True)
    denoised = noisy + jnp.einsum("c,czyx->zyx", head_weight, second_hidden, precision=lax.Precision.HIGHEST)
    features = jnp.maximum(convolve(denoised[None], seg_weight_in) + seg_bias_in[:, None, None, None], 0.0)
    segmented = convolve(features, seg_weight_out) + seg_bias_out[:, None, None, None]
    return denoised, segmented
```

```python
import functools

import jax
import jax.numpy as jnp
from jax import lax
from jax.experimental import pallas as pl
from jax.experimental.pallas import tpu as pltpu
from jax.sharding import PartitionSpec as P

LANES = 128
F32 = jnp.float32
BF16 = jnp.bfloat16
MESH = pl.DeviceIdType.MESH


def split(value):
    high = value.astype(BF16)
    return high, (value - high.astype(F32)).astype(BF16)


def left_rows(weight):
    high, low = split(weight)
    return jnp.concatenate([high, high, low], axis=1)


def right_rows(high, low):
    return jnp.concatenate([high, low, high], axis=0)


def mxu(left, right):
    return jnp.dot(left, right, preferred_element_type=F32)


def lane_of(shape):
    return lax.broadcasted_iota(jnp.int32, shape, len(shape) - 1)


def row_of(shape):
    return lax.broadcasted_iota(jnp.int32, shape, 0)


def column(row_ref):
    count = row_ref.shape[1]
    shape = (count, count)
    spread = jnp.broadcast_to(row_ref[...], shape)
    return jnp.sum(jnp.where(row_of(shape) == lane_of(shape), spread, 0.0), axis=1, keepdims=True)


def times(count, step, carry, backward=False):
    if count <= 16:
        for i in range(count):
            carry = step(count - 1 - i if backward else i, carry)
        return carry
    return lax.fori_loop(0, count, lambda i, c: step(count - 1 - i if backward else i, c), carry)


def aligned(start, unit):
    return start if isinstance(start, int) else pl.multiple_of(start, unit)


def matches(left, right):
    return jnp.where(left == right, 1.0, 0.0).astype(BF16)


def spread_narrow(weight, shift):
    taps = weight.shape[1]
    shape = (taps, 48)
    tap, col = row_of(shape), lane_of(shape)
    plane = (tap >= 9).astype(jnp.int32) + (tap >= 18).astype(jnp.int32)
    rest = tap - 9 * plane
    line = (rest >= 3).astype(jnp.int32) + (rest >= 6).astype(jnp.int32)
    place = matches(col, tap + 7 * plane + 2 * line + shift)
    return tuple(mxu(part, place).astype(BF16) for part in split(weight))


def narrow_left(weight):
    parts = weight.shape[0] // 16
    highs, lows = [], []
    for part in range(parts):
        for shift in range(3):
            high, low = spread_narrow(weight[16 * part : 16 * part + 16], shift)
            highs.append(high)
            lows.append(low)
    high, low = jnp.concatenate(highs, axis=0), jnp.concatenate(lows, axis=0)
    return jnp.concatenate([high, high, low], axis=1)


def wide_left(turned):
    flat = turned.T
    taps = flat.shape[1] // 3
    return left_rows(
        jnp.concatenate([flat[:, taps * a : taps * (a + 1)] for a in range(3)], axis=0)
    )


def last_left(weight):
    outs, ins, taps = weight.shape
    shape = (taps, taps * ins)
    place = matches(row_of(shape), lane_of(shape) // ins)
    shape = (outs * ins, taps * ins)
    keep = (row_of(shape) % ins) == (lane_of(shape) % ins)
    shape = (outs, outs * ins)
    gather = matches(row_of(shape), lane_of(shape) // ins)
    parts = []
    for part in split(weight.reshape(outs * ins, taps)):
        grown = jnp.where(keep, mxu(part, place), 0.0).astype(BF16)
        parts.append(mxu(gather, grown).astype(BF16))
    third = taps * ins // 3
    high, low = (
        jnp.concatenate([p[:, third * a : third * (a + 1)] for a in range(3)], axis=0) for p in parts
    )
    return jnp.concatenate([high, high, low], axis=1)


def whole_kernel(
    sizes, bz, by, bx,
    noisy_any, w1_any, b1_any, w2_any, b2_any, head_any, w3_any, b3_any, w4_any, b4_any,
    clean_ref, out_ref,
    noisy_ref, w1_ref, b1_ref, w2_ref, b2_ref, head_ref, w3_ref, b3_ref, w4_ref, b4_ref, load_sem,
    m1, x1, my, xy, halo, m1_send, m1_recv, x1_send, x1_recv,
    wide_taps, taps_high, taps_low, product, fix, packed,
    m3, x3, m3_send, m3_recv, x3_send, x3_recv,
    middle_ref, edge_ref, seg_taps, result,
):
    gz, gy, gx = sizes
    depth = gz * bz
    slab = bx // gz
    out_lanes = by * slab
    tiles = wide_taps.shape[0]
    me = lax.axis_index("gz")
    at_y = lax.axis_index("gy")
    at_x = lax.axis_index("gx")
    low_slab = me == 0
    high_slab = me == gz - 1
    def exists(dy, dx):
        ok = None
        for where, step, count in ((at_y, dy, gy), (at_x, dx, gx)):
            if step == 0:
                continue
            here = where > 0 if step < 0 else where < count - 1
            ok = here if ok is None else ok & here
        return ok

    def when(ok, action):
        if ok is None:
            action()
        else:
            pl.when(ok)(action)

    def device(z, dy, dx):
        return {
            "win": lax.axis_index("win"),
            "gz": z,
            "gy": lax.rem(at_y + dy + gy, gy),
            "gx": lax.rem(at_x + dx + gx, gx),
        }

    def peer(k):
        return lax.rem(me + k, gz)

    steps_y = (0,) + ((-1, 1) if gy > 1 else ())
    steps_x = (0,) + ((-1, 1) if gx > 1 else ())

    def payload(dy):
        return noisy_ref if dy == 0 else halo.at[(dy + 1) // 2]

    def slot(edge, dy, z):
        if dy == 0:
            return (x1 if edge else m1).at[pl.ds(aligned(z * bz * by, bz * by), bz * by), :]
        return (xy if edge else my).at[(dy + 1) // 2, pl.ds(aligned(z * bz * 2, bz * 2), bz * 2), :]

    loads = [
        pltpu.make_async_copy(source, target, load_sem.at[i])
        for i, (source, target) in enumerate(
            (
                (noisy_any, noisy_ref),
                (w1_any.at[:, 0, :], w1_ref),
                (w2_any, w2_ref),
                (w3_any.at[:, 0, :], w3_ref),
                (w4_any, w4_ref),
                (b1_any, b1_ref),
                (b2_any, b2_ref),
                (head_any, head_ref),
                (b3_any, b3_ref),
                (b4_any, b4_ref),
            )
        )
    ]
    loads[0].start()
    barrier = pltpu.get_barrier_semaphore()
    for dy in steps_y:
        for dx in steps_x:
            for k in range(gz):
                if (dy, dx, k) != (0, 0, 0):
                    def greet(dy=dy, dx=dx, k=k):
                        pl.semaphore_signal(
                            barrier, inc=1, device_id=device(peer(k), dy, dx), device_id_type=MESH
                        )
                    when(exists(dy, dx), greet)
    for load in loads[1:]:
        load.start()
    loads[0].wait()
    for side, first in ((0, 0), (1, by - 2)):
        for z in range(noisy_ref.shape[0] // by):
            halo[side, 2 * z : 2 * z + 2, :] = noisy_ref[z * by + first : z * by + first + 2, :]

    span_y = 1 + (at_y > 0).astype(jnp.int32) + (at_y < gy - 1).astype(jnp.int32)
    span_x = 1 + (at_x > 0).astype(jnp.int32) + (at_x < gx - 1).astype(jnp.int32)
    pl.semaphore_wait(barrier, gz * span_y * span_x - 1)

    def noisy_middle(dy, k):
        target = peer(k)
        return pltpu.make_async_remote_copy(
            src_ref=payload(dy),
            dst_ref=slot(False, -dy, me),
            send_sem=m1_send.at[dy + 1, k],
            recv_sem=m1_recv.at[1 - dy, me],
            device_id=device(target, dy, 0),
            device_id_type=MESH,
        )

    def noisy_edge(dy, dx):
        target = 0 if dx > 0 else gz - 1
        side = (dx + 1) // 2
        return pltpu.make_async_remote_copy(
            src_ref=payload(dy),
            dst_ref=slot(True, -dy, me),
            send_sem=x1_send.at[dy + 1, side],
            recv_sem=x1_recv.at[1 - dy, me],
            device_id=device(target, dy, dx),
            device_id_type=MESH,
        )

    sends = []
    for dy in steps_y:
        for k in range(gz - 1, -1, -1):
            if (dy, k) != (0, 0):
                sends.append((exists(dy, 0), functools.partial(noisy_middle, dy, k)))
    for dy in steps_y:
        for dx in steps_x:
            if dx != 0:
                sends.append((exists(dy, dx), functools.partial(noisy_edge, dy, dx)))
    for ok, make in sends:
        when(ok, lambda make=make: make().start())

    m1[pl.ds(aligned(me * bz * by, bz * by), bz * by), :] = noisy_ref[...]
    for index, ok in ((0, at_y == 0), (1, at_y == gy - 1)):
        def no_row(index=index):
            my[index] = jnp.zeros(my.shape[1:], F32)
            xy[index] = jnp.zeros(xy.shape[1:], F32)
        pl.when(ok)(no_row)
    no_edge = jnp.logical_not((low_slab & (at_x > 0)) | (high_slab & (at_x < gx - 1)))

    def no_neighbour():
        x1[...] = jnp.zeros(x1.shape, F32)
        xy[...] = jnp.zeros(xy.shape, F32)

    pl.when(no_edge)(no_neighbour)
    for load in loads[1:]:
        load.wait()
    wide_taps[...] = jnp.zeros(wide_taps.shape, F32)
    for plane in (0, depth + 1):
        product[plane] = jnp.zeros(product.shape[1:], F32)
    fix[...] = jnp.zeros(fix.shape, F32)
    turned = w1_ref[...].T
    first_left = narrow_left(turned)
    second_left = wide_left(w2_ref[...].reshape(-1, w2_ref.shape[2]))
    in_left = narrow_left(w3_ref[...])
    out_left = last_left(w4_ref[...])
    in_bias = jnp.concatenate([column(b3_ref)] * 3, axis=0)
    out_bias = column(b4_ref)
    first_bias = jnp.concatenate([column(b1_ref)] * 3, axis=0)
    second_bias = column(b2_ref)
    head = column(head_ref)
    shape = (48, tiles * LANES)
    lane, row = lane_of(shape), row_of(shape)
    place_y = at_y * by + lane // slab - 1
    place_x = at_x * bx + me * slab + lane % slab + row // 16 - 1
    inside = (place_y >= 0) & (place_y < gy * by) & (place_x >= 0) & (place_x < gx * bx)
    mask = jnp.where(inside, 1.0, 0.0).astype(F32)

    for dy in steps_y:
        for k in range(gz):
            if (dy, k) != (0, 0):
                source = peer(k)
                def await_middle(dy=dy, source=source):
                    pltpu.make_async_remote_copy(
                        src_ref=payload(dy),
                        dst_ref=slot(False, dy, source),
                        send_sem=m1_send.at[1 + dy, 0],
                        recv_sem=m1_recv.at[1 + dy, source],
                        device_id=device(source, dy, 0),
                        device_id_type=MESH,
                    ).wait_recv()
                when(exists(dy, 0), await_middle)
    for dy in steps_y:
        for dx in steps_x:
            if dx != 0:
                ok = exists(dy, dx) & (low_slab if dx < 0 else high_slab)
                for source in range(gz):
                    def await_edge(dy=dy, dx=dx, source=source):
                        pltpu.make_async_remote_copy(
                            src_ref=payload(dy),
                            dst_ref=slot(True, dy, source),
                            send_sem=x1_send.at[1 + dy, 0],
                            recv_sem=x1_recv.at[1 + dy, source],
                            device_id=device(source, dy, dx),
                            device_id_type=MESH,
                        ).wait_recv()
                    pl.when(ok)(await_edge)

    lane = lane_of((depth, LANES))
    take_edge = (low_slab & (lane >= bx - 2)) | (high_slab & (lane < 2))
    windows = []
    turn = lax.rem(2 - me * slab + bx, bx)
    for line in range(by + 4):
        rows = []
        for source, beside in ((m1, my), (x1, xy)):
            if 2 <= line < by + 2:
                rows.append(source[pl.ds(line - 2, depth, stride=by), :])
            else:
                side, place = (0, line) if line < 2 else (1, line - by - 2)
                rows.append(beside[side, pl.ds(place, depth, stride=2), :])
        windows.append(pltpu.roll(jnp.where(take_edge, rows[1], rows[0]), turn, 1))
    wide_tiles = -(-(by + 4) * slab // LANES)
    for s in range(5):
        strips = []
        for tile in range(wide_tiles):
            strip = jnp.zeros((depth, LANES), F32)
            for line in range(by + 4):
                if line * slab // LANES == tile:
                    begin = line * slab % LANES
                    piece = pltpu.roll(windows[line], (begin - s) % LANES, 1)
                    strip = jnp.where((lane >= begin) & (lane < begin + slab), piece, strip)
            strips.append(strip)
        strips.append(jnp.zeros((depth, LANES), F32))
        for b in range(3):
            for tile in range(tiles):
                jump, off = divmod(b * slab, LANES)
                value = strips[min(tile + jump, wide_tiles)]
                if off:
                    after = strips[min(tile + jump + 1, wide_tiles)]
                    value = jnp.where(
                        lane < LANES - off,
                        pltpu.roll(value, LANES - off, 1),
                        pltpu.roll(after, LANES - off, 1),
                    )
                wide_taps[tile, pl.ds(16 + b * 5 + s, depth, stride=16), :] = value
    high, low = split(wide_taps[...])
    taps_high[...] = high
    taps_low[...] = low

    def forward(z, hidden):
        rows = pl.ds(aligned(z * 16, 16), 48)
        high = jnp.concatenate([taps_high[t, rows, :] for t in range(tiles)], axis=1)
        low = jnp.concatenate([taps_low[t, rows, :] for t in range(tiles)], axis=1)
        pre = mxu(first_left, right_rows(high, low))
        cand = jnp.tanh(pre[0:48])
        change = jax.nn.sigmoid(pre[48:96] + first_bias)
        hidden = hidden + change * (mask * cand - hidden)
        field = jnp.concatenate(
            [hidden[:, b * slab : b * slab + out_lanes] for b in range(3)], axis=0
        )
        high, low = split(field)
        product[z + 1] = mxu(second_left, right_rows(high, low))
        return hidden

    times(depth, forward, jnp.zeros((48, tiles * LANES), F32))

    def back(z, hidden):
        pre = product[z, 0:32] + product[z + 1, 32:64] + product[z + 2, 64:96]
        cand = jnp.tanh(pre[0:16])
        change = jax.nn.sigmoid(pre[16:32] + second_bias)
        hidden = hidden + change * (cand - hidden)
        fix[pl.ds(z + 2, 1), 0:out_lanes] = jnp.sum(head * hidden, axis=0, keepdims=True)
        return hidden

    times(depth, back, jnp.zeros((16, out_lanes), F32), True)
    for tile in range(-(-out_lanes // LANES)):
        lanes = slice(tile * LANES, (tile + 1) * LANES)
        centre = wide_taps[tile, pl.ds(16 + 12, depth, stride=16), :]
        fix[2 : 2 + depth, lanes] = fix[2 : 2 + depth, lanes] + centre
    for target in range(gz):
        packed[target] = fix[bz * target : bz * target + bz + 4, :]


    wide = packed.shape[2]
    last = (by - 2) * slab // LANES * LANES

    def part(dy):
        return {0: slice(0, wide), 1: slice(last, last + LANES), -1: slice(0, LANES)}[dy]

    def clean_middle(dy, k):
        target = peer(k)
        return pltpu.make_async_remote_copy(
            src_ref=packed.at[target, :, part(dy)],
            dst_ref=m3.at[1 - dy, me, :, part(dy)],
            send_sem=m3_send.at[dy + 1, k],
            recv_sem=m3_recv.at[1 - dy, me],
            device_id=device(target, dy, 0),
            device_id_type=MESH,
        )

    def clean_edge(dy, dx, k):
        target = peer(k)
        side = (dx + 1) // 2
        return pltpu.make_async_remote_copy(
            src_ref=packed.at[target, :, part(dy)],
            dst_ref=x3.at[1 - dy, 1 - side, :, part(dy)],
            send_sem=x3_send.at[dy + 1, side, k],
            recv_sem=x3_recv.at[1 - dy, 1 - side],
            device_id=device(target, dy, dx),
            device_id_type=MESH,
        )

    late = []
    for dy in steps_y:
        for k in range(gz - 1, -1, -1):
            if (dy, k) != (0, 0):
                late.append((exists(dy, 0), functools.partial(clean_middle, dy, k)))
    for dy in steps_y:
        for dx in steps_x:
            if dx != 0:
                ok = exists(dy, dx) & (high_slab if dx > 0 else low_slab)
                for k in range(gz):
                    late.append((ok, functools.partial(clean_edge, dy, dx, k)))
    for ok, make in late:
        when(ok, lambda make=make: make().start())
    m3[1, me] = packed[me]
    for index, ok in ((0, at_y == 0), (2, at_y == gy - 1)):
        def no_row_again(index=index):
            m3[index] = jnp.zeros(m3.shape[1:], F32)
            x3[index] = jnp.zeros(x3.shape[1:], F32)
        pl.when(ok)(no_row_again)
    for side, ok in ((0, at_x == 0), (1, at_x == gx - 1)):
        def no_side(side=side):
            for index in range(3):
                x3[index, side] = jnp.zeros(x3.shape[2:], F32)
        pl.when(ok)(no_side)
    for dy in steps_y:
        for k in range(gz):
            if (dy, k) != (0, 0):
                source = peer(k)
                def await_clean(dy=dy, source=source):
                    pltpu.make_async_remote_copy(
                        src_ref=packed.at[0, :, part(-dy)],
                        dst_ref=m3.at[1 + dy, source, :, part(-dy)],
                        send_sem=m3_send.at[1 + dy, 0],
                        recv_sem=m3_recv.at[1 + dy, source],
                        device_id=device(source, dy, 0),
                        device_id_type=MESH,
                    ).wait_recv()
                when(exists(dy, 0), await_clean)
    for dy in steps_y:
        for dx in steps_x:
            if dx != 0:
                side = (dx + 1) // 2
                source = gz - 1 if dx < 0 else 0
                def await_side(dy=dy, dx=dx, side=side, source=source):
                    pltpu.make_async_remote_copy(
                        src_ref=packed.at[0, :, part(-dy)],
                        dst_ref=x3.at[1 + dy, side, :, part(-dy)],
                        send_sem=x3_send.at[1 + dy, side, 0],
                        recv_sem=x3_recv.at[1 + dy, side],
                        device_id=device(source, dy, dx),
                        device_id_type=MESH,
                    ).wait_recv()
                when(exists(dy, dx), await_side)

    lines, planes = by + 4, bz + 4
    slab = bx // gz
    lane = lane_of((bz + 4, LANES))
    for line in range(by + 4):
        index, y = (0, by - 2 + line) if line < 2 else (1, line - 2) if line < by + 2 else (2, line - by - 2)
        tile, off = divmod(y * slab, LANES)
        lanes = slice(tile * LANES, (tile + 1) * LANES)
        whole = jnp.zeros((bz + 4, LANES), F32)
        for source in range(gz):
            begin = source * slab
            piece = pltpu.roll(m3[index, source, :, lanes], (begin - off) % LANES, 1)
            whole = jnp.where((lane >= begin) & (lane < begin + slab), piece, whole)
        middle_ref[line] = whole
        before = pltpu.roll(x3[index, 0, :, lanes], (bx - off - slab) % LANES, 1)
        after = pltpu.roll(x3[index, 1, :, lanes], (-off) % LANES, 1)
        edge_ref[line] = jnp.where(lane < LANES // 2, after, before)

    for y in range(by + 2):
        seg_taps[y, pl.ds(15, planes, stride=16), :] = jnp.zeros((planes, bx), F32)
    lane = lane_of((planes, bx))
    for line in range(lines):
        middle, edge = middle_ref[line], edge_ref[line]
        for s in range(5):
            value = middle
            if s < 2:
                value = pltpu.roll(jnp.where(lane >= bx - (2 - s), edge, middle), 2 - s, 1)
            if s > 2:
                value = pltpu.roll(jnp.where(lane < s - 2, edge, middle), bx - (s - 2), 1)
            for b in range(3):
                if 0 <= line - b < by + 2:
                    seg_taps[line - b, pl.ds(b * 5 + s, planes, stride=16), :] = value

    for z in range(bz):
        clean_ref[z] = middle_ref[2 : 2 + by, 2 + z, :]
    shape = (48, (by + 2) * bx)
    lane, row = lane_of(shape), row_of(shape)
    place_y = at_y * by + lane // bx - 1
    place_x = at_x * bx + lane % bx + row // 16 - 1
    inside = (place_y >= 0) & (place_y < gy * by) & (place_x >= 0) & (place_x < gx * bx)
    mask = jnp.where(inside, 1.0, 0.0).astype(F32)
    partial = []
    for z in range(bz + 2):
        rows = jnp.concatenate([seg_taps[y, z * 16 : z * 16 + 48, :] for y in range(by + 2)], axis=1)
        high, low = split(rows)
        grown = jnp.maximum(mxu(in_left, right_rows(high, low)) + in_bias, 0.0) * mask
        if z == 0:
            grown = grown * jnp.where(me > 0, 1.0, 0.0).astype(F32)
        if z == bz + 1:
            grown = grown * jnp.where(me < gz - 1, 1.0, 0.0).astype(F32)
        high, low = split(grown)
        field_high = jnp.concatenate([high[:, b * bx : (b + by) * bx] for b in range(3)], axis=0)
        field_low = jnp.concatenate([low[:, b * bx : (b + by) * bx] for b in range(3)], axis=0)
        partial.append(mxu(out_left, right_rows(field_high, field_low)))
        if z >= 2:
            total = partial[z - 2][0:16] + partial[z - 1][16:32] + partial[z][32:48] + out_bias
            for y in range(by):
                result[pl.ds((z - 2) * by + y, 16, stride=bz * by), :] = total[:, y * bx : (y + 1) * bx]
    out_ref[...] = result[0 : 16 * bz * by, :]
    for ok, make in sends:
        when(ok, lambda make=make: make().wait_send())
    for ok, make in late:
        when(ok, lambda make=make: make().wait_send())


def body(sizes, noisy, first_weight, first_bias, second_weight, second_bias, head_weight,
         seg_weight_in, seg_bias_in, seg_weight_out, seg_bias_out):
    gz, gy, gx = sizes
    bz, by, bx = noisy.shape
    depth = gz * bz
    slab = bx // gz
    tiles = -(-(by + 2) * slab // LANES)
    out_lanes = by * slab
    out_tiles = -(-out_lanes // LANES)
    lanes = out_tiles * LANES
    args = [
        noisy.reshape(bz * by, bx),
        first_weight.transpose(2, 1, 0),
        first_bias.reshape(1, -1),
        second_weight.transpose(2, 1, 0),
        second_bias.reshape(1, -1),
        head_weight.reshape(1, -1),
        seg_weight_in,
        seg_bias_in.reshape(1, -1),
        seg_weight_out,
        seg_bias_out.reshape(1, -1),
    ]
    vmem = pl.BlockSpec(memory_space=pltpu.VMEM)
    dma = pltpu.SemaphoreType.DMA
    rest = pl.BlockSpec(memory_space=pl.ANY)

    def room(*shape):
        return pltpu.VMEM(shape, F32)

    stages = [
        room(*(a.shape if i not in (1, 6) else (a.shape[0], a.shape[2]))) for i, a in enumerate(args)
    ]
    clean, features = pl.pallas_call(
        functools.partial(whole_kernel, sizes, bz, by, bx),
        out_shape=[
            jax.ShapeDtypeStruct((bz, by, bx), F32),
            jax.ShapeDtypeStruct((16 * bz * by, bx), F32),
        ],
        in_specs=[rest] * len(args),
        out_specs=[vmem] * 2,
        scratch_shapes=stages
        + [
            dma((len(args),)),
            room(depth * by, bx),
            room(depth * by, bx),
            room(2, depth * 2, bx),
            room(2, depth * 2, bx),
            room(2, bz * 2, bx),
            dma((3, gz)),
            dma((3, gz)),
            dma((3, 2)),
            dma((3, gz)),
            room(tiles, (depth + 2) * 16, LANES),
            pltpu.VMEM((tiles, (depth + 2) * 16, LANES), BF16),
            pltpu.VMEM((tiles, (depth + 2) * 16, LANES), BF16),
            room(depth + 2, 96, out_lanes),
            room(depth + 16, lanes),
            room(gz, bz + 4, lanes),
            room(3, gz, bz + 4, lanes),
            room(3, 2, bz + 4, lanes),
            dma((3, gz)),
            dma((3, gz)),
            dma((3, 2, gz)),
            dma((3, 2)),
            room(by + 4, bz + 4, bx),
            room(by + 4, bz + 4, bx),
            room(by + 2, (bz + 5) * 16, bx),
            room(17 * bz * by, bx),
        ],
        compiler_params=pltpu.CompilerParams(collective_id=0, has_side_effects=True),
        name="whole",
    )(*args)
    return clean, features.reshape(16, bz, by, bx)


def solution(mesh):
    sizes = (mesh.shape["gz"], mesh.shape["gy"], mesh.shape["gx"])
    in_specs = (P(("win", "gz"), "gy", "gx"), P(), P(), P(), P(), P(), P(), P(), P(), P())
    out_specs = (P(("win", "gz"), "gy", "gx"), P(None, ("win", "gz"), "gy", "gx"))
    return jax.shard_map(
        functools.partial(body, sizes), mesh=mesh, in_specs=in_specs, out_specs=out_specs, check_vma=False
    )
```

```python
import functools

import jax
import jax.numpy as jnp
from jax import lax
from jax.experimental import pallas as pl
from jax.experimental.pallas import tpu as pltpu
from jax.sharding import PartitionSpec as P

LANES = 128
GRANT = 40 << 20
F32 = jnp.float32
BF16 = jnp.bfloat16
MESH = pl.DeviceIdType.MESH


def split(value):
    high = value.astype(BF16)
    return high, (value - high.astype(F32)).astype(BF16)


def left_rows(weight):
    high, low = split(weight)
    return jnp.concatenate([high, high, low], axis=1)


def right_rows(high, low):
    return jnp.concatenate([high, low, high], axis=0)


def mxu(left, right):
    return jnp.dot(left, right, preferred_element_type=F32)


def lane_of(shape):
    return lax.broadcasted_iota(jnp.int32, shape, len(shape) - 1)


def row_of(shape):
    return lax.broadcasted_iota(jnp.int32, shape, 0)


def column(row_ref):
    count = row_ref.shape[1]
    shape = (count, count)
    spread = jnp.broadcast_to(row_ref[...], shape)
    return jnp.sum(jnp.where(row_of(shape) == lane_of(shape), spread, 0.0), axis=1, keepdims=True)


def times(count, step, carry, backward=False):
    if count <= 16:
        for i in range(count):
            carry = step(count - 1 - i if backward else i, carry)
        return carry
    return lax.fori_loop(0, count, lambda i, c: step(count - 1 - i if backward else i, c), carry)


def aligned(start, unit):
    return start if isinstance(start, int) else pl.multiple_of(start, unit)


def matches(left, right):
    return jnp.where(left == right, 1.0, 0.0).astype(BF16)


def spread_narrow(weight, shift):
    taps = weight.shape[1]
    shape = (taps, 48)
    tap, col = row_of(shape), lane_of(shape)
    plane = (tap >= 9).astype(jnp.int32) + (tap >= 18).astype(jnp.int32)
    rest = tap - 9 * plane
    line = (rest >= 3).astype(jnp.int32) + (rest >= 6).astype(jnp.int32)
    place = matches(col, tap + 7 * plane + 2 * line + shift)
    return tuple(mxu(part, place).astype(BF16) for part in split(weight))


def narrow_left(weight):
    parts = weight.shape[0] // 16
    highs, lows = [], []
    for part in range(parts):
        for shift in range(3):
            high, low = spread_narrow(weight[16 * part : 16 * part + 16], shift)
            highs.append(high)
            lows.append(low)
    high, low = jnp.concatenate(highs, axis=0), jnp.concatenate(lows, axis=0)
    return jnp.concatenate([high, high, low], axis=1)


def wide_left(turned):
    flat = turned.T
    taps = flat.shape[1] // 3
    return left_rows(
        jnp.concatenate([flat[:, taps * a : taps * (a + 1)] for a in range(3)], axis=0)
    )


def last_left(weight):
    outs, ins, taps = weight.shape
    shape = (taps, taps * ins)
    place = matches(row_of(shape), lane_of(shape) // ins)
    shape = (outs * ins, taps * ins)
    keep = (row_of(shape) % ins) == (lane_of(shape) % ins)
    shape = (outs, outs * ins)
    gather = matches(row_of(shape), lane_of(shape) // ins)
    parts = []
    for part in split(weight.reshape(outs * ins, taps)):
        grown = jnp.where(keep, mxu(part, place), 0.0).astype(BF16)
        parts.append(mxu(gather, grown).astype(BF16))
    third = taps * ins // 3
    high, low = (
        jnp.concatenate([p[:, third * a : third * (a + 1)] for a in range(3)], axis=0) for p in parts
    )
    return jnp.concatenate([high, high, low], axis=1)


def layers_kernel(
    sizes, bz, by, bx,
    noisy_any, w1_any, b1_any, w2_any, b2_any, head_any, w3_any, b3_any, w4_any, b4_any,
    middle_ref, edge_ref, in_left_ref, out_left_ref, in_bias_ref, out_bias_ref,
    noisy_ref, w1_ref, b1_ref, w2_ref, b2_ref, head_ref, w3_ref, b3_ref, w4_ref, b4_ref, load_sem,
    m1, x1, my, xy, halo, m1_send, m1_recv, x1_send, x1_recv,
    wide_taps, taps_high, taps_low, product, fix, packed,
    m3, x3, m3_send, m3_recv, x3_send, x3_recv,
):
    gz, gy, gx = sizes
    depth = gz * bz
    slab = bx // gz
    out_lanes = by * slab
    tiles = wide_taps.shape[0]
    me = lax.axis_index("gz")
    at_y = lax.axis_index("gy")
    at_x = lax.axis_index("gx")
    low_slab = me == 0
    high_slab = me == gz - 1
    def exists(dy, dx):
        ok = None
        for where, step, count in ((at_y, dy, gy), (at_x, dx, gx)):
            if step == 0:
                continue
            here = where > 0 if step < 0 else where < count - 1
            ok = here if ok is None else ok & here
        return ok

    def when(ok, action):
        if ok is None:
            action()
        else:
            pl.when(ok)(action)

    def device(z, dy, dx):
        return {
            "win": lax.axis_index("win"),
            "gz": z,
            "gy": lax.rem(at_y + dy + gy, gy),
            "gx": lax.rem(at_x + dx + gx, gx),
        }

    def peer(k):
        return lax.rem(me + k, gz)

    steps_y = (0,) + ((-1, 1) if gy > 1 else ())
    steps_x = (0,) + ((-1, 1) if gx > 1 else ())

    def payload(dy):
        return noisy_ref if dy == 0 else halo.at[(dy + 1) // 2]

    def slot(edge, dy, z):
        if dy == 0:
            return (x1 if edge else m1).at[pl.ds(aligned(z * bz * by, bz * by), bz * by), :]
        return (xy if edge else my).at[(dy + 1) // 2, pl.ds(aligned(z * bz * 2, bz * 2), bz * 2), :]

    loads = [
        pltpu.make_async_copy(source, target, load_sem.at[i])
        for i, (source, target) in enumerate(
            (
                (noisy_any, noisy_ref),
                (w1_any.at[:, 0, :], w1_ref),
                (w2_any, w2_ref),
                (w3_any.at[:, 0, :], w3_ref),
                (w4_any, w4_ref),
                (b1_any, b1_ref),
                (b2_any, b2_ref),
                (head_any, head_ref),
                (b3_any, b3_ref),
                (b4_any, b4_ref),
            )
        )
    ]
    loads[0].start()
    barrier = pltpu.get_barrier_semaphore()
    for dy in steps_y:
        for dx in steps_x:
            for k in range(gz):
                if (dy, dx, k) != (0, 0, 0):
                    def greet(dy=dy, dx=dx, k=k):
                        pl.semaphore_signal(
                            barrier, inc=1, device_id=device(peer(k), dy, dx), device_id_type=MESH
                        )
                    when(exists(dy, dx), greet)
    for load in loads[1:]:
        load.start()
    loads[0].wait()
    for side, first in ((0, 0), (1, by - 2)):
        for z in range(noisy_ref.shape[0] // by):
            halo[side, 2 * z : 2 * z + 2, :] = noisy_ref[z * by + first : z * by + first + 2, :]

    span_y = 1 + (at_y > 0).astype(jnp.int32) + (at_y < gy - 1).astype(jnp.int32)
    span_x = 1 + (at_x > 0).astype(jnp.int32) + (at_x < gx - 1).astype(jnp.int32)
    pl.semaphore_wait(barrier, gz * span_y * span_x - 1)

    def noisy_middle(dy, k):
        target = peer(k)
        return pltpu.make_async_remote_copy(
            src_ref=payload(dy),
            dst_ref=slot(False, -dy, me),
            send_sem=m1_send.at[dy + 1, k],
            recv_sem=m1_recv.at[1 - dy, me],
            device_id=device(target, dy, 0),
            device_id_type=MESH,
        )

    def noisy_edge(dy, dx):
        target = 0 if dx > 0 else gz - 1
        side = (dx + 1) // 2
        return pltpu.make_async_remote_copy(
            src_ref=payload(dy),
            dst_ref=slot(True, -dy, me),
            send_sem=x1_send.at[dy + 1, side],
            recv_sem=x1_recv.at[1 - dy, me],
            device_id=device(target, dy, dx),
            device_id_type=MESH,
        )

    sends = []
    for dy in steps_y:
        for k in range(gz - 1, -1, -1):
            if (dy, k) != (0, 0):
                sends.append((exists(dy, 0), functools.partial(noisy_middle, dy, k)))
    for dy in steps_y:
        for dx in steps_x:
            if dx != 0:
                sends.append((exists(dy, dx), functools.partial(noisy_edge, dy, dx)))
    for ok, make in sends:
        when(ok, lambda make=make: make().start())

    m1[pl.ds(aligned(me * bz * by, bz * by), bz * by), :] = noisy_ref[...]
    for index, ok in ((0, at_y == 0), (1, at_y == gy - 1)):
        def no_row(index=index):
            my[index] = jnp.zeros(my.shape[1:], F32)
            xy[index] = jnp.zeros(xy.shape[1:], F32)
        pl.when(ok)(no_row)
    no_edge = jnp.logical_not((low_slab & (at_x > 0)) | (high_slab & (at_x < gx - 1)))

    def no_neighbour():
        x1[...] = jnp.zeros(x1.shape, F32)
        xy[...] = jnp.zeros(xy.shape, F32)

    pl.when(no_edge)(no_neighbour)
    for load in loads[1:]:
        load.wait()
    wide_taps[...] = jnp.zeros(wide_taps.shape, F32)
    for plane in (0, depth + 1):
        product[plane] = jnp.zeros(product.shape[1:], F32)
    fix[...] = jnp.zeros(fix.shape, F32)
    turned = w1_ref[...].T
    first_left = narrow_left(turned)
    second_left = wide_left(w2_ref[...].reshape(-1, w2_ref.shape[2]))
    in_left_ref[...] = narrow_left(w3_ref[...])
    out_left_ref[...] = last_left(w4_ref[...])
    in_bias_ref[...] = jnp.broadcast_to(
        jnp.concatenate([column(b3_ref)] * 3, axis=0), in_bias_ref.shape
    )
    out_bias_ref[...] = jnp.broadcast_to(column(b4_ref), out_bias_ref.shape)
    first_bias = jnp.concatenate([column(b1_ref)] * 3, axis=0)
    second_bias = column(b2_ref)
    head = column(head_ref)
    shape = (48, tiles * LANES)
    lane, row = lane_of(shape), row_of(shape)
    place_y = at_y * by + lane // slab - 1
    place_x = at_x * bx + me * slab + lane % slab + row // 16 - 1
    inside = (place_y >= 0) & (place_y < gy * by) & (place_x >= 0) & (place_x < gx * bx)
    mask = jnp.where(inside, 1.0, 0.0).astype(F32)

    for dy in steps_y:
        for k in range(gz):
            if (dy, k) != (0, 0):
                source = peer(k)
                def await_middle(dy=dy, source=source):
                    pltpu.make_async_remote_copy(
                        src_ref=payload(dy),
                        dst_ref=slot(False, dy, source),
                        send_sem=m1_send.at[1 + dy, 0],
                        recv_sem=m1_recv.at[1 + dy, source],
                        device_id=device(source, dy, 0),
                        device_id_type=MESH,
                    ).wait_recv()
                when(exists(dy, 0), await_middle)
    for dy in steps_y:
        for dx in steps_x:
            if dx != 0:
                ok = exists(dy, dx) & (low_slab if dx < 0 else high_slab)
                for source in range(gz):
                    def await_edge(dy=dy, dx=dx, source=source):
                        pltpu.make_async_remote_copy(
                            src_ref=payload(dy),
                            dst_ref=slot(True, dy, source),
                            send_sem=x1_send.at[1 + dy, 0],
                            recv_sem=x1_recv.at[1 + dy, source],
                            device_id=device(source, dy, dx),
                            device_id_type=MESH,
                        ).wait_recv()
                    pl.when(ok)(await_edge)

    lane = lane_of((depth, LANES))
    take_edge = (low_slab & (lane >= bx - 2)) | (high_slab & (lane < 2))
    windows = []
    turn = lax.rem(2 - me * slab + bx, bx)
    for line in range(by + 4):
        rows = []
        for source, beside in ((m1, my), (x1, xy)):
            if 2 <= line < by + 2:
                rows.append(source[pl.ds(line - 2, depth, stride=by), :])
            else:
                side, place = (0, line) if line < 2 else (1, line - by - 2)
                rows.append(beside[side, pl.ds(place, depth, stride=2), :])
        windows.append(pltpu.roll(jnp.where(take_edge, rows[1], rows[0]), turn, 1))
    wide_tiles = -(-(by + 4) * slab // LANES)
    for s in range(5):
        strips = []
        for tile in range(wide_tiles):
            strip = jnp.zeros((depth, LANES), F32)
            for line in range(by + 4):
                if line * slab // LANES == tile:
                    begin = line * slab % LANES
                    piece = pltpu.roll(windows[line], (begin - s) % LANES, 1)
                    strip = jnp.where((lane >= begin) & (lane < begin + slab), piece, strip)
            strips.append(strip)
        strips.append(jnp.zeros((depth, LANES), F32))
        for b in range(3):
            for tile in range(tiles):
                jump, off = divmod(b * slab, LANES)
                value = strips[min(tile + jump, wide_tiles)]
                if off:
                    after = strips[min(tile + jump + 1, wide_tiles)]
                    value = jnp.where(
                        lane < LANES - off,
                        pltpu.roll(value, LANES - off, 1),
                        pltpu.roll(after, LANES - off, 1),
                    )
                wide_taps[tile, pl.ds(16 + b * 5 + s, depth, stride=16), :] = value
    high, low = split(wide_taps[...])
    taps_high[...] = high
    taps_low[...] = low

    def forward(z, hidden):
        rows = pl.ds(aligned(z * 16, 16), 48)
        high = jnp.concatenate([taps_high[t, rows, :] for t in range(tiles)], axis=1)
        low = jnp.concatenate([taps_low[t, rows, :] for t in range(tiles)], axis=1)
        pre = mxu(first_left, right_rows(high, low))
        cand = jnp.tanh(pre[0:48])
        change = jax.nn.sigmoid(pre[48:96] + first_bias)
        hidden = hidden + change * (mask * cand - hidden)
        field = jnp.concatenate(
            [hidden[:, b * slab : b * slab + out_lanes] for b in range(3)], axis=0
        )
        high, low = split(field)
        product[z + 1] = mxu(second_left, right_rows(high, low))
        return hidden

    times(depth, forward, jnp.zeros((48, tiles * LANES), F32))

    def back(z, hidden):
        pre = product[z, 0:32] + product[z + 1, 32:64] + product[z + 2, 64:96]
        cand = jnp.tanh(pre[0:16])
        change = jax.nn.sigmoid(pre[16:32] + second_bias)
        hidden = hidden + change * (cand - hidden)
        fix[pl.ds(z + 2, 1), 0:out_lanes] = jnp.sum(head * hidden, axis=0, keepdims=True)
        return hidden

    times(depth, back, jnp.zeros((16, out_lanes), F32), True)
    for tile in range(-(-out_lanes // LANES)):
        lanes = slice(tile * LANES, (tile + 1) * LANES)
        centre = wide_taps[tile, pl.ds(16 + 12, depth, stride=16), :]
        fix[2 : 2 + depth, lanes] = fix[2 : 2 + depth, lanes] + centre
    for target in range(gz):
        packed[target] = fix[bz * target : bz * target + bz + 4, :]


    wide = packed.shape[2]
    last = (by - 2) * slab // LANES * LANES

    def part(dy):
        return {0: slice(0, wide), 1: slice(last, last + LANES), -1: slice(0, LANES)}[dy]

    def clean_middle(dy, k):
        target = peer(k)
        return pltpu.make_async_remote_copy(
            src_ref=packed.at[target, :, part(dy)],
            dst_ref=m3.at[1 - dy, me, :, part(dy)],
            send_sem=m3_send.at[dy + 1, k],
            recv_sem=m3_recv.at[1 - dy, me],
            device_id=device(target, dy, 0),
            device_id_type=MESH,
        )

    def clean_edge(dy, dx, k):
        target = peer(k)
        side = (dx + 1) // 2
        return pltpu.make_async_remote_copy(
            src_ref=packed.at[target, :, part(dy)],
            dst_ref=x3.at[1 - dy, 1 - side, :, part(dy)],
            send_sem=x3_send.at[dy + 1, side, k],
            recv_sem=x3_recv.at[1 - dy, 1 - side],
            device_id=device(target, dy, dx),
            device_id_type=MESH,
        )

    late = []
    for dy in steps_y:
        for k in range(gz - 1, -1, -1):
            if (dy, k) != (0, 0):
                late.append((exists(dy, 0), functools.partial(clean_middle, dy, k)))
    for dy in steps_y:
        for dx in steps_x:
            if dx != 0:
                ok = exists(dy, dx) & (high_slab if dx > 0 else low_slab)
                for k in range(gz):
                    late.append((ok, functools.partial(clean_edge, dy, dx, k)))
    for ok, make in late:
        when(ok, lambda make=make: make().start())
    m3[1, me] = packed[me]
    for index, ok in ((0, at_y == 0), (2, at_y == gy - 1)):
        def no_row_again(index=index):
            m3[index] = jnp.zeros(m3.shape[1:], F32)
            x3[index] = jnp.zeros(x3.shape[1:], F32)
        pl.when(ok)(no_row_again)
    for side, ok in ((0, at_x == 0), (1, at_x == gx - 1)):
        def no_side(side=side):
            for index in range(3):
                x3[index, side] = jnp.zeros(x3.shape[2:], F32)
        pl.when(ok)(no_side)
    for dy in steps_y:
        for k in range(gz):
            if (dy, k) != (0, 0):
                source = peer(k)
                def await_clean(dy=dy, source=source):
                    pltpu.make_async_remote_copy(
                        src_ref=packed.at[0, :, part(-dy)],
                        dst_ref=m3.at[1 + dy, source, :, part(-dy)],
                        send_sem=m3_send.at[1 + dy, 0],
                        recv_sem=m3_recv.at[1 + dy, source],
                        device_id=device(source, dy, 0),
                        device_id_type=MESH,
                    ).wait_recv()
                when(exists(dy, 0), await_clean)
    for dy in steps_y:
        for dx in steps_x:
            if dx != 0:
                side = (dx + 1) // 2
                source = gz - 1 if dx < 0 else 0
                def await_side(dy=dy, dx=dx, side=side, source=source):
                    pltpu.make_async_remote_copy(
                        src_ref=packed.at[0, :, part(-dy)],
                        dst_ref=x3.at[1 + dy, side, :, part(-dy)],
                        send_sem=x3_send.at[1 + dy, side, 0],
                        recv_sem=x3_recv.at[1 + dy, side],
                        device_id=device(source, dy, dx),
                        device_id_type=MESH,
                    ).wait_recv()
                when(exists(dy, dx), await_side)

    lines, planes = by + 4, bz + 4
    slab = bx // gz
    lane = lane_of((bz + 4, LANES))
    for line in range(by + 4):
        index, y = (0, by - 2 + line) if line < 2 else (1, line - 2) if line < by + 2 else (2, line - by - 2)
        tile, off = divmod(y * slab, LANES)
        lanes = slice(tile * LANES, (tile + 1) * LANES)
        whole = jnp.zeros((bz + 4, LANES), F32)
        for source in range(gz):
            begin = source * slab
            piece = pltpu.roll(m3[index, source, :, lanes], (begin - off) % LANES, 1)
            whole = jnp.where((lane >= begin) & (lane < begin + slab), piece, whole)
        middle_ref[line] = whole
        before = pltpu.roll(x3[index, 0, :, lanes], (bx - off - slab) % LANES, 1)
        after = pltpu.roll(x3[index, 1, :, lanes], (-off) % LANES, 1)
        edge_ref[line] = jnp.where(lane < LANES // 2, after, before)
    for ok, make in sends:
        when(ok, lambda make=make: make().wait_send())
    for ok, make in late:
        when(ok, lambda make=make: make().wait_send())


def segment_kernel(
    sizes, middle_ref, edge_ref, in_left_ref, out_left_ref, in_bias_ref, out_bias_ref,
    clean_ref, out_ref, seg_taps, result,
):
    gz, gy, gx = sizes
    lines, planes, bx = middle_ref.shape
    by, bz = lines - 4, planes - 4
    me = lax.axis_index("gz")
    at_y = lax.axis_index("gy")
    at_x = lax.axis_index("gx")
    in_left = in_left_ref[...]
    out_left = out_left_ref[...]
    in_bias = in_bias_ref[:, 0:1]
    out_bias = out_bias_ref[:, 0:1]
    for y in range(by + 2):
        seg_taps[y, pl.ds(15, planes, stride=16), :] = jnp.zeros((planes, bx), F32)
    lane = lane_of((planes, bx))
    for line in range(lines):
        middle, edge = middle_ref[line], edge_ref[line]
        for s in range(5):
            value = middle
            if s < 2:
                value = pltpu.roll(jnp.where(lane >= bx - (2 - s), edge, middle), 2 - s, 1)
            if s > 2:
                value = pltpu.roll(jnp.where(lane < s - 2, edge, middle), bx - (s - 2), 1)
            for b in range(3):
                if 0 <= line - b < by + 2:
                    seg_taps[line - b, pl.ds(b * 5 + s, planes, stride=16), :] = value

    for z in range(bz):
        clean_ref[z] = middle_ref[2 : 2 + by, 2 + z, :]
    shape = (48, (by + 2) * bx)
    lane, row = lane_of(shape), row_of(shape)
    place_y = at_y * by + lane // bx - 1
    place_x = at_x * bx + lane % bx + row // 16 - 1
    inside = (place_y >= 0) & (place_y < gy * by) & (place_x >= 0) & (place_x < gx * bx)
    mask = jnp.where(inside, 1.0, 0.0).astype(F32)
    partial = []
    for z in range(bz + 2):
        rows = jnp.concatenate([seg_taps[y, z * 16 : z * 16 + 48, :] for y in range(by + 2)], axis=1)
        high, low = split(rows)
        grown = jnp.maximum(mxu(in_left, right_rows(high, low)) + in_bias, 0.0) * mask
        if z == 0:
            grown = grown * jnp.where(me > 0, 1.0, 0.0).astype(F32)
        if z == bz + 1:
            grown = grown * jnp.where(me < gz - 1, 1.0, 0.0).astype(F32)
        high, low = split(grown)
        field_high = jnp.concatenate([high[:, b * bx : (b + by) * bx] for b in range(3)], axis=0)
        field_low = jnp.concatenate([low[:, b * bx : (b + by) * bx] for b in range(3)], axis=0)
        partial.append(mxu(out_left, right_rows(field_high, field_low)))
        if z >= 2:
            total = partial[z - 2][0:16] + partial[z - 1][16:32] + partial[z][32:48] + out_bias
            for y in range(by):
                result[pl.ds((z - 2) * by + y, 16, stride=bz * by), :] = total[:, y * bx : (y + 1) * bx]
    out_ref[...] = result[0 : 16 * bz * by, :]

def body(sizes, noisy, first_weight, first_bias, second_weight, second_bias, head_weight,
         seg_weight_in, seg_bias_in, seg_weight_out, seg_bias_out):
    gz, gy, gx = sizes
    bz, by, bx = noisy.shape
    depth = gz * bz
    slab = bx // gz
    tiles = -(-(by + 2) * slab // LANES)
    out_lanes = by * slab
    out_tiles = -(-out_lanes // LANES)
    lanes = out_tiles * LANES
    args = [
        noisy.reshape(bz * by, bx),
        first_weight.transpose(2, 1, 0),
        first_bias.reshape(1, -1),
        second_weight.transpose(2, 1, 0),
        second_bias.reshape(1, -1),
        head_weight.reshape(1, -1),
        seg_weight_in,
        seg_bias_in.reshape(1, -1),
        seg_weight_out,
        seg_bias_out.reshape(1, -1),
    ]
    vmem = pl.BlockSpec(memory_space=pltpu.VMEM)
    dma = pltpu.SemaphoreType.DMA
    rest = pl.BlockSpec(memory_space=pl.ANY)

    def room(*shape):
        return pltpu.VMEM(shape, F32)

    stages = [
        room(*(a.shape if i not in (1, 6) else (a.shape[0], a.shape[2]))) for i, a in enumerate(args)
    ]
    handed = pl.pallas_call(
        functools.partial(layers_kernel, sizes, bz, by, bx),
        out_shape=[
            room(by + 4, bz + 4, bx),
            room(by + 4, bz + 4, bx),
            pltpu.VMEM((48, 144), BF16),
            pltpu.VMEM((48, 432), BF16),
            room(48, LANES),
            room(16, LANES),
        ],
        in_specs=[rest] * len(args),
        out_specs=[vmem] * 6,
        scratch_shapes=stages
        + [
            dma((len(args),)),
            room(depth * by, bx),
            room(depth * by, bx),
            room(2, depth * 2, bx),
            room(2, depth * 2, bx),
            room(2, bz * 2, bx),
            dma((3, gz)),
            dma((3, gz)),
            dma((3, 2)),
            dma((3, gz)),
            room(tiles, (depth + 2) * 16, LANES),
            pltpu.VMEM((tiles, (depth + 2) * 16, LANES), BF16),
            pltpu.VMEM((tiles, (depth + 2) * 16, LANES), BF16),
            room(depth + 2, 96, out_lanes),
            room(depth + 16, lanes),
            room(gz, bz + 4, lanes),
            room(3, gz, bz + 4, lanes),
            room(3, 2, bz + 4, lanes),
            dma((3, gz)),
            dma((3, gz)),
            dma((3, 2, gz)),
            dma((3, 2)),
        ],
        compiler_params=pltpu.CompilerParams(
            collective_id=0, has_side_effects=True, vmem_limit_bytes=GRANT
        ),
        name="layers",
    )(*(pltpu.with_memory_space_constraint(a, pltpu.HBM) for a in args))
    clean, features = pl.pallas_call(
        functools.partial(segment_kernel, sizes),
        out_shape=[
            jax.ShapeDtypeStruct((bz, by, bx), F32),
            jax.ShapeDtypeStruct((16 * bz * by, bx), F32),
        ],
        in_specs=[vmem] * 6,
        out_specs=[vmem] * 2,
        scratch_shapes=[room(by + 2, (bz + 5) * 16, bx), room(17 * bz * by, bx)],
        compiler_params=pltpu.CompilerParams(vmem_limit_bytes=GRANT),
        name="segment",
    )(*handed)
    return clean, features.reshape(16, bz, by, bx)


def solution(mesh):
    sizes = (mesh.shape["gz"], mesh.shape["gy"], mesh.shape["gx"])
    in_specs = (P(("win", "gz"), "gy", "gx"), P(), P(), P(), P(), P(), P(), P(), P(), P())
    out_specs = (P(("win", "gz"), "gy", "gx"), P(None, ("win", "gz"), "gy", "gx"))
    return jax.shard_map(
        functools.partial(body, sizes), mesh=mesh, in_specs=in_specs, out_specs=out_specs, check_vma=False
    )
```

```python
import functools

import jax
import jax.numpy as jnp
from jax import lax
from jax.experimental import pallas as pl
from jax.experimental.pallas import tpu as pltpu
from jax.sharding import PartitionSpec as P

LANES = 128
GRANT = 40 << 20
F32 = jnp.float32
BF16 = jnp.bfloat16
MESH = pl.DeviceIdType.MESH


def split(value):
    high = value.astype(BF16)
    return high, (value - high.astype(F32)).astype(BF16)


def left_rows(weight):
    high, low = split(weight)
    return jnp.concatenate([high, high, low], axis=1)


def right_rows(high, low):
    return jnp.concatenate([high, low, high], axis=0)


def mxu(left, right):
    return jnp.dot(left, right, preferred_element_type=F32)


def lane_of(shape):
    return lax.broadcasted_iota(jnp.int32, shape, len(shape) - 1)


def row_of(shape):
    return lax.broadcasted_iota(jnp.int32, shape, 0)


def column(row_ref):
    count = row_ref.shape[1]
    shape = (count, count)
    spread = jnp.broadcast_to(row_ref[...], shape)
    return jnp.sum(jnp.where(row_of(shape) == lane_of(shape), spread, 0.0), axis=1, keepdims=True)


def times(count, step, carry, backward=False):
    if count <= 16:
        for i in range(count):
            carry = step(count - 1 - i if backward else i, carry)
        return carry
    return lax.fori_loop(0, count, lambda i, c: step(count - 1 - i if backward else i, c), carry)


def aligned(start, unit):
    return start if isinstance(start, int) else pl.multiple_of(start, unit)


def matches(left, right):
    return jnp.where(left == right, 1.0, 0.0).astype(BF16)


def spread_narrow(weight, shift):
    taps = weight.shape[1]
    shape = (taps, 48)
    tap, col = row_of(shape), lane_of(shape)
    plane = (tap >= 9).astype(jnp.int32) + (tap >= 18).astype(jnp.int32)
    rest = tap - 9 * plane
    line = (rest >= 3).astype(jnp.int32) + (rest >= 6).astype(jnp.int32)
    place = matches(col, tap + 7 * plane + 2 * line + shift)
    return tuple(mxu(part, place).astype(BF16) for part in split(weight))


def narrow_left(weight):
    parts = weight.shape[0] // 16
    highs, lows = [], []
    for part in range(parts):
        for shift in range(3):
            high, low = spread_narrow(weight[16 * part : 16 * part + 16], shift)
            highs.append(high)
            lows.append(low)
    high, low = jnp.concatenate(highs, axis=0), jnp.concatenate(lows, axis=0)
    return jnp.concatenate([high, high, low], axis=1)


def first_rows(weight, bias, lines):
    taps = weight.shape[1]
    block = 10 * (lines + 4)
    shape = (taps, 3 * block)
    tap, col = row_of(shape), lane_of(shape)
    plane = (tap >= 9).astype(jnp.int32) + (tap >= 18).astype(jnp.int32)
    rest = tap - 9 * plane
    line = (rest >= 3).astype(jnp.int32) + (rest >= 6).astype(jnp.int32)
    start = (lines + 4) * (3 * (rest - 3 * line) + plane) + line
    high, low = split(weight)
    half = weight.shape[0] // 2
    shape = (half, 3 * block)
    steady = jnp.zeros(shape, F32)
    for piece in range(3):
        piece_of = bias.astype(BF16).astype(F32)
        steady = jnp.where(lane_of(shape) == 9 * (lines + 4) + piece, piece_of, steady)
        bias = bias - piece_of
    steady = jnp.concatenate([jnp.zeros(shape, F32), steady], axis=0)
    parts = []
    for at in range(lines + 2):
        first = matches(col, start + at) + matches(col, start + at + block)
        last = matches(col, start + at + 2 * block)
        parts.append((mxu(high, first) + mxu(low, last) + steady).astype(BF16))
    return jnp.concatenate([p[:half] for p in parts] + [p[half:] for p in parts], axis=0)


def second_rows(turned, ins):
    return left_rows(
        jnp.concatenate(
            [
                jnp.concatenate(
                    [
                        turned[ins * (9 * a + 3 * b + c) : ins * (9 * a + 3 * b + c + 1)]
                        for c in range(3)
                        for b in range(3)
                    ],
                    axis=0,
                ).T
                for a in range(3)
            ],
            axis=0,
        )
    )


def last_left(weight):
    outs, ins, taps = weight.shape
    shape = (taps, taps * ins)
    place = matches(row_of(shape), lane_of(shape) // ins)
    shape = (outs * ins, taps * ins)
    keep = (row_of(shape) % ins) == (lane_of(shape) % ins)
    shape = (outs, outs * ins)
    gather = matches(row_of(shape), lane_of(shape) // ins)
    parts = []
    for part in split(weight.reshape(outs * ins, taps)):
        grown = jnp.where(keep, mxu(part, place), 0.0).astype(BF16)
        parts.append(mxu(gather, grown).astype(BF16))
    third = taps * ins // 3
    high, low = (
        jnp.concatenate([p[:, third * a : third * (a + 1)] for a in range(3)], axis=0) for p in parts
    )
    return jnp.concatenate([high, high, low], axis=1)


def layers_kernel(
    sizes, ranks, bz, by, bx,
    noisy_any, w1_any, b1_any, w2_any, b2_any, head_any, w3_any, b3_any, w4_any, b4_any,
    own_ref, beside_ref, edge_ref, in_left_ref, out_left_ref, in_bias_ref, out_bias_ref,
    noisy_ref, w1_ref, b1_ref, w2_ref, b2_ref, head_ref, w3_ref, b3_ref, w4_ref, b4_ref, load_sem,
    m1, my, x1, halo, rim, send1, recv1,
    shifted, ready, product, fix, packed, packed_rim,
    x3, own_send, own_recv, beside_send, beside_recv, edge_send, corner_send, edge_recv,
):
    gz, gy, gx = sizes
    depth = gz * bz
    part = by // ranks
    lines = part + 4
    rows = part + 2
    me = lax.axis_index("gz")
    at_y = lax.axis_index("gy")
    at_x = lax.axis_index("gx")
    works = me < ranks
    steps_y = (-1, 1) if gy > 1 else ()
    steps_x = (-1, 1) if gx > 1 else ()

    def exists(dy, dx):
        ok = None
        for where, step, count in ((at_y, dy, gy), (at_x, dx, gx)):
            if step == 0:
                continue
            here = where > 0 if step < 0 else where < count - 1
            ok = here if ok is None else ok & here
        return ok

    def both(first, second):
        return second if first is None else first if second is None else first & second

    def when(ok, action):
        if ok is None:
            action()
        else:
            pl.when(ok)(action)

    def device(z, dy, dx):
        return {
            "win": lax.axis_index("win"),
            "gz": z,
            "gy": lax.rem(at_y + dy + gy, gy),
            "gx": lax.rem(at_x + dx + gx, gx),
        }

    def peer(k):
        return lax.rem(me + k, gz)

    def rank_towards(dy):
        return 0 if dy > 0 else ranks - 1

    def side(step):
        return (step + 1) // 2

    loads = [
        pltpu.make_async_copy(source, target, load_sem.at[i])
        for i, (source, target) in enumerate(
            (
                (noisy_any, noisy_ref),
                (w1_any.at[:, 0, :], w1_ref),
                (w2_any, w2_ref),
                (w3_any.at[:, 0, :], w3_ref),
                (w4_any, w4_ref),
                (b1_any, b1_ref),
                (b2_any, b2_ref),
                (head_any, head_ref),
                (b3_any, b3_ref),
                (b4_any, b4_ref),
            )
        )
    ]
    loads[0].start()
    barrier = pltpu.get_barrier_semaphore()

    def greet(dy, dx):
        for k in range(gz - 1, -1, -1):
            if (dy, dx, k) != (0, 0, 0):
                pl.semaphore_signal(barrier, inc=1, device_id=device(peer(k), dy, dx), device_id_type=MESH)

    for dx in (0,) + steps_x:
        when(both(works, exists(0, dx)), functools.partial(greet, 0, dx))
    for dy in steps_y:
        for dx in (0,) + steps_x:
            when(both(me == rank_towards(-dy), exists(dy, dx)), functools.partial(greet, dy, dx))
    for load in loads[1:]:
        load.start()

    loads[0].wait()
    for index, first in ((0, 0), (1, by - 2)):
        for z in range(bz):
            halo[index, 2 * z : 2 * z + 2, :] = noisy_ref[z * by + first : z * by + first + 2, :]
    lane = lane_of((by, bx))
    corner = jnp.zeros((by, bx), F32)
    for z in range(bz):
        turned = pltpu.roll(noisy_ref[z * by : (z + 1) * by, :], 4 * z + 2, 1)
        corner = jnp.where((lane >= 4 * z) & (lane < 4 * z + 4), turned, corner)
    rim[...] = corner

    count_y = (at_y > 0).astype(jnp.int32) + (at_y < gy - 1).astype(jnp.int32)
    count_x = (at_x > 0).astype(jnp.int32) + (at_x < gx - 1).astype(jnp.int32)
    pl.semaphore_wait(
        barrier, ranks - works.astype(jnp.int32) + count_y + count_x * ranks + count_y * count_x
    )

    def rows_of(z, count):
        return pl.ds(aligned(z * count, count), count)

    def own_first(k, source):
        return pltpu.make_async_remote_copy(
            src_ref=noisy_ref,
            dst_ref=m1.at[rows_of(source, bz * by), :],
            send_sem=send1.at[0, k],
            recv_sem=recv1.at[0, source],
            device_id=device(k, 0, 0),
            device_id_type=MESH,
        )

    def halo_first(dy, source):
        return pltpu.make_async_remote_copy(
            src_ref=halo.at[side(dy)],
            dst_ref=my.at[side(-dy), rows_of(source, bz * 2), :],
            send_sem=send1.at[1, side(dy)],
            recv_sem=recv1.at[1 + side(-dy), source],
            device_id=device(rank_towards(dy), dy, 0),
            device_id_type=MESH,
        )

    def edge_first(dx, k, source):
        return pltpu.make_async_remote_copy(
            src_ref=rim,
            dst_ref=x1.at[0, side(-dx), source],
            send_sem=send1.at[2 + side(dx), k],
            recv_sem=recv1.at[3 + side(-dx), source],
            device_id=device(k, 0, dx),
            device_id_type=MESH,
        )

    def corner_first(dy, dx, source):
        return pltpu.make_async_remote_copy(
            src_ref=rim,
            dst_ref=x1.at[1 + side(-dy), side(-dx), source],
            send_sem=send1.at[4 + side(dy), side(dx)],
            recv_sem=recv1.at[5 + 2 * side(-dy) + side(-dx), source],
            device_id=device(rank_towards(dy), dy, dx),
            device_id_type=MESH,
        )

    early = []
    for dy in steps_y:
        early.append((exists(dy, 0), functools.partial(halo_first, dy)))
        for dx in steps_x:
            early.append((exists(dy, dx), functools.partial(corner_first, dy, dx)))
    for k in range(ranks):
        early.append((me != k, functools.partial(own_first, k)))
        for dx in steps_x:
            early.append((exists(0, dx), functools.partial(edge_first, dx, k)))
    for ok, make in early:
        when(ok, lambda make=make: make(me).start())

    for load in loads[1:]:
        load.wait()
    for index, ok in ((0, at_y == 0), (1, at_y == gy - 1)):
        def no_row(index=index):
            my[index] = jnp.zeros(my.shape[1:], F32)
            x1[1 + index] = jnp.zeros(x1.shape[1:], F32)
            beside_ref[index] = jnp.zeros(beside_ref.shape[1:], F32)
            x3[ranks + index] = jnp.zeros(x3.shape[1:], F32)
        pl.when(ok)(no_row)
    for index, ok in ((0, at_x == 0), (1, at_x == gx - 1)):
        def no_side(index=index):
            for slot in range(3):
                x1[slot, index] = jnp.zeros(x1.shape[2:], F32)
            for slot in range(ranks + 2):
                x3[slot, index] = jnp.zeros(x3.shape[2:], F32)
        pl.when(ok)(no_side)
    in_left_ref[...] = narrow_left(w3_ref[...])
    out_left_ref[...] = last_left(w4_ref[...])
    in_bias_ref[...] = jnp.broadcast_to(jnp.concatenate([column(b3_ref)] * 3, axis=0), in_bias_ref.shape)
    out_bias_ref[...] = jnp.broadcast_to(column(b4_ref), out_bias_ref.shape)

    def own_last(k, target):
        return pltpu.make_async_remote_copy(
            src_ref=packed.at[target],
            dst_ref=own_ref.at[k],
            send_sem=own_send.at[target],
            recv_sem=own_recv.at[k],
            device_id=device(target, 0, 0),
            device_id_type=MESH,
        )

    def halo_last(dy, target):
        start = 0 if dy < 0 else (part - 2) * bx
        return pltpu.make_async_remote_copy(
            src_ref=packed.at[target, :, start : start + 2 * bx],
            dst_ref=beside_ref.at[side(-dy)],
            send_sem=beside_send.at[side(dy), target],
            recv_sem=beside_recv.at[side(-dy)],
            device_id=device(target, dy, 0),
            device_id_type=MESH,
        )

    def edge_last(dx, k, target):
        return pltpu.make_async_remote_copy(
            src_ref=packed_rim.at[target],
            dst_ref=x3.at[k, side(-dx)],
            send_sem=edge_send.at[side(dx), target],
            recv_sem=edge_recv.at[k, side(-dx)],
            device_id=device(target, 0, dx),
            device_id_type=MESH,
        )

    def corner_last(dy, dx, target):
        return pltpu.make_async_remote_copy(
            src_ref=packed_rim.at[target],
            dst_ref=x3.at[ranks + side(-dy), side(-dx)],
            send_sem=corner_send.at[side(dy), side(dx), target],
            recv_sem=edge_recv.at[ranks + side(-dy), side(-dx)],
            device_id=device(target, dy, dx),
            device_id_type=MESH,
        )

    late = []
    for target in range(gz):
        late.append((me != target, functools.partial(own_last, me, target)))
        for dy in steps_y:
            ok = both(me == rank_towards(-dy), exists(dy, 0))
            late.append((ok, functools.partial(halo_last, dy, target)))
        for dx in steps_x:
            late.append((exists(0, dx), functools.partial(edge_last, dx, me, target)))
        for dy in steps_y:
            for dx in steps_x:
                ok = both(me == rank_towards(-dy), exists(dy, dx))
                late.append((ok, functools.partial(corner_last, dy, dx, target)))

    @pl.when(works)
    def layers():
        first_left = first_rows(w1_ref[...].T, column(b1_ref), part)
        second_left = second_rows(w2_ref[...].reshape(-1, w2_ref.shape[2]), w2_ref.shape[1])
        second_bias = column(b2_ref)
        head = column(head_ref)
        shape = (16 * rows, 2 * bx)
        lane, row = lane_of(shape), row_of(shape)
        place_y = at_y * by + me * part + row // 16 - 1
        outside = (place_y < 0) | (place_y >= gy * by)
        outside = outside | ((at_x == 0) & (lane == 2 * bx - 1)) | ((at_x == gx - 1) & (lane == bx))
        mask = jnp.where(outside, 0.0, 1.0).astype(F32)
        for s in range(6):
            for plane in (0, depth + 1):
                shifted[s, plane * lines : (plane + 1) * lines, :] = jnp.zeros((lines, bx), F32)
        for plane in (0, depth + 1):
            product[plane] = jnp.zeros(product.shape[1:], F32)
        fix[...] = jnp.zeros(fix.shape, F32)
        m1[rows_of(me, bz * by), :] = noisy_ref[...]

        for k in range(1, gz):
            own_first(0, peer(k)).wait_recv()
        for dx in steps_x:
            def await_edges(dx=dx):
                for source in range(gz):
                    edge_first(-dx, 0, source).wait_recv()
            when(exists(0, dx), await_edges)
        for dy in steps_y:
            def await_halos(dy=dy):
                for source in range(gz):
                    halo_first(-dy, source).wait_recv()
            when(both(me == rank_towards(-dy), exists(dy, 0)), await_halos)
            for dx in steps_x:
                def await_corners(dy=dy, dx=dx):
                    for source in range(gz):
                        corner_first(-dy, -dx, source).wait_recv()
                when(both(me == rank_towards(-dy), exists(dy, dx)), await_corners)

        lane = lane_of((lines, bx))
        place = lane_of((by, bx)) % 4

        def mine(full):
            value = full[0:lines]
            for k in range(1, ranks):
                value = jnp.where(me == k, full[part * k : part * k + lines], value)
            return value

        def gather(m, carry):
            rims = [jnp.where(place < 2, x1[slot, 0, m], x1[slot, 1, m]) for slot in range(3)]
            border = mine(jnp.concatenate([rims[1][by - 2 : by], rims[0], rims[2][0:2]], axis=0))
            below = my[0, rows_of(m, bz * 2), :]
            above = my[1, rows_of(m, bz * 2), :]
            block = m1[rows_of(m, bz * by), :]
            for z in range(bz):
                value = mine(
                    jnp.concatenate(
                        [below[2 * z : 2 * z + 2], block[z * by : (z + 1) * by], above[2 * z : 2 * z + 2]],
                        axis=0,
                    )
                )
                beyond = pltpu.roll(border, (bx - 2 - 4 * z) % bx, 1)
                where = pl.ds(aligned((m * bz + z + 1) * lines, lines), lines)
                shifted[0, where, :] = pltpu.roll(jnp.where(lane == bx - 1, beyond, value), 1, 1)
                shifted[1, where, :] = value
                shifted[2, where, :] = pltpu.roll(jnp.where(lane == 0, beyond, value), bx - 1, 1)
                shifted[3, where, :] = pltpu.roll(jnp.where(lane == bx - 2, beyond, value), 1, 1)
                shifted[4, where, :] = beyond
                shifted[5, where, :] = pltpu.roll(jnp.where(lane == 1, beyond, value), bx - 1, 1)
            return carry

        times(gz, gather, 0)
        lane = lane_of((16 * rows, bx))
        spare = jnp.ones((lines, bx), F32)

        def gates(z, slot):
            window = pl.ds(aligned(z * lines, lines), 3 * lines)
            halves = [
                jnp.concatenate([shifted[s, window, :] for s in three] + [spare], axis=0)
                for three in (range(3), range(3, 6))
            ]
            high, low = split(jnp.concatenate(halves, axis=1))
            pre = mxu(first_left, right_rows(high, low))
            ready[0, slot] = mask * jnp.tanh(pre[0 : 16 * rows])
            ready[1, slot] = jax.nn.sigmoid(pre[16 * rows :])

        def advance(z, slot, hidden):
            hidden = hidden + ready[1, slot] * (ready[0, slot] - hidden)
            inner, outer = hidden[:, 0:bx], hidden[:, bx:]
            fields = (
                pltpu.roll(jnp.where(lane == bx - 1, outer, inner), 1, 1),
                inner,
                pltpu.roll(jnp.where(lane == 0, outer, inner), bx - 1, 1),
            )
            highs, lows = zip(*(split(f) for f in fields))

            def stacked(values):
                return jnp.concatenate(
                    [
                        jnp.concatenate([v[16 * j : 16 * j + 48] for j in range(part)], axis=1)
                        for v in values
                    ],
                    axis=0,
                )

            product[z + 1] = mxu(second_left, right_rows(stacked(highs), stacked(lows)))
            return hidden

        chunk = ready.shape[1]

        def forward(step, hidden):
            ahead = 16
            for slot in range(min(ahead, chunk)):
                gates(step * chunk + slot, slot)
            for slot in range(chunk):
                if slot + ahead < chunk:
                    gates(step * chunk + slot + ahead, slot + ahead)
                hidden = advance(step * chunk + slot, slot, hidden)
            return hidden

        times(depth // chunk, forward, jnp.zeros((16 * rows, 2 * bx), F32))

        def back(z, hidden):
            pre = product[z, 0:32] + product[z + 1, 32:64] + product[z + 2, 64:96]
            cand = jnp.tanh(pre[0:16])
            change = jax.nn.sigmoid(pre[16:32] + second_bias)
            hidden = hidden + change * (cand - hidden)
            fix[pl.ds(z + 2, 1), :] = jnp.sum(head * hidden, axis=0, keepdims=True)
            return hidden

        times(depth, back, jnp.zeros((16, part * bx), F32), True)
        lane = lane_of((fix.shape[0], bx))
        border = jnp.zeros((fix.shape[0], bx), F32)
        for j in range(part):
            lanes = slice(j * bx, (j + 1) * bx)
            centre = shifted[1, pl.ds(lines + j + 2, depth, stride=lines), :]
            fix[2 : 2 + depth, lanes] = fix[2 : 2 + depth, lanes] + centre
            turned = pltpu.roll(fix[:, lanes], 4 * j + 2, 1)
            border = jnp.where((lane >= 4 * j) & (lane < 4 * j + 4), turned, border)
        for target in range(gz):
            packed[target] = fix[bz * target : bz * target + bz + 4, :]
            packed_rim[target] = border[bz * target : bz * target + bz + 4]
        for ok, make in late:
            when(ok, lambda make=make: make().start())
        for k in range(ranks):
            def keep(k=k):
                own_ref[k] = packed[k]
            pl.when(me == k)(keep)

    for k in range(ranks):
        def await_own(k=k):
            own_last(k, 0).wait_recv()
        pl.when(me != k)(await_own)
    for dy in steps_y:
        def await_beside(dy=dy):
            halo_last(-dy, 0).wait_recv()
        when(exists(dy, 0), await_beside)
    for dx in steps_x:
        def await_rims(dx=dx):
            for k in range(ranks):
                edge_last(-dx, k, 0).wait_recv()
        when(exists(0, dx), await_rims)
        for dy in steps_y:
            def await_corner(dy=dy, dx=dx):
                corner_last(-dy, -dx, 0).wait_recv()
            when(exists(dy, dx), await_corner)
    place = lane_of((bz + 4, bx)) % 4
    for line in range(by + 4):
        if line < 2:
            slot, j = ranks, part - 2 + line
        elif line < by + 2:
            slot, j = (line - 2) // part, (line - 2) % part
        else:
            slot, j = ranks + 1, line - by - 2
        beyond = jnp.where(place < 2, x3[slot, 0], x3[slot, 1])
        edge_ref[line] = pltpu.roll(beyond, (bx - 2 - 4 * j) % bx, 1)
    for ok, make in early:
        when(ok, lambda make=make: make(me).wait_send())

    @pl.when(works)
    def drain():
        for ok, make in late:
            when(ok, lambda make=make: make().wait_send())


def segment_kernel(
    sizes, own_ref, beside_ref, edge_ref, in_left_ref, out_left_ref, in_bias_ref, out_bias_ref,
    clean_ref, out_ref, seg_taps, result,
):
    gz, gy, gx = sizes
    ranks = own_ref.shape[0]
    lines, planes, bx = edge_ref.shape
    by, bz = lines - 4, planes - 4
    part = by // ranks

    def middle_of(line):
        if 2 <= line < by + 2:
            k, j = divmod(line - 2, part)
            return own_ref[k, :, j * bx : (j + 1) * bx]
        index, j = (0, line) if line < 2 else (1, line - by - 2)
        return beside_ref[index, :, j * bx : (j + 1) * bx]

    me = lax.axis_index("gz")
    at_y = lax.axis_index("gy")
    at_x = lax.axis_index("gx")
    in_left = in_left_ref[...]
    out_left = out_left_ref[...]
    in_bias = in_bias_ref[:, 0:1]
    out_bias = out_bias_ref[:, 0:1]
    for y in range(by + 2):
        seg_taps[y, pl.ds(15, planes, stride=16), :] = jnp.zeros((planes, bx), F32)
    lane = lane_of((planes, bx))
    for line in range(lines):
        middle, edge = middle_of(line), edge_ref[line]
        for s in range(5):
            value = middle
            if s < 2:
                value = pltpu.roll(jnp.where(lane >= bx - (2 - s), edge, middle), 2 - s, 1)
            if s > 2:
                value = pltpu.roll(jnp.where(lane < s - 2, edge, middle), bx - (s - 2), 1)
            for b in range(3):
                if 0 <= line - b < by + 2:
                    seg_taps[line - b, pl.ds(b * 5 + s, planes, stride=16), :] = value

    for z in range(bz):
        for y in range(by):
            clean_ref[z, y : y + 1, :] = middle_of(2 + y)[2 + z : 3 + z]
    shape = (48, (by + 2) * bx)
    lane, row = lane_of(shape), row_of(shape)
    place_y = at_y * by + lane // bx - 1
    place_x = at_x * bx + lane % bx + row // 16 - 1
    inside = (place_y >= 0) & (place_y < gy * by) & (place_x >= 0) & (place_x < gx * bx)
    mask = jnp.where(inside, 1.0, 0.0).astype(F32)
    partial = []
    for z in range(bz + 2):
        rows = jnp.concatenate([seg_taps[y, z * 16 : z * 16 + 48, :] for y in range(by + 2)], axis=1)
        high, low = split(rows)
        grown = jnp.maximum(mxu(in_left, right_rows(high, low)) + in_bias, 0.0) * mask
        if z == 0:
            grown = grown * jnp.where(me > 0, 1.0, 0.0).astype(F32)
        if z == bz + 1:
            grown = grown * jnp.where(me < gz - 1, 1.0, 0.0).astype(F32)
        high, low = split(grown)
        field_high = jnp.concatenate([high[:, b * bx : (b + by) * bx] for b in range(3)], axis=0)
        field_low = jnp.concatenate([low[:, b * bx : (b + by) * bx] for b in range(3)], axis=0)
        partial.append(mxu(out_left, right_rows(field_high, field_low)))
        if z >= 2:
            total = partial[z - 2][0:16] + partial[z - 1][16:32] + partial[z][32:48] + out_bias
            for y in range(by):
                result[pl.ds((z - 2) * by + y, 16, stride=bz * by), :] = total[:, y * bx : (y + 1) * bx]
    out_ref[...] = result[0 : 16 * bz * by, :]


def body(sizes, noisy, first_weight, first_bias, second_weight, second_bias, head_weight,
         seg_weight_in, seg_bias_in, seg_weight_out, seg_bias_out):
    gz, gy, gx = sizes
    bz, by, bx = noisy.shape
    ranks = by // 4
    part = by // ranks
    lines = part + 4
    depth = gz * bz
    args = [
        noisy.reshape(bz * by, bx),
        first_weight.transpose(2, 1, 0),
        first_bias.reshape(1, -1),
        second_weight.transpose(2, 1, 0),
        second_bias.reshape(1, -1),
        head_weight.reshape(1, -1),
        seg_weight_in,
        seg_bias_in.reshape(1, -1),
        seg_weight_out,
        seg_bias_out.reshape(1, -1),
    ]
    vmem = pl.BlockSpec(memory_space=pltpu.VMEM)
    dma = pltpu.SemaphoreType.DMA
    rest = pl.BlockSpec(memory_space=pl.ANY)

    def room(*shape):
        return pltpu.VMEM(shape, F32)

    stages = [
        room(*(a.shape if i not in (1, 6) else (a.shape[0], a.shape[2]))) for i, a in enumerate(args)
    ]
    handed = pl.pallas_call(
        functools.partial(layers_kernel, sizes, ranks, bz, by, bx),
        out_shape=[
            room(ranks, bz + 4, part * bx),
            room(2, bz + 4, 2 * bx),
            room(by + 4, bz + 4, bx),
            pltpu.VMEM((48, 144), BF16),
            pltpu.VMEM((48, 432), BF16),
            room(48, LANES),
            room(16, LANES),
        ],
        in_specs=[rest] * len(args),
        out_specs=[vmem] * 7,
        scratch_shapes=stages
        + [
            dma((len(args),)),
            room(depth * by, bx),
            room(2, depth * 2, bx),
            room(3, 2, gz, by, bx),
            room(2, bz * 2, bx),
            room(by, bx),
            dma((6, max(ranks, 2))),
            dma((9, gz)),
            room(6, (depth + 2) * lines, bx),
            room(2, min(depth, 16), 16 * (part + 2), 2 * bx),
            room(depth + 2, 96, part * bx),
            room(depth + 16, part * bx),
            room(gz, bz + 4, part * bx),
            room(gz, bz + 4, bx),
            room(ranks + 2, 2, bz + 4, bx),
            dma((gz,)),
            dma((ranks,)),
            dma((2, gz)),
            dma((2,)),
            dma((2, gz)),
            dma((2, 2, gz)),
            dma((ranks + 2, 2)),
        ],
        compiler_params=pltpu.CompilerParams(
            collective_id=0, has_side_effects=True, vmem_limit_bytes=GRANT
        ),
        name="layers",
    )(*(pltpu.with_memory_space_constraint(a, pltpu.HBM) for a in args))
    clean, features = pl.pallas_call(
        functools.partial(segment_kernel, sizes),
        out_shape=[
            jax.ShapeDtypeStruct((bz, by, bx), F32),
            jax.ShapeDtypeStruct((16 * bz * by, bx), F32),
        ],
        in_specs=[vmem] * 7,
        out_specs=[vmem] * 2,
        scratch_shapes=[room(by + 2, (bz + 5) * 16, bx), room(17 * bz * by, bx)],
        compiler_params=pltpu.CompilerParams(vmem_limit_bytes=GRANT),
        name="segment",
    )(*handed)
    return clean, features.reshape(16, bz, by, bx)


def solution(mesh):
    sizes = (mesh.shape["gz"], mesh.shape["gy"], mesh.shape["gx"])
    in_specs = (P(("win", "gz"), "gy", "gx"), P(), P(), P(), P(), P(), P(), P(), P(), P())
    out_specs = (P(("win", "gz"), "gy", "gx"), P(None, ("win", "gz"), "gy", "gx"))
    return jax.shard_map(
        functools.partial(body, sizes), mesh=mesh, in_specs=in_specs, out_specs=out_specs, check_vma=False
    )
```

```python
import functools

import jax
import jax.numpy as jnp
from jax import lax
from jax.experimental import pallas as pl
from jax.experimental.pallas import tpu as pltpu
from jax.sharding import PartitionSpec as P

LANES = 128
GRANT = 40 << 20
F32 = jnp.float32
BF16 = jnp.bfloat16
MESH = pl.DeviceIdType.MESH


def split(value):
    high = value.astype(BF16)
    return high, (value - high.astype(F32)).astype(BF16)


def left_rows(weight):
    high, low = split(weight)
    return jnp.concatenate([high, high, low], axis=1)


def right_rows(high, low):
    return jnp.concatenate([high, low, high], axis=0)


def mxu(left, right):
    return jnp.dot(left, right, preferred_element_type=F32)


def lane_of(shape):
    return lax.broadcasted_iota(jnp.int32, shape, len(shape) - 1)


def row_of(shape):
    return lax.broadcasted_iota(jnp.int32, shape, 0)


def column(row_ref):
    count = row_ref.shape[1]
    shape = (count, count)
    spread = jnp.broadcast_to(row_ref[...], shape)
    return jnp.sum(jnp.where(row_of(shape) == lane_of(shape), spread, 0.0), axis=1, keepdims=True)


def times(count, step, carry, backward=False):
    if count <= 16:
        for i in range(count):
            carry = step(count - 1 - i if backward else i, carry)
        return carry
    return lax.fori_loop(0, count, lambda i, c: step(count - 1 - i if backward else i, c), carry)


def aligned(start, unit):
    return start if isinstance(start, int) else pl.multiple_of(start, unit)


def matches(left, right):
    return jnp.where(left == right, 1.0, 0.0).astype(BF16)


def spread_narrow(weight, shift):
    taps = weight.shape[1]
    shape = (taps, 48)
    tap, col = row_of(shape), lane_of(shape)
    plane = (tap >= 9).astype(jnp.int32) + (tap >= 18).astype(jnp.int32)
    rest = tap - 9 * plane
    line = (rest >= 3).astype(jnp.int32) + (rest >= 6).astype(jnp.int32)
    place = matches(col, tap + 7 * plane + 2 * line + shift)
    return tuple(mxu(part, place).astype(BF16) for part in split(weight))


def narrow_left(weight):
    parts = weight.shape[0] // 16
    highs, lows = [], []
    for part in range(parts):
        for shift in range(3):
            high, low = spread_narrow(weight[16 * part : 16 * part + 16], shift)
            highs.append(high)
            lows.append(low)
    high, low = jnp.concatenate(highs, axis=0), jnp.concatenate(lows, axis=0)
    return jnp.concatenate([high, high, low], axis=1)


def first_rows(weight, bias, lines):
    taps = weight.shape[1]
    block = 10 * (lines + 4)
    shape = (taps, 3 * block)
    tap, col = row_of(shape), lane_of(shape)
    plane = (tap >= 9).astype(jnp.int32) + (tap >= 18).astype(jnp.int32)
    rest = tap - 9 * plane
    line = (rest >= 3).astype(jnp.int32) + (rest >= 6).astype(jnp.int32)
    start = (lines + 4) * (3 * (rest - 3 * line) + plane) + line
    high, low = split(weight)
    half = weight.shape[0] // 2
    shape = (half, 3 * block)
    steady = jnp.zeros(shape, F32)
    for piece in range(3):
        piece_of = bias.astype(BF16).astype(F32)
        steady = jnp.where(lane_of(shape) == 9 * (lines + 4) + piece, piece_of, steady)
        bias = bias - piece_of
    steady = jnp.concatenate([jnp.zeros(shape, F32), steady], axis=0)
    parts = []
    for at in range(lines + 2):
        first = matches(col, start + at) + matches(col, start + at + block)
        last = matches(col, start + at + 2 * block)
        parts.append((mxu(high, first) + mxu(low, last) + steady).astype(BF16))
    return jnp.concatenate([p[:half] for p in parts] + [p[half:] for p in parts], axis=0)


def second_rows(turned, ins):
    return left_rows(
        jnp.concatenate(
            [
                jnp.concatenate(
                    [
                        turned[ins * (9 * a + 3 * b + c) : ins * (9 * a + 3 * b + c + 1)]
                        for c in range(3)
                        for b in range(3)
                    ],
                    axis=0,
                ).T
                for a in range(3)
            ],
            axis=0,
        )
    )


def last_left(weight):
    outs, ins, taps = weight.shape
    shape = (taps, taps * ins)
    place = matches(row_of(shape), lane_of(shape) // ins)
    shape = (outs * ins, taps * ins)
    keep = (row_of(shape) % ins) == (lane_of(shape) % ins)
    shape = (outs, outs * ins)
    gather = matches(row_of(shape), lane_of(shape) // ins)
    parts = []
    for part in split(weight.reshape(outs * ins, taps)):
        grown = jnp.where(keep, mxu(part, place), 0.0).astype(BF16)
        parts.append(mxu(gather, grown).astype(BF16))
    third = taps * ins // 3
    high, low = (
        jnp.concatenate([p[:, third * a : third * (a + 1)] for a in range(3)], axis=0) for p in parts
    )
    return jnp.concatenate([high, high, low], axis=1)


def layers_kernel(
    sizes, ranks, bz, by, bx,
    noisy_any, w1_any, b1_any, w2_any, b2_any, head_any, w3_any, b3_any, w4_any, b4_any,
    own_ref, beside_ref, edge_ref, in_left_ref, out_left_ref, in_bias_ref, out_bias_ref,
    noisy_ref, w1_ref, b1_ref, w2_ref, b2_ref, head_ref, w3_ref, b3_ref, w4_ref, b4_ref, load_sem,
    m1, my, x1, halo, rim, send1, recv1,
    shifted, ready, product, fix, packed, packed_rim,
    x3, own_send, own_recv, beside_send, beside_recv, edge_send, corner_send, edge_recv,
):
    gz, gy, gx = sizes
    depth = gz * bz
    part = by // ranks
    lines = part + 4
    rows = part + 2
    me = lax.axis_index("gz")
    at_y = lax.axis_index("gy")
    at_x = lax.axis_index("gx")
    works = me < ranks
    turned_round = 1 - lax.rem(at_y, 2)
    mine = me + turned_round * (ranks - 1 - 2 * me)
    steps_y = (-1, 1) if gy > 1 else ()
    steps_x = (-1, 1) if gx > 1 else ()

    def exists(dy, dx):
        ok = None
        for where, step, count in ((at_y, dy, gy), (at_x, dx, gx)):
            if step == 0:
                continue
            here = where > 0 if step < 0 else where < count - 1
            ok = here if ok is None else ok & here
        return ok

    def both(first, second):
        return second if first is None else first if second is None else first & second

    def when(ok, action):
        if ok is None:
            action()
        else:
            pl.when(ok)(action)

    def device(z, dy, dx):
        return {
            "win": lax.axis_index("win"),
            "gz": z,
            "gy": lax.rem(at_y + dy + gy, gy),
            "gx": lax.rem(at_x + dx + gx, gx),
        }

    def peer(k):
        return lax.rem(me + k, gz)

    def rank_towards(dy):
        return 0 if dy > 0 else ranks - 1

    def home_towards(dy):
        rank = rank_towards(dy)
        return rank + (1 - turned_round) * (ranks - 1 - 2 * rank)

    def side(step):
        return (step + 1) // 2

    loads = [
        pltpu.make_async_copy(source, target, load_sem.at[i])
        for i, (source, target) in enumerate(
            (
                (noisy_any, noisy_ref),
                (w1_any.at[:, 0, :], w1_ref),
                (w2_any, w2_ref),
                (w3_any.at[:, 0, :], w3_ref),
                (w4_any, w4_ref),
                (b1_any, b1_ref),
                (b2_any, b2_ref),
                (head_any, head_ref),
                (b3_any, b3_ref),
                (b4_any, b4_ref),
            )
        )
    ]
    loads[0].start()
    barrier = pltpu.get_barrier_semaphore()

    def greet(dy, dx):
        for k in range(gz - 1, -1, -1):
            if (dy, dx, k) != (0, 0, 0):
                pl.semaphore_signal(barrier, inc=1, device_id=device(peer(k), dy, dx), device_id_type=MESH)

    for dy in steps_y:
        for dx in (0,) + steps_x:
            when(both(mine == rank_towards(-dy), exists(dy, dx)), functools.partial(greet, dy, dx))
    for dx in (0,) + steps_x:
        when(both(works, exists(0, dx)), functools.partial(greet, 0, dx))
    for load in loads[1:]:
        load.start()

    loads[0].wait()
    for index, first in ((0, 0), (1, by - 2)):
        for z in range(bz):
            halo[index, 2 * z : 2 * z + 2, :] = noisy_ref[z * by + first : z * by + first + 2, :]
    lane = lane_of((by, bx))
    corner = jnp.zeros((by, bx), F32)
    for z in range(bz):
        turned = pltpu.roll(noisy_ref[z * by : (z + 1) * by, :], 4 * z + 2, 1)
        corner = jnp.where((lane >= 4 * z) & (lane < 4 * z + 4), turned, corner)
    rim[...] = corner

    count_y = (at_y > 0).astype(jnp.int32) + (at_y < gy - 1).astype(jnp.int32)
    count_x = (at_x > 0).astype(jnp.int32) + (at_x < gx - 1).astype(jnp.int32)
    pl.semaphore_wait(
        barrier, ranks - works.astype(jnp.int32) + count_y + count_x * ranks + count_y * count_x
    )

    def rows_of(z, count):
        return pl.ds(aligned(z * count, count), count)

    def own_first(k, source):
        return pltpu.make_async_remote_copy(
            src_ref=noisy_ref,
            dst_ref=m1.at[rows_of(source, bz * by), :],
            send_sem=send1.at[0, k],
            recv_sem=recv1.at[0, source],
            device_id=device(k, 0, 0),
            device_id_type=MESH,
        )

    def halo_first(dy, source):
        return pltpu.make_async_remote_copy(
            src_ref=halo.at[side(dy)],
            dst_ref=my.at[side(-dy), rows_of(source, bz * 2), :],
            send_sem=send1.at[1, side(dy)],
            recv_sem=recv1.at[1 + side(-dy), source],
            device_id=device(home_towards(dy), dy, 0),
            device_id_type=MESH,
        )

    def edge_first(dx, k, source):
        return pltpu.make_async_remote_copy(
            src_ref=rim,
            dst_ref=x1.at[0, side(-dx), source],
            send_sem=send1.at[2 + side(dx), k],
            recv_sem=recv1.at[3 + side(-dx), source],
            device_id=device(k, 0, dx),
            device_id_type=MESH,
        )

    def corner_first(dy, dx, source):
        return pltpu.make_async_remote_copy(
            src_ref=rim,
            dst_ref=x1.at[1 + side(-dy), side(-dx), source],
            send_sem=send1.at[4 + side(dy), side(dx)],
            recv_sem=recv1.at[5 + 2 * side(-dy) + side(-dx), source],
            device_id=device(home_towards(dy), dy, dx),
            device_id_type=MESH,
        )

    early = []
    for dy in steps_y:
        early.append((exists(dy, 0), functools.partial(halo_first, dy)))
        for dx in steps_x:
            early.append((exists(dy, dx), functools.partial(corner_first, dy, dx)))
    for k in range(ranks):
        early.append((me != k, functools.partial(own_first, k)))
        for dx in steps_x:
            early.append((exists(0, dx), functools.partial(edge_first, dx, k)))
    for ok, make in early:
        when(ok, lambda make=make: make(me).start())

    for load in loads[1:]:
        load.wait()
    for index, ok in ((0, at_y == 0), (1, at_y == gy - 1)):
        def no_row(index=index):
            my[index] = jnp.zeros(my.shape[1:], F32)
            x1[1 + index] = jnp.zeros(x1.shape[1:], F32)
            beside_ref[index] = jnp.zeros(beside_ref.shape[1:], F32)
            x3[ranks + index] = jnp.zeros(x3.shape[1:], F32)
        pl.when(ok)(no_row)
    for index, ok in ((0, at_x == 0), (1, at_x == gx - 1)):
        def no_side(index=index):
            for slot in range(3):
                x1[slot, index] = jnp.zeros(x1.shape[2:], F32)
            for slot in range(ranks + 2):
                x3[slot, index] = jnp.zeros(x3.shape[2:], F32)
        pl.when(ok)(no_side)
    in_left_ref[...] = narrow_left(w3_ref[...])
    out_left_ref[...] = last_left(w4_ref[...])
    in_bias_ref[...] = jnp.broadcast_to(jnp.concatenate([column(b3_ref)] * 3, axis=0), in_bias_ref.shape)
    out_bias_ref[...] = jnp.broadcast_to(column(b4_ref), out_bias_ref.shape)

    def own_last(k, target):
        return pltpu.make_async_remote_copy(
            src_ref=packed.at[target],
            dst_ref=own_ref.at[k],
            send_sem=own_send.at[target],
            recv_sem=own_recv.at[k],
            device_id=device(target, 0, 0),
            device_id_type=MESH,
        )

    def halo_last(dy, target):
        start = 0 if dy < 0 else (part - 2) * bx
        return pltpu.make_async_remote_copy(
            src_ref=packed.at[target, :, start : start + 2 * bx],
            dst_ref=beside_ref.at[side(-dy)],
            send_sem=beside_send.at[side(dy), target],
            recv_sem=beside_recv.at[side(-dy)],
            device_id=device(target, dy, 0),
            device_id_type=MESH,
        )

    def edge_last(dx, k, target):
        return pltpu.make_async_remote_copy(
            src_ref=packed_rim.at[target],
            dst_ref=x3.at[k, side(-dx)],
            send_sem=edge_send.at[side(dx), target],
            recv_sem=edge_recv.at[k, side(-dx)],
            device_id=device(target, 0, dx),
            device_id_type=MESH,
        )

    def corner_last(dy, dx, target):
        return pltpu.make_async_remote_copy(
            src_ref=packed_rim.at[target],
            dst_ref=x3.at[ranks + side(-dy), side(-dx)],
            send_sem=corner_send.at[side(dy), side(dx), target],
            recv_sem=edge_recv.at[ranks + side(-dy), side(-dx)],
            device_id=device(target, dy, dx),
            device_id_type=MESH,
        )

    late = []
    for target in range(gz):
        late.append((me != target, functools.partial(own_last, mine, target)))
        for dy in steps_y:
            ok = both(mine == rank_towards(-dy), exists(dy, 0))
            late.append((ok, functools.partial(halo_last, dy, target)))
        for dx in steps_x:
            late.append((exists(0, dx), functools.partial(edge_last, dx, mine, target)))
        for dy in steps_y:
            for dx in steps_x:
                ok = both(mine == rank_towards(-dy), exists(dy, dx))
                late.append((ok, functools.partial(corner_last, dy, dx, target)))

    for ok, make in early:
        when(ok, lambda make=make: make(me).wait_send())

    @pl.when(works)
    def layers():
        first_left = first_rows(w1_ref[...].T, column(b1_ref), part)
        second_left = second_rows(w2_ref[...].reshape(-1, w2_ref.shape[2]), w2_ref.shape[1])
        second_bias = column(b2_ref)
        head = column(head_ref)
        shape = (16 * rows, 2 * bx)
        lane, row = lane_of(shape), row_of(shape)
        place_y = at_y * by + mine * part + row // 16 - 1
        outside = (place_y < 0) | (place_y >= gy * by)
        outside = outside | ((at_x == 0) & (lane == 2 * bx - 1)) | ((at_x == gx - 1) & (lane == bx))
        mask = jnp.where(outside, 0.0, 1.0).astype(F32)
        for s in range(6):
            for plane in (0, depth + 1):
                shifted[s, plane * lines : (plane + 1) * lines, :] = jnp.zeros((lines, bx), F32)
        for plane in (0, depth + 1):
            product[plane] = jnp.zeros(product.shape[1:], F32)
        fix[...] = jnp.zeros(fix.shape, F32)
        m1[rows_of(me, bz * by), :] = noisy_ref[...]

        def arrive(m):
            def await_own():
                own_first(0, m).wait_recv()
            pl.when(me != m)(await_own)
            for dx in steps_x:
                def await_edge(dx=dx):
                    edge_first(-dx, 0, m).wait_recv()
                when(exists(0, dx), await_edge)
            for dy in steps_y:
                def await_halo(dy=dy):
                    halo_first(-dy, m).wait_recv()
                when(both(mine == rank_towards(-dy), exists(dy, 0)), await_halo)
                for dx in steps_x:
                    def await_corner(dy=dy, dx=dx):
                        corner_first(-dy, -dx, m).wait_recv()
                    when(both(mine == rank_towards(-dy), exists(dy, dx)), await_corner)

        flat = lane_of((lines, bx))
        place = lane_of((by, bx)) % 4

        def cut(full):
            value = full[0:lines]
            for k in range(1, ranks):
                value = jnp.where(mine == k, full[part * k : part * k + lines], value)
            return value

        def gather(m):
            rims = [jnp.where(place < 2, x1[slot, 0, m], x1[slot, 1, m]) for slot in range(3)]
            border = cut(jnp.concatenate([rims[1][by - 2 : by], rims[0], rims[2][0:2]], axis=0))
            below = my[0, rows_of(m, bz * 2), :]
            above = my[1, rows_of(m, bz * 2), :]
            block = m1[rows_of(m, bz * by), :]
            for z in range(bz):
                value = cut(
                    jnp.concatenate(
                        [below[2 * z : 2 * z + 2], block[z * by : (z + 1) * by], above[2 * z : 2 * z + 2]],
                        axis=0,
                    )
                )
                beyond = pltpu.roll(border, (bx - 2 - 4 * z) % bx, 1)
                where = pl.ds(aligned((m * bz + z + 1) * lines, lines), lines)
                shifted[0, where, :] = pltpu.roll(jnp.where(flat == bx - 1, beyond, value), 1, 1)
                shifted[1, where, :] = value
                shifted[2, where, :] = pltpu.roll(jnp.where(flat == 0, beyond, value), bx - 1, 1)
                shifted[3, where, :] = pltpu.roll(jnp.where(flat == bx - 2, beyond, value), 1, 1)
                shifted[4, where, :] = beyond
                shifted[5, where, :] = pltpu.roll(jnp.where(flat == 1, beyond, value), bx - 1, 1)

        lane = lane_of((16 * rows, bx))
        spare = jnp.ones((lines, bx), F32)

        def gates(z, slot):
            window = pl.ds(aligned(z * lines, lines), 3 * lines)
            halves = [
                jnp.concatenate([shifted[s, window, :] for s in three] + [spare], axis=0)
                for three in (range(3), range(3, 6))
            ]
            high, low = split(jnp.concatenate(halves, axis=1))
            pre = mxu(first_left, right_rows(high, low))
            ready[0, slot] = mask * jnp.tanh(pre[0 : 16 * rows])
            ready[1, slot] = jax.nn.sigmoid(pre[16 * rows :])

        def advance(z, slot, hidden):
            hidden = hidden + ready[1, slot] * (ready[0, slot] - hidden)
            inner, outer = hidden[:, 0:bx], hidden[:, bx:]
            fields = (
                pltpu.roll(jnp.where(lane == bx - 1, outer, inner), 1, 1),
                inner,
                pltpu.roll(jnp.where(lane == 0, outer, inner), bx - 1, 1),
            )
            highs, lows = zip(*(split(f) for f in fields))

            def stacked(values):
                return jnp.concatenate(
                    [
                        jnp.concatenate([v[16 * j : 16 * j + 48] for j in range(part)], axis=1)
                        for v in values
                    ],
                    axis=0,
                )

            product[z + 1] = mxu(second_left, right_rows(stacked(highs), stacked(lows)))
            return hidden

        def reach(m, first, count, hidden):
            arrive(m)
            gather(m)
            for slot in range(count):
                gates(first + slot, slot)
            for slot in range(count):
                hidden = advance(first + slot, slot, hidden)
            return hidden

        def later(i, hidden):
            return reach(i + 1, (i + 1) * bz - 1, bz, hidden)

        hidden = reach(0, 0, bz - 1, jnp.zeros((16 * rows, 2 * bx), F32))
        hidden = times(gz - 2, later, hidden)
        reach(gz - 1, depth - bz - 1, bz + 1, hidden)

        def back(z, hidden):
            pre = product[z, 0:32] + product[z + 1, 32:64] + product[z + 2, 64:96]
            cand = jnp.tanh(pre[0:16])
            change = jax.nn.sigmoid(pre[16:32] + second_bias)
            hidden = hidden + change * (cand - hidden)
            fix[pl.ds(z + 2, 1), :] = jnp.sum(head * hidden, axis=0, keepdims=True)
            return hidden

        times(depth, back, jnp.zeros((16, part * bx), F32), True)
        lane = lane_of((fix.shape[0], bx))
        border = jnp.zeros((fix.shape[0], bx), F32)
        for j in range(part):
            lanes = slice(j * bx, (j + 1) * bx)
            centre = shifted[1, pl.ds(lines + j + 2, depth, stride=lines), :]
            fix[2 : 2 + depth, lanes] = fix[2 : 2 + depth, lanes] + centre
            turned = pltpu.roll(fix[:, lanes], 4 * j + 2, 1)
            border = jnp.where((lane >= 4 * j) & (lane < 4 * j + 4), turned, border)
        for target in range(gz):
            packed[target] = fix[bz * target : bz * target + bz + 4, :]
            packed_rim[target] = border[bz * target : bz * target + bz + 4]
        for ok, make in late:
            when(ok, lambda make=make: make().start())
        own_ref[mine] = packed[me]

    for k in range(ranks):
        def await_own(k=k):
            own_last(k, 0).wait_recv()
        pl.when(mine != k)(await_own)
    for dy in steps_y:
        def await_beside(dy=dy):
            halo_last(-dy, 0).wait_recv()
        when(exists(dy, 0), await_beside)
    for dx in steps_x:
        def await_rims(dx=dx):
            for k in range(ranks):
                edge_last(-dx, k, 0).wait_recv()
        when(exists(0, dx), await_rims)
        for dy in steps_y:
            def await_corner(dy=dy, dx=dx):
                corner_last(-dy, -dx, 0).wait_recv()
            when(exists(dy, dx), await_corner)
    place = lane_of((bz + 4, bx)) % 4
    for line in range(by + 4):
        if line < 2:
            slot, j = ranks, part - 2 + line
        elif line < by + 2:
            slot, j = (line - 2) // part, (line - 2) % part
        else:
            slot, j = ranks + 1, line - by - 2
        beyond = jnp.where(place < 2, x3[slot, 0], x3[slot, 1])
        edge_ref[line] = pltpu.roll(beyond, (bx - 2 - 4 * j) % bx, 1)

    @pl.when(works)
    def drain():
        for ok, make in late:
            when(ok, lambda make=make: make().wait_send())


def segment_kernel(
    sizes, own_ref, beside_ref, edge_ref, in_left_ref, out_left_ref, in_bias_ref, out_bias_ref,
    clean_ref, out_ref, seg_taps, result,
):
    gz, gy, gx = sizes
    ranks = own_ref.shape[0]
    lines, planes, bx = edge_ref.shape
    by, bz = lines - 4, planes - 4
    part = by // ranks

    def middle_of(line):
        if 2 <= line < by + 2:
            k, j = divmod(line - 2, part)
            return own_ref[k, :, j * bx : (j + 1) * bx]
        index, j = (0, line) if line < 2 else (1, line - by - 2)
        return beside_ref[index, :, j * bx : (j + 1) * bx]

    me = lax.axis_index("gz")
    at_y = lax.axis_index("gy")
    at_x = lax.axis_index("gx")
    in_left = in_left_ref[...]
    out_left = out_left_ref[...]
    in_bias = in_bias_ref[:, 0:1]
    out_bias = out_bias_ref[:, 0:1]
    for y in range(by + 2):
        seg_taps[y, pl.ds(15, planes, stride=16), :] = jnp.zeros((planes, bx), F32)
    lane = lane_of((planes, bx))
    for line in range(lines):
        middle, edge = middle_of(line), edge_ref[line]
        for s in range(5):
            value = middle
            if s < 2:
                value = pltpu.roll(jnp.where(lane >= bx - (2 - s), edge, middle), 2 - s, 1)
            if s > 2:
                value = pltpu.roll(jnp.where(lane < s - 2, edge, middle), bx - (s - 2), 1)
            for b in range(3):
                if 0 <= line - b < by + 2:
                    seg_taps[line - b, pl.ds(b * 5 + s, planes, stride=16), :] = value

    for z in range(bz):
        for y in range(by):
            clean_ref[z, y : y + 1, :] = middle_of(2 + y)[2 + z : 3 + z]
    shape = (48, (by + 2) * bx)
    lane, row = lane_of(shape), row_of(shape)
    place_y = at_y * by + lane // bx - 1
    place_x = at_x * bx + lane % bx + row // 16 - 1
    inside = (place_y >= 0) & (place_y < gy * by) & (place_x >= 0) & (place_x < gx * bx)
    mask = jnp.where(inside, 1.0, 0.0).astype(F32)
    partial = []
    for z in range(bz + 2):
        rows = jnp.concatenate([seg_taps[y, z * 16 : z * 16 + 48, :] for y in range(by + 2)], axis=1)
        high, low = split(rows)
        grown = jnp.maximum(mxu(in_left, right_rows(high, low)) + in_bias, 0.0) * mask
        if z == 0:
            grown = grown * jnp.where(me > 0, 1.0, 0.0).astype(F32)
        if z == bz + 1:
            grown = grown * jnp.where(me < gz - 1, 1.0, 0.0).astype(F32)
        high, low = split(grown)
        field_high = jnp.concatenate([high[:, b * bx : (b + by) * bx] for b in range(3)], axis=0)
        field_low = jnp.concatenate([low[:, b * bx : (b + by) * bx] for b in range(3)], axis=0)
        partial.append(mxu(out_left, right_rows(field_high, field_low)))
        if z >= 2:
            total = partial[z - 2][0:16] + partial[z - 1][16:32] + partial[z][32:48] + out_bias
            for y in range(by):
                result[pl.ds((z - 2) * by + y, 16, stride=bz * by), :] = total[:, y * bx : (y + 1) * bx]
    out_ref[...] = result[0 : 16 * bz * by, :]


def body(sizes, noisy, first_weight, first_bias, second_weight, second_bias, head_weight,
         seg_weight_in, seg_bias_in, seg_weight_out, seg_bias_out):
    gz, gy, gx = sizes
    bz, by, bx = noisy.shape
    ranks = by // 4
    part = by // ranks
    lines = part + 4
    depth = gz * bz
    args = [
        noisy.reshape(bz * by, bx),
        first_weight.transpose(2, 1, 0),
        first_bias.reshape(1, -1),
        second_weight.transpose(2, 1, 0),
        second_bias.reshape(1, -1),
        head_weight.reshape(1, -1),
        seg_weight_in,
        seg_bias_in.reshape(1, -1),
        seg_weight_out,
        seg_bias_out.reshape(1, -1),
    ]
    vmem = pl.BlockSpec(memory_space=pltpu.VMEM)
    dma = pltpu.SemaphoreType.DMA
    rest = pl.BlockSpec(memory_space=pl.ANY)

    def room(*shape):
        return pltpu.VMEM(shape, F32)

    stages = [
        room(*(a.shape if i not in (1, 6) else (a.shape[0], a.shape[2]))) for i, a in enumerate(args)
    ]
    handed = pl.pallas_call(
        functools.partial(layers_kernel, sizes, ranks, bz, by, bx),
        out_shape=[
            room(ranks, bz + 4, part * bx),
            room(2, bz + 4, 2 * bx),
            room(by + 4, bz + 4, bx),
            pltpu.VMEM((48, 144), BF16),
            pltpu.VMEM((48, 432), BF16),
            room(48, LANES),
            room(16, LANES),
        ],
        in_specs=[rest] * len(args),
        out_specs=[vmem] * 7,
        scratch_shapes=stages
        + [
            dma((len(args),)),
            room(depth * by, bx),
            room(2, depth * 2, bx),
            room(3, 2, gz, by, bx),
            room(2, bz * 2, bx),
            room(by, bx),
            dma((6, max(ranks, 2))),
            dma((9, gz)),
            room(6, (depth + 2) * lines, bx),
            room(2, bz + 1, 16 * (part + 2), 2 * bx),
            room(depth + 2, 96, part * bx),
            room(depth + 16, part * bx),
            room(gz, bz + 4, part * bx),
            room(gz, bz + 4, bx),
            room(ranks + 2, 2, bz + 4, bx),
            dma((gz,)),
            dma((ranks,)),
            dma((2, gz)),
            dma((2,)),
            dma((2, gz)),
            dma((2, 2, gz)),
            dma((ranks + 2, 2)),
        ],
        compiler_params=pltpu.CompilerParams(
            collective_id=0, has_side_effects=True, vmem_limit_bytes=GRANT
        ),
        name="layers",
    )(*(pltpu.with_memory_space_constraint(a, pltpu.HBM) for a in args))
    clean, features = pl.pallas_call(
        functools.partial(segment_kernel, sizes),
        out_shape=[
            jax.ShapeDtypeStruct((bz, by, bx), F32),
            jax.ShapeDtypeStruct((16 * bz * by, bx), F32),
        ],
        in_specs=[vmem] * 7,
        out_specs=[vmem] * 2,
        scratch_shapes=[room(by + 2, (bz + 5) * 16, bx), room(17 * bz * by, bx)],
        compiler_params=pltpu.CompilerParams(vmem_limit_bytes=GRANT),
        name="segment",
    )(*handed)
    return clean, features.reshape(16, bz, by, bx)


def solution(mesh):
    sizes = (mesh.shape["gz"], mesh.shape["gy"], mesh.shape["gx"])
    in_specs = (P(("win", "gz"), "gy", "gx"), P(), P(), P(), P(), P(), P(), P(), P(), P())
    out_specs = (P(("win", "gz"), "gy", "gx"), P(None, ("win", "gz"), "gy", "gx"))
    return jax.shard_map(
        functools.partial(body, sizes), mesh=mesh, in_specs=in_specs, out_specs=out_specs, check_vma=False
    )
```

```python
import functools

import jax
import jax.numpy as jnp
from jax import lax
from jax.experimental import pallas as pl
from jax.experimental.pallas import tpu as pltpu
from jax.sharding import PartitionSpec as P

LANES = 128
GRANT = 40 << 20
F32 = jnp.float32
BF16 = jnp.bfloat16
MESH = pl.DeviceIdType.MESH


def split(value):
    high = value.astype(BF16)
    return high, (value - high.astype(F32)).astype(BF16)


def left_rows(weight):
    high, low = split(weight)
    return jnp.concatenate([high, high, low], axis=1)


def right_rows(high, low):
    return jnp.concatenate([high, low, high], axis=0)


def mxu(left, right):
    return jnp.dot(left, right, preferred_element_type=F32)


def lane_of(shape):
    return lax.broadcasted_iota(jnp.int32, shape, len(shape) - 1)


def row_of(shape):
    return lax.broadcasted_iota(jnp.int32, shape, 0)


def column(row_ref):
    count = row_ref.shape[1]
    shape = (count, count)
    spread = jnp.broadcast_to(row_ref[...], shape)
    return jnp.sum(jnp.where(row_of(shape) == lane_of(shape), spread, 0.0), axis=1, keepdims=True)


def times(count, step, carry, backward=False):
    if count <= 16:
        for i in range(count):
            carry = step(count - 1 - i if backward else i, carry)
        return carry
    return lax.fori_loop(0, count, lambda i, c: step(count - 1 - i if backward else i, c), carry)


def aligned(start, unit):
    return start if isinstance(start, int) else pl.multiple_of(start, unit)


def matches(left, right):
    return jnp.where(left == right, 1.0, 0.0).astype(BF16)


def tap_parts(tap):
    plane = (tap >= 9).astype(jnp.int32) + (tap >= 18).astype(jnp.int32)
    rest = tap - 9 * plane
    line = (rest >= 3).astype(jnp.int32) + (rest >= 6).astype(jnp.int32)
    return plane, line, rest - 3 * line


def banded_rows(weight, bias, count, over_planes):
    outs, taps = weight.shape
    size = count + 2
    block = 10 * size
    shape = (taps, 3 * block)
    plane, line, step = tap_parts(row_of(shape))
    slow, fast = (line, plane) if over_planes else (plane, line)
    start = size * (3 * step + slow) + fast
    col = lane_of(shape)
    high, low = split(weight)
    shape = (outs, 3 * block)
    steady = jnp.zeros(shape, F32)
    for piece in range(3):
        piece_of = bias.astype(BF16).astype(F32)
        steady = jnp.where(lane_of(shape) == 9 * size + piece, piece_of, steady)
        bias = bias - piece_of
    parts = []
    for at in range(count):
        first = matches(col, start + at) + matches(col, start + at + block)
        last = matches(col, start + at + 2 * block)
        parts.append((mxu(high, first) + mxu(low, last) + steady).astype(BF16))
    return parts


def second_rows(turned, ins):
    return left_rows(
        jnp.concatenate(
            [
                jnp.concatenate(
                    [
                        turned[ins * (9 * a + 3 * b + c) : ins * (9 * a + 3 * b + c + 1)]
                        for c in range(3)
                        for b in range(3)
                    ],
                    axis=0,
                ).T
                for a in range(3)
            ],
            axis=0,
        )
    )


def last_rows(weight):
    outs, ins, taps = weight.shape
    shape = (taps, taps * ins)
    plane, line, step = tap_parts(row_of(shape))
    place = matches(3 * (3 * line + step) + plane, lane_of(shape) // ins)
    shape = (outs * ins, taps * ins)
    keep = (row_of(shape) % ins) == (lane_of(shape) % ins)
    shape = (outs, outs * ins)
    collect = matches(row_of(shape), lane_of(shape) // ins)
    parts = []
    for part in split(weight.reshape(outs * ins, taps)):
        grown = jnp.where(keep, mxu(part, place), 0.0).astype(BF16)
        parts.append(mxu(collect, grown).astype(BF16))
    third = taps * ins // 3
    high, low = (
        jnp.concatenate([p[:, third * b : third * (b + 1)] for b in range(3)], axis=0) for p in parts
    )
    return jnp.concatenate([high, high, low], axis=1)


def window_of(shifted, start, count, spare):
    halves = [
        jnp.concatenate([shifted[s, pl.ds(start, count), :] for s in three] + [spare], axis=0)
        for three in (range(3), range(3, 6))
    ]
    return right_rows(*split(jnp.concatenate(halves, axis=1)))


def store_shifts(shifted, where, value, beyond):
    size = value.shape[1]
    lane = lane_of(value.shape)
    shifted[0, where, :] = pltpu.roll(jnp.where(lane == size - 1, beyond, value), 1, 1)
    shifted[1, where, :] = value
    shifted[2, where, :] = pltpu.roll(jnp.where(lane == 0, beyond, value), size - 1, 1)
    shifted[3, where, :] = pltpu.roll(jnp.where(lane == size - 2, beyond, value), 1, 1)
    shifted[4, where, :] = beyond
    shifted[5, where, :] = pltpu.roll(jnp.where(lane == 1, beyond, value), size - 1, 1)


def stacked_shifts(field, count):
    size = field.shape[1] // 2
    inner, outer = field[:, 0:size], field[:, size:]
    lane = lane_of(inner.shape)
    fields = (
        pltpu.roll(jnp.where(lane == size - 1, outer, inner), 1, 1),
        inner,
        pltpu.roll(jnp.where(lane == 0, outer, inner), size - 1, 1),
    )
    return right_rows(
        *(
            jnp.concatenate(
                [jnp.concatenate([v[16 * j : 16 * j + 48] for j in range(count)], axis=1) for v in values],
                axis=0,
            )
            for values in zip(*(split(f) for f in fields))
        )
    )


def layers_kernel(
    sizes, ranks, bz, by, bx,
    noisy_any, w1_any, b1_any, w2_any, b2_any, head_any, w3_any, b3_any, w4_any, b4_any,
    own_ref, beside_ref, edge_ref, in_left_ref, out_left_ref, out_bias_ref,
    noisy_ref, w1_ref, b1_ref, w2_ref, b2_ref, head_ref, w3_ref, b3_ref, w4_ref, b4_ref, load_sem,
    m1, my, x1, halo, rim, send1, recv1,
    shifted, ready, product, fix, packed, packed_rim,
    x3, own_send, own_recv, beside_send, beside_recv, edge_send, corner_send, edge_recv,
):
    gz, gy, gx = sizes
    depth = gz * bz
    part = by // ranks
    lines = part + 4
    rows = part + 2
    me = lax.axis_index("gz")
    at_y = lax.axis_index("gy")
    at_x = lax.axis_index("gx")
    works = me < ranks
    turned_round = 1 - lax.rem(at_y, 2)
    mine = me + turned_round * (ranks - 1 - 2 * me)
    steps_y = (-1, 1) if gy > 1 else ()
    steps_x = (-1, 1) if gx > 1 else ()

    def exists(dy, dx):
        ok = None
        for where, step, count in ((at_y, dy, gy), (at_x, dx, gx)):
            if step == 0:
                continue
            here = where > 0 if step < 0 else where < count - 1
            ok = here if ok is None else ok & here
        return ok

    def both(first, second):
        return second if first is None else first if second is None else first & second

    def when(ok, action):
        if ok is None:
            action()
        else:
            pl.when(ok)(action)

    def device(z, dy, dx):
        return {
            "win": lax.axis_index("win"),
            "gz": z,
            "gy": lax.rem(at_y + dy + gy, gy),
            "gx": lax.rem(at_x + dx + gx, gx),
        }

    def peer(k):
        return lax.rem(me + k, gz)

    def rank_towards(dy):
        return 0 if dy > 0 else ranks - 1

    def home_towards(dy):
        rank = rank_towards(dy)
        return rank + (1 - turned_round) * (ranks - 1 - 2 * rank)

    def side(step):
        return (step + 1) // 2

    loads = [
        pltpu.make_async_copy(source, target, load_sem.at[i])
        for i, (source, target) in enumerate(
            (
                (noisy_any, noisy_ref),
                (w1_any.at[:, 0, :], w1_ref),
                (w2_any, w2_ref),
                (w3_any.at[:, 0, :], w3_ref),
                (w4_any, w4_ref),
                (b1_any, b1_ref),
                (b2_any, b2_ref),
                (head_any, head_ref),
                (b3_any, b3_ref),
                (b4_any, b4_ref),
            )
        )
    ]
    loads[0].start()
    barrier = pltpu.get_barrier_semaphore()

    def greet(dy, dx):
        for k in range(gz - 1, -1, -1):
            if (dy, dx, k) != (0, 0, 0):
                pl.semaphore_signal(barrier, inc=1, device_id=device(peer(k), dy, dx), device_id_type=MESH)

    for dy in steps_y:
        for dx in (0,) + steps_x:
            when(both(mine == rank_towards(-dy), exists(dy, dx)), functools.partial(greet, dy, dx))
    for dx in (0,) + steps_x:
        when(both(works, exists(0, dx)), functools.partial(greet, 0, dx))
    for load in loads[1:]:
        load.start()

    loads[0].wait()
    for index, first in ((0, 0), (1, by - 2)):
        for z in range(bz):
            halo[index, 2 * z : 2 * z + 2, :] = noisy_ref[z * by + first : z * by + first + 2, :]
    lane = lane_of((by, bx))
    corner = jnp.zeros((by, bx), F32)
    for z in range(bz):
        turned = pltpu.roll(noisy_ref[z * by : (z + 1) * by, :], 4 * z + 2, 1)
        corner = jnp.where((lane >= 4 * z) & (lane < 4 * z + 4), turned, corner)
    rim[...] = corner

    count_y = (at_y > 0).astype(jnp.int32) + (at_y < gy - 1).astype(jnp.int32)
    count_x = (at_x > 0).astype(jnp.int32) + (at_x < gx - 1).astype(jnp.int32)
    pl.semaphore_wait(
        barrier, ranks - works.astype(jnp.int32) + count_y + count_x * ranks + count_y * count_x
    )

    def rows_of(z, count):
        return pl.ds(aligned(z * count, count), count)

    def own_first(k, source):
        return pltpu.make_async_remote_copy(
            src_ref=noisy_ref,
            dst_ref=m1.at[rows_of(source, bz * by), :],
            send_sem=send1.at[0, k],
            recv_sem=recv1.at[0, source],
            device_id=device(k, 0, 0),
            device_id_type=MESH,
        )

    def halo_first(dy, source):
        return pltpu.make_async_remote_copy(
            src_ref=halo.at[side(dy)],
            dst_ref=my.at[side(-dy), rows_of(source, bz * 2), :],
            send_sem=send1.at[1, side(dy)],
            recv_sem=recv1.at[1 + side(-dy), source],
            device_id=device(home_towards(dy), dy, 0),
            device_id_type=MESH,
        )

    def edge_first(dx, k, source):
        return pltpu.make_async_remote_copy(
            src_ref=rim,
            dst_ref=x1.at[0, side(-dx), source],
            send_sem=send1.at[2 + side(dx), k],
            recv_sem=recv1.at[3 + side(-dx), source],
            device_id=device(k, 0, dx),
            device_id_type=MESH,
        )

    def corner_first(dy, dx, source):
        return pltpu.make_async_remote_copy(
            src_ref=rim,
            dst_ref=x1.at[1 + side(-dy), side(-dx), source],
            send_sem=send1.at[4 + side(dy), side(dx)],
            recv_sem=recv1.at[5 + 2 * side(-dy) + side(-dx), source],
            device_id=device(home_towards(dy), dy, dx),
            device_id_type=MESH,
        )

    early = []
    for dy in steps_y:
        early.append((exists(dy, 0), functools.partial(halo_first, dy)))
        for dx in steps_x:
            early.append((exists(dy, dx), functools.partial(corner_first, dy, dx)))
    for k in range(ranks):
        early.append((me != k, functools.partial(own_first, k)))
        for dx in steps_x:
            early.append((exists(0, dx), functools.partial(edge_first, dx, k)))
    for ok, make in early:
        when(ok, lambda make=make: make(me).start())

    for load in loads[1:]:
        load.wait()
    for index, ok in ((0, at_y == 0), (1, at_y == gy - 1)):
        def no_row(index=index):
            my[index] = jnp.zeros(my.shape[1:], F32)
            x1[1 + index] = jnp.zeros(x1.shape[1:], F32)
            beside_ref[index] = jnp.zeros(beside_ref.shape[1:], F32)
            x3[ranks + index] = jnp.zeros(x3.shape[1:], F32)
        pl.when(ok)(no_row)
    for index, ok in ((0, at_x == 0), (1, at_x == gx - 1)):
        def no_side(index=index):
            for slot in range(3):
                x1[slot, index] = jnp.zeros(x1.shape[2:], F32)
            for slot in range(ranks + 2):
                x3[slot, index] = jnp.zeros(x3.shape[2:], F32)
        pl.when(ok)(no_side)
    in_left_ref[...] = jnp.concatenate(
        banded_rows(w3_ref[...], column(b3_ref), bz + 2, True), axis=0
    )
    out_left_ref[...] = last_rows(w4_ref[...])
    out_bias_ref[...] = jnp.broadcast_to(column(b4_ref), out_bias_ref.shape)

    def own_last(k, target):
        return pltpu.make_async_remote_copy(
            src_ref=packed.at[target],
            dst_ref=own_ref.at[k],
            send_sem=own_send.at[target],
            recv_sem=own_recv.at[k],
            device_id=device(target, 0, 0),
            device_id_type=MESH,
        )

    def halo_last(dy, target):
        start = 0 if dy < 0 else (part - 2) * bx
        return pltpu.make_async_remote_copy(
            src_ref=packed.at[target, :, start : start + 2 * bx],
            dst_ref=beside_ref.at[side(-dy)],
            send_sem=beside_send.at[side(dy), target],
            recv_sem=beside_recv.at[side(-dy)],
            device_id=device(target, dy, 0),
            device_id_type=MESH,
        )

    def edge_last(dx, k, target):
        return pltpu.make_async_remote_copy(
            src_ref=packed_rim.at[target],
            dst_ref=x3.at[k, side(-dx)],
            send_sem=edge_send.at[side(dx), target],
            recv_sem=edge_recv.at[k, side(-dx)],
            device_id=device(target, 0, dx),
            device_id_type=MESH,
        )

    def corner_last(dy, dx, target):
        return pltpu.make_async_remote_copy(
            src_ref=packed_rim.at[target],
            dst_ref=x3.at[ranks + side(-dy), side(-dx)],
            send_sem=corner_send.at[side(dy), side(dx), target],
            recv_sem=edge_recv.at[ranks + side(-dy), side(-dx)],
            device_id=device(target, dy, dx),
            device_id_type=MESH,
        )

    late = []
    for target in range(gz):
        late.append((me != target, functools.partial(own_last, mine, target)))
        for dy in steps_y:
            ok = both(mine == rank_towards(-dy), exists(dy, 0))
            late.append((ok, functools.partial(halo_last, dy, target)))
        for dx in steps_x:
            late.append((exists(0, dx), functools.partial(edge_last, dx, mine, target)))
        for dy in steps_y:
            for dx in steps_x:
                ok = both(mine == rank_towards(-dy), exists(dy, dx))
                late.append((ok, functools.partial(corner_last, dy, dx, target)))

    for ok, make in early:
        when(ok, lambda make=make: make(me).wait_send())

    @pl.when(works)
    def layers():
        gate_bias = jnp.concatenate([jnp.zeros((16, 1), F32), column(b1_ref)], axis=0)
        parts = banded_rows(w1_ref[...].T, gate_bias, rows, False)
        first_left = jnp.concatenate([p[:16] for p in parts] + [p[16:] for p in parts], axis=0)
        second_left = second_rows(w2_ref[...].reshape(-1, w2_ref.shape[2]), w2_ref.shape[1])
        second_bias = column(b2_ref)
        head = column(head_ref)
        shape = (16 * rows, 2 * bx)
        lane, row = lane_of(shape), row_of(shape)
        place_y = at_y * by + mine * part + row // 16 - 1
        outside = (place_y < 0) | (place_y >= gy * by)
        outside = outside | ((at_x == 0) & (lane == 2 * bx - 1)) | ((at_x == gx - 1) & (lane == bx))
        mask = jnp.where(outside, 0.0, 1.0).astype(F32)
        for s in range(6):
            for plane in (0, depth + 1):
                shifted[s, plane * lines : (plane + 1) * lines, :] = jnp.zeros((lines, bx), F32)
        for plane in (0, depth + 1):
            product[plane] = jnp.zeros(product.shape[1:], F32)
        fix[...] = jnp.zeros(fix.shape, F32)
        m1[rows_of(me, bz * by), :] = noisy_ref[...]

        def arrive(m):
            def await_own():
                own_first(0, m).wait_recv()
            pl.when(me != m)(await_own)
            for dx in steps_x:
                def await_edge(dx=dx):
                    edge_first(-dx, 0, m).wait_recv()
                when(exists(0, dx), await_edge)
            for dy in steps_y:
                def await_halo(dy=dy):
                    halo_first(-dy, m).wait_recv()
                when(both(mine == rank_towards(-dy), exists(dy, 0)), await_halo)
                for dx in steps_x:
                    def await_corner(dy=dy, dx=dx):
                        corner_first(-dy, -dx, m).wait_recv()
                    when(both(mine == rank_towards(-dy), exists(dy, dx)), await_corner)

        place = lane_of((by, bx)) % 4

        def cut(full):
            value = full[0:lines]
            for k in range(1, ranks):
                value = jnp.where(mine == k, full[part * k : part * k + lines], value)
            return value

        def gather(m):
            rims = [jnp.where(place < 2, x1[slot, 0, m], x1[slot, 1, m]) for slot in range(3)]
            border = cut(jnp.concatenate([rims[1][by - 2 : by], rims[0], rims[2][0:2]], axis=0))
            below = my[0, rows_of(m, bz * 2), :]
            above = my[1, rows_of(m, bz * 2), :]
            block = m1[rows_of(m, bz * by), :]
            for z in range(bz):
                value = cut(
                    jnp.concatenate(
                        [below[2 * z : 2 * z + 2], block[z * by : (z + 1) * by], above[2 * z : 2 * z + 2]],
                        axis=0,
                    )
                )
                beyond = pltpu.roll(border, (bx - 2 - 4 * z) % bx, 1)
                where = pl.ds(aligned((m * bz + z + 1) * lines, lines), lines)
                store_shifts(shifted, where, value, beyond)

        spare = jnp.ones((lines, bx), F32)

        def gates(z, slot):
            pre = mxu(first_left, window_of(shifted, aligned(z * lines, lines), 3 * lines, spare))
            ready[0, slot] = mask * jnp.tanh(pre[0 : 16 * rows])
            ready[1, slot] = jax.nn.sigmoid(pre[16 * rows :])

        def advance(z, slot, hidden):
            hidden = hidden + ready[1, slot] * (ready[0, slot] - hidden)
            product[z + 1] = mxu(second_left, stacked_shifts(hidden, part))
            return hidden

        def reach(m, first, count, hidden):
            arrive(m)
            gather(m)
            for slot in range(count):
                gates(first + slot, slot)
            for slot in range(count):
                hidden = advance(first + slot, slot, hidden)
            return hidden

        def later(i, hidden):
            return reach(i + 1, (i + 1) * bz - 1, bz, hidden)

        hidden = reach(0, 0, bz - 1, jnp.zeros((16 * rows, 2 * bx), F32))
        hidden = times(gz - 2, later, hidden)
        reach(gz - 1, depth - bz - 1, bz + 1, hidden)

        def back(z, hidden):
            pre = product[z, 0:32] + product[z + 1, 32:64] + product[z + 2, 64:96]
            cand = jnp.tanh(pre[0:16])
            change = jax.nn.sigmoid(pre[16:32] + second_bias)
            hidden = hidden + change * (cand - hidden)
            fix[pl.ds(z + 2, 1), :] = jnp.sum(head * hidden, axis=0, keepdims=True)
            return hidden

        times(depth, back, jnp.zeros((16, part * bx), F32), True)
        lane = lane_of((fix.shape[0], bx))
        border = jnp.zeros((fix.shape[0], bx), F32)
        for j in range(part):
            lanes = slice(j * bx, (j + 1) * bx)
            centre = shifted[1, pl.ds(lines + j + 2, depth, stride=lines), :]
            fix[2 : 2 + depth, lanes] = fix[2 : 2 + depth, lanes] + centre
            turned = pltpu.roll(fix[:, lanes], 4 * j + 2, 1)
            border = jnp.where((lane >= 4 * j) & (lane < 4 * j + 4), turned, border)
        for target in range(gz):
            packed[target] = fix[bz * target : bz * target + bz + 4, :]
            packed_rim[target] = border[bz * target : bz * target + bz + 4]
        for ok, make in late:
            when(ok, lambda make=make: make().start())
        own_ref[mine] = packed[me]

    for k in range(ranks):
        def await_own(k=k):
            own_last(k, 0).wait_recv()
        pl.when(mine != k)(await_own)
    for dy in steps_y:
        def await_beside(dy=dy):
            halo_last(-dy, 0).wait_recv()
        when(exists(dy, 0), await_beside)
    for dx in steps_x:
        def await_rims(dx=dx):
            for k in range(ranks):
                edge_last(-dx, k, 0).wait_recv()
        when(exists(0, dx), await_rims)
        for dy in steps_y:
            def await_corner(dy=dy, dx=dx):
                corner_last(-dy, -dx, 0).wait_recv()
            when(exists(dy, dx), await_corner)
    place = lane_of((bz + 4, bx)) % 4
    for line in range(by + 4):
        if line < 2:
            slot, j = ranks, part - 2 + line
        elif line < by + 2:
            slot, j = (line - 2) // part, (line - 2) % part
        else:
            slot, j = ranks + 1, line - by - 2
        beyond = jnp.where(place < 2, x3[slot, 0], x3[slot, 1])
        edge_ref[line] = pltpu.roll(beyond, (bx - 2 - 4 * j) % bx, 1)

    @pl.when(works)
    def drain():
        for ok, make in late:
            when(ok, lambda make=make: make().wait_send())


def segment_kernel(
    sizes, own_ref, beside_ref, edge_ref, in_left_ref, out_left_ref, out_bias_ref,
    clean_ref, out_ref, shifted, ready, product, result,
):
    gz, gy, gx = sizes
    ranks = own_ref.shape[0]
    lines, planes, bx = edge_ref.shape
    by, bz = lines - 4, planes - 4
    part = by // ranks
    me = lax.axis_index("gz")
    at_y = lax.axis_index("gy")
    at_x = lax.axis_index("gx")

    def middle_of(line):
        if 2 <= line < by + 2:
            k, j = divmod(line - 2, part)
            return own_ref[k, :, j * bx : (j + 1) * bx]
        index, j = (0, line) if line < 2 else (1, line - by - 2)
        return beside_ref[index, :, j * bx : (j + 1) * bx]

    for line in range(lines):
        store_shifts(shifted, slice(line * planes, (line + 1) * planes), middle_of(line), edge_ref[line])
    in_left = in_left_ref[...]
    out_left = out_left_ref[...]
    out_bias = out_bias_ref[:, 0:1]
    shape = (16 * (bz + 2), 2 * bx)
    lane, plane = lane_of(shape), row_of(shape) // 16
    outside = ((me == 0) & (plane == 0)) | ((me == gz - 1) & (plane == bz + 1))
    outside = outside | ((at_x == 0) & (lane == 2 * bx - 1)) | ((at_x == gx - 1) & (lane == bx))
    mask = jnp.where(outside, 0.0, 1.0).astype(F32)
    spare = jnp.ones((planes, bx), F32)
    for y in range(by + 2):
        grown = jnp.maximum(mxu(in_left, window_of(shifted, y * planes, 3 * planes, spare)), 0.0) * mask
        if y == 0:
            grown = grown * jnp.where(at_y > 0, 1.0, 0.0).astype(F32)
        if y == by + 1:
            grown = grown * jnp.where(at_y < gy - 1, 1.0, 0.0).astype(F32)
        ready[y] = grown
    for z in range(bz):
        for y in range(by):
            clean_ref[z, y : y + 1, :] = middle_of(2 + y)[2 + z : 3 + z]
    for y in range(by + 2):
        product[y] = mxu(out_left, stacked_shifts(ready[y], bz))
        if y >= 2:
            total = product[y - 2, 0:16] + product[y - 1, 16:32] + product[y, 32:48] + out_bias
            for z in range(bz):
                result[pl.ds(z * by + y - 2, 16, stride=bz * by), :] = total[:, z * bx : (z + 1) * bx]
    out_ref[...] = result[0 : 16 * bz * by, :]


def body(sizes, noisy, first_weight, first_bias, second_weight, second_bias, head_weight,
         seg_weight_in, seg_bias_in, seg_weight_out, seg_bias_out):
    gz, gy, gx = sizes
    bz, by, bx = noisy.shape
    ranks = by // 4
    part = by // ranks
    lines = part + 4
    depth = gz * bz
    args = [
        noisy.reshape(bz * by, bx),
        first_weight.transpose(2, 1, 0),
        first_bias.reshape(1, -1),
        second_weight.transpose(2, 1, 0),
        second_bias.reshape(1, -1),
        head_weight.reshape(1, -1),
        seg_weight_in,
        seg_bias_in.reshape(1, -1),
        seg_weight_out,
        seg_bias_out.reshape(1, -1),
    ]
    vmem = pl.BlockSpec(memory_space=pltpu.VMEM)
    dma = pltpu.SemaphoreType.DMA
    rest = pl.BlockSpec(memory_space=pl.ANY)

    def room(*shape):
        return pltpu.VMEM(shape, F32)

    stages = [
        room(*(a.shape if i not in (1, 6) else (a.shape[0], a.shape[2]))) for i, a in enumerate(args)
    ]
    handed = pl.pallas_call(
        functools.partial(layers_kernel, sizes, ranks, bz, by, bx),
        out_shape=[
            room(ranks, bz + 4, part * bx),
            room(2, bz + 4, 2 * bx),
            room(by + 4, bz + 4, bx),
            pltpu.VMEM((16 * (bz + 2), 30 * (bz + 4)), BF16),
            pltpu.VMEM((48, 432), BF16),
            room(16, LANES),
        ],
        in_specs=[rest] * len(args),
        out_specs=[vmem] * 6,
        scratch_shapes=stages
        + [
            dma((len(args),)),
            room(depth * by, bx),
            room(2, depth * 2, bx),
            room(3, 2, gz, by, bx),
            room(2, bz * 2, bx),
            room(by, bx),
            dma((6, max(ranks, 2))),
            dma((9, gz)),
            room(6, (depth + 2) * lines, bx),
            room(2, bz + 1, 16 * (part + 2), 2 * bx),
            room(depth + 2, 96, part * bx),
            room(depth + 16, part * bx),
            room(gz, bz + 4, part * bx),
            room(gz, bz + 4, bx),
            room(ranks + 2, 2, bz + 4, bx),
            dma((gz,)),
            dma((ranks,)),
            dma((2, gz)),
            dma((2,)),
            dma((2, gz)),
            dma((2, 2, gz)),
            dma((ranks + 2, 2)),
        ],
        compiler_params=pltpu.CompilerParams(
            collective_id=0, has_side_effects=True, vmem_limit_bytes=GRANT
        ),
        name="layers",
    )(*(pltpu.with_memory_space_constraint(a, pltpu.HBM) for a in args))
    clean, features = pl.pallas_call(
        functools.partial(segment_kernel, sizes),
        out_shape=[
            jax.ShapeDtypeStruct((bz, by, bx), F32),
            jax.ShapeDtypeStruct((16 * bz * by, bx), F32),
        ],
        in_specs=[vmem] * 6,
        out_specs=[vmem] * 2,
        scratch_shapes=[
            room(6, (by + 4) * (bz + 4), bx),
            room(by + 2, 16 * (bz + 2), 2 * bx),
            room(by + 2, 48, bz * bx),
            room(17 * bz * by, bx),
        ],
        compiler_params=pltpu.CompilerParams(vmem_limit_bytes=GRANT),
        name="segment",
    )(*handed)
    return clean, features.reshape(16, bz, by, bx)


def solution(mesh):
    sizes = (mesh.shape["gz"], mesh.shape["gy"], mesh.shape["gx"])
    in_specs = (P(("win", "gz"), "gy", "gx"), P(), P(), P(), P(), P(), P(), P(), P(), P())
    out_specs = (P(("win", "gz"), "gy", "gx"), P(None, ("win", "gz"), "gy", "gx"))
    return jax.shard_map(
        functools.partial(body, sizes), mesh=mesh, in_specs=in_specs, out_specs=out_specs, check_vma=False
    )
```

```python
import functools

import jax
import jax.numpy as jnp
from jax import lax
from jax.experimental import pallas as pl
from jax.experimental.pallas import tpu as pltpu
from jax.sharding import PartitionSpec as P

LANES = 128
GRANT = 40 << 20
F32 = jnp.float32
BF16 = jnp.bfloat16
MESH = pl.DeviceIdType.MESH


def split(value):
    high = value.astype(BF16)
    return high, (value - high.astype(F32)).astype(BF16)


def left_rows(weight):
    high, low = split(weight)
    return jnp.concatenate([high, high, low], axis=1)


def right_rows(high, low):
    return jnp.concatenate([high, low, high], axis=0)


def mxu(left, right):
    return jnp.dot(left, right, preferred_element_type=F32)


def lane_of(shape):
    return lax.broadcasted_iota(jnp.int32, shape, len(shape) - 1)


def row_of(shape):
    return lax.broadcasted_iota(jnp.int32, shape, 0)


def column(row_ref):
    count = row_ref.shape[1]
    shape = (count, count)
    spread = jnp.broadcast_to(row_ref[...], shape)
    return jnp.sum(jnp.where(row_of(shape) == lane_of(shape), spread, 0.0), axis=1, keepdims=True)


def times(count, step, carry, backward=False):
    if count <= 16:
        for i in range(count):
            carry = step(count - 1 - i if backward else i, carry)
        return carry
    return lax.fori_loop(0, count, lambda i, c: step(count - 1 - i if backward else i, c), carry)


class Step:
    def __init__(self, step, side, ok):
        self.step, self.side, self.ok = step, side, ok

    def back(self):
        return Step(-self.step, 1 - self.side, self.ok)


def steps_along(at, count):
    if count == 1:
        return []
    if count == 2:
        return [Step(1 - 2 * at, 1 - at, None)]
    return [Step(-1, 0, at > 0), Step(1, 1, at < count - 1)]


STAY = Step(0, 0, None)


def aligned(start, unit):
    return start if isinstance(start, int) else pl.multiple_of(start, unit)


def matches(left, right):
    return jnp.where(left == right, 1.0, 0.0).astype(BF16)


def tap_parts(tap):
    plane = (tap >= 9).astype(jnp.int32) + (tap >= 18).astype(jnp.int32)
    rest = tap - 9 * plane
    line = (rest >= 3).astype(jnp.int32) + (rest >= 6).astype(jnp.int32)
    return plane, line, rest - 3 * line


def banded_rows(weight, bias, count, over_planes):
    outs, taps = weight.shape
    size = count + 2
    block = 10 * size
    shape = (taps, 3 * block)
    plane, line, step = tap_parts(row_of(shape))
    slow, fast = (line, plane) if over_planes else (plane, line)
    start = size * (3 * step + slow) + fast
    col = lane_of(shape)
    high, low = split(weight)
    shape = (outs, 3 * block)
    steady = jnp.zeros(shape, F32)
    for piece in range(3):
        piece_of = bias.astype(BF16).astype(F32)
        steady = jnp.where(lane_of(shape) == 9 * size + piece, piece_of, steady)
        bias = bias - piece_of
    parts = []
    for at in range(count):
        first = matches(col, start + at) + matches(col, start + at + block)
        last = matches(col, start + at + 2 * block)
        parts.append((mxu(high, first) + mxu(low, last) + steady).astype(BF16))
    return parts


def second_rows(turned, ins):
    return left_rows(
        jnp.concatenate(
            [
                jnp.concatenate(
                    [
                        turned[ins * (9 * a + 3 * b + c) : ins * (9 * a + 3 * b + c + 1)]
                        for c in range(3)
                        for b in range(3)
                    ],
                    axis=0,
                ).T
                for a in range(3)
            ],
            axis=0,
        )
    )


def last_rows(weight):
    outs, ins, taps = weight.shape
    shape = (taps, taps * ins)
    plane, line, step = tap_parts(row_of(shape))
    place = matches(3 * (3 * line + step) + plane, lane_of(shape) // ins)
    shape = (outs * ins, taps * ins)
    keep = (row_of(shape) % ins) == (lane_of(shape) % ins)
    shape = (outs, outs * ins)
    collect = matches(row_of(shape), lane_of(shape) // ins)
    parts = []
    for part in split(weight.reshape(outs * ins, taps)):
        grown = jnp.where(keep, mxu(part, place), 0.0).astype(BF16)
        parts.append(mxu(collect, grown).astype(BF16))
    third = taps * ins // 3
    high, low = (
        jnp.concatenate([p[:, third * b : third * (b + 1)] for b in range(3)], axis=0) for p in parts
    )
    return jnp.concatenate([high, low], axis=0)


def window_of(shifted, start, count, spare):
    halves = [
        jnp.concatenate([shifted[s, pl.ds(start, count), :] for s in three] + [spare], axis=0)
        for three in (range(3), range(3, 6))
    ]
    return right_rows(*split(jnp.concatenate(halves, axis=1)))


def store_shifts(shifted, where, value, beyond):
    size = value.shape[1]
    lane = lane_of(value.shape)
    shifted[0, where, :] = pltpu.roll(jnp.where(lane == size - 1, beyond, value), 1, 1)
    shifted[1, where, :] = value
    shifted[2, where, :] = pltpu.roll(jnp.where(lane == 0, beyond, value), size - 1, 1)
    shifted[3, where, :] = pltpu.roll(jnp.where(lane == size - 2, beyond, value), 1, 1)
    shifted[4, where, :] = beyond
    shifted[5, where, :] = pltpu.roll(jnp.where(lane == 1, beyond, value), size - 1, 1)


def stacked_shifts(field, count):
    size = field.shape[1] // 2
    inner, outer = field[:, 0:size], field[:, size:]
    lane = lane_of(inner.shape)
    fields = (
        pltpu.roll(jnp.where(lane == size - 1, outer, inner), 1, 1),
        inner,
        pltpu.roll(jnp.where(lane == 0, outer, inner), size - 1, 1),
    )
    return tuple(
        jnp.concatenate(
            [jnp.concatenate([v[16 * j : 16 * j + 48] for j in range(count)], axis=1) for v in values],
            axis=0,
        )
        for values in zip(*(split(f) for f in fields))
    )


def layers_kernel(
    sizes, ranks, bz, by, bx,
    noisy_any, w1_any, b1_any, w2_any, b2_any, head_any, w3_any, b3_any, w4_any, b4_any,
    own_ref, beside_ref, edge_ref, in_left_ref, out_left_ref, out_bias_ref,
    noisy_ref, w1_ref, b1_ref, w2_ref, b2_ref, head_ref, w3_ref, b3_ref, w4_ref, b4_ref, load_sem,
    m1, my, x1, halo, rim, send1, recv1,
    shifted, ready, product, fix, packed, packed_rim,
    x3, own_send, own_recv, beside_send, beside_recv, edge_send, corner_send, edge_recv,
):
    gz, gy, gx = sizes
    depth = gz * bz
    part = by // ranks
    lines = part + 4
    rows = part + 2
    me = lax.axis_index("gz")
    at_y = lax.axis_index("gy")
    at_x = lax.axis_index("gx")
    works = me < ranks
    turned_round = 1 - lax.rem(at_y, 2)
    mine = me + turned_round * (ranks - 1 - 2 * me)
    steps_y = steps_along(at_y, gy)
    steps_x = steps_along(at_x, gx)

    def both(first, second):
        return second if first is None else first if second is None else first & second

    def when(ok, action):
        if ok is None:
            action()
        else:
            pl.when(ok)(action)

    def device(z, dy, dx):
        return {
            "win": lax.axis_index("win"),
            "gz": z,
            "gy": lax.rem(at_y + dy.step + gy, gy),
            "gx": lax.rem(at_x + dx.step + gx, gx),
        }

    def peer(k):
        return lax.rem(me + k, gz)

    def rank_towards(dy):
        return (1 - dy.side) * (ranks - 1)

    def beside(dy):
        return both(mine == rank_towards(dy.back()), dy.ok)

    def home_towards(dy):
        rank = rank_towards(dy)
        return rank + (1 - turned_round) * (ranks - 1 - 2 * rank)

    loads = [
        pltpu.make_async_copy(source, target, load_sem.at[i])
        for i, (source, target) in enumerate(
            (
                (noisy_any, noisy_ref),
                (w1_any.at[:, 0, :], w1_ref),
                (w2_any, w2_ref),
                (w3_any.at[:, 0, :], w3_ref),
                (w4_any, w4_ref),
                (b1_any, b1_ref),
                (b2_any, b2_ref),
                (head_any, head_ref),
                (b3_any, b3_ref),
                (b4_any, b4_ref),
            )
        )
    ]
    loads[0].start()
    barrier = pltpu.get_barrier_semaphore()

    def greet(dy, dx):
        for k in range(gz - 1, 0 if dy is STAY and dx is STAY else -1, -1):
            pl.semaphore_signal(barrier, inc=1, device_id=device(peer(k), dy, dx), device_id_type=MESH)

    for dy in steps_y:
        @functools.partial(when, beside(dy))
        def greet_beside(dy=dy):
            for dx in [STAY] + steps_x:
                when(dx.ok, functools.partial(greet, dy, dx))

    @pl.when(works)
    def greet_along():
        for dx in [STAY] + steps_x:
            when(dx.ok, functools.partial(greet, STAY, dx))

    for load in loads[1:]:
        load.start()

    loads[0].wait()
    for index, first in ((0, 0), (1, by - 2)):
        for z in range(bz):
            halo[index, 2 * z : 2 * z + 2, :] = noisy_ref[z * by + first : z * by + first + 2, :]
    lane = lane_of((by, bx))
    corner = jnp.zeros((by, bx), F32)
    for z in range(bz):
        turned = pltpu.roll(noisy_ref[z * by : (z + 1) * by, :], 4 * z + 2, 1)
        corner = jnp.where((lane >= 4 * z) & (lane < 4 * z + 4), turned, corner)
    rim[...] = corner

    count_y = (at_y > 0).astype(jnp.int32) + (at_y < gy - 1).astype(jnp.int32)
    count_x = (at_x > 0).astype(jnp.int32) + (at_x < gx - 1).astype(jnp.int32)
    pl.semaphore_wait(
        barrier, ranks - works.astype(jnp.int32) + count_y + count_x * ranks + count_y * count_x
    )

    def rows_of(z, count):
        return pl.ds(aligned(z * count, count), count)

    def own_first(k, source):
        return pltpu.make_async_remote_copy(
            src_ref=noisy_ref,
            dst_ref=m1.at[rows_of(source, bz * by), :],
            send_sem=send1.at[0, k],
            recv_sem=recv1.at[0, source],
            device_id=device(k, STAY, STAY),
            device_id_type=MESH,
        )

    def halo_first(dy, source):
        return pltpu.make_async_remote_copy(
            src_ref=halo.at[dy.side],
            dst_ref=my.at[1 - dy.side, rows_of(source, bz * 2), :],
            send_sem=send1.at[1, dy.side],
            recv_sem=recv1.at[2 - dy.side, source],
            device_id=device(home_towards(dy), dy, STAY),
            device_id_type=MESH,
        )

    def edge_first(dx, k, source):
        return pltpu.make_async_remote_copy(
            src_ref=rim,
            dst_ref=x1.at[0, 1 - dx.side, source],
            send_sem=send1.at[2 + dx.side, k],
            recv_sem=recv1.at[4 - dx.side, source],
            device_id=device(k, STAY, dx),
            device_id_type=MESH,
        )

    def corner_first(dy, dx, source):
        return pltpu.make_async_remote_copy(
            src_ref=rim,
            dst_ref=x1.at[2 - dy.side, 1 - dx.side, source],
            send_sem=send1.at[4 + dy.side, dx.side],
            recv_sem=recv1.at[8 - 2 * dy.side - dx.side, source],
            device_id=device(home_towards(dy), dy, dx),
            device_id_type=MESH,
        )

    early = []
    for dy in steps_y:
        early.append((dy.ok, functools.partial(halo_first, dy)))
        for dx in steps_x:
            early.append((both(dy.ok, dx.ok), functools.partial(corner_first, dy, dx)))
    for k in range(ranks):
        early.append((me != k, functools.partial(own_first, k)))
        for dx in steps_x:
            early.append((dx.ok, functools.partial(edge_first, dx, k)))
    for ok, make in early:
        when(ok, lambda make=make: make(me).start())

    for load in loads[1:]:
        load.wait()
    for index, ok in ((0, at_y == 0), (1, at_y == gy - 1)):
        def no_row(index=index):
            my[index] = jnp.zeros(my.shape[1:], F32)
            x1[1 + index] = jnp.zeros(x1.shape[1:], F32)
            beside_ref[index] = jnp.zeros(beside_ref.shape[1:], F32)
            x3[ranks + index] = jnp.zeros(x3.shape[1:], F32)
        pl.when(ok)(no_row)
    for index, ok in ((0, at_x == 0), (1, at_x == gx - 1)):
        def no_side(index=index):
            for slot in range(3):
                x1[slot, index] = jnp.zeros(x1.shape[2:], F32)
            for slot in range(ranks + 2):
                x3[slot, index] = jnp.zeros(x3.shape[2:], F32)
        pl.when(ok)(no_side)
    in_left_ref[...] = jnp.concatenate(
        banded_rows(w3_ref[...], column(b3_ref), bz + 2, True), axis=0
    )
    out_left_ref[...] = last_rows(w4_ref[...])
    out_bias_ref[...] = jnp.broadcast_to(column(b4_ref), out_bias_ref.shape)

    def own_last(k, target):
        return pltpu.make_async_remote_copy(
            src_ref=packed.at[target],
            dst_ref=own_ref.at[k],
            send_sem=own_send.at[target],
            recv_sem=own_recv.at[k],
            device_id=device(target, STAY, STAY),
            device_id_type=MESH,
        )

    def halo_last(dy, target):
        start = aligned(dy.side * ((part - 2) * bx), LANES)
        return pltpu.make_async_remote_copy(
            src_ref=packed.at[target, :, pl.ds(start, 2 * bx)],
            dst_ref=beside_ref.at[1 - dy.side],
            send_sem=beside_send.at[dy.side, target],
            recv_sem=beside_recv.at[1 - dy.side],
            device_id=device(target, dy, STAY),
            device_id_type=MESH,
        )

    def edge_last(dx, k, target):
        return pltpu.make_async_remote_copy(
            src_ref=packed_rim.at[target],
            dst_ref=x3.at[k, 1 - dx.side],
            send_sem=edge_send.at[dx.side, target],
            recv_sem=edge_recv.at[k, 1 - dx.side],
            device_id=device(target, STAY, dx),
            device_id_type=MESH,
        )

    def corner_last(dy, dx, target):
        return pltpu.make_async_remote_copy(
            src_ref=packed_rim.at[target],
            dst_ref=x3.at[ranks + 1 - dy.side, 1 - dx.side],
            send_sem=corner_send.at[dy.side, dx.side, target],
            recv_sem=edge_recv.at[ranks + 1 - dy.side, 1 - dx.side],
            device_id=device(target, dy, dx),
            device_id_type=MESH,
        )

    def late(act):
        def to_beside(dy, targets):
            for target in targets:
                act(halo_last(dy, target))
                for dx in steps_x:
                    when(dx.ok, lambda: act(corner_last(dy, dx, target)))

        def to_own(target):
            act(own_last(mine, target))

        def to_edge(target):
            for dx in steps_x:
                when(dx.ok, lambda: act(edge_last(dx, mine, target)))

        for dy in steps_y:
            when(beside(dy), functools.partial(to_beside, dy, range(ranks)))
        for k in range(1, ranks):
            to_own(lax.rem(me + k, ranks))
        for target in range(ranks):
            to_edge(target)
        for target in range(ranks, gz):
            to_own(target)
            to_edge(target)
        for dy in steps_y:
            when(beside(dy), functools.partial(to_beside, dy, range(ranks, gz)))

    for ok, make in early:
        when(ok, lambda make=make: make(me).wait_send())

    @pl.when(works)
    def layers():
        gate_bias = jnp.concatenate([jnp.zeros((16, 1), F32), column(b1_ref)], axis=0)
        parts = banded_rows(w1_ref[...].T, gate_bias, rows, False)
        first_left = jnp.concatenate([p[:16] for p in parts] + [p[16:] for p in parts], axis=0)
        second_left = second_rows(w2_ref[...].reshape(-1, w2_ref.shape[2]), w2_ref.shape[1])
        second_bias = column(b2_ref)
        head = column(head_ref)
        shape = (16 * rows, 2 * bx)
        lane, row = lane_of(shape), row_of(shape)
        place_y = at_y * by + mine * part + row // 16 - 1
        outside = (place_y < 0) | (place_y >= gy * by)
        outside = outside | ((at_x == 0) & (lane == 2 * bx - 1)) | ((at_x == gx - 1) & (lane == bx))
        mask = jnp.where(outside, 0.0, 1.0).astype(F32)
        for s in range(6):
            for plane in (0, depth + 1):
                shifted[s, plane * lines : (plane + 1) * lines, :] = jnp.zeros((lines, bx), F32)
        for plane in (0, depth + 1):
            product[plane] = jnp.zeros(product.shape[1:], F32)
        fix[...] = jnp.zeros(fix.shape, F32)
        m1[rows_of(me, bz * by), :] = noisy_ref[...]

        def arrive(m):
            def await_own():
                own_first(0, m).wait_recv()
            pl.when(me != m)(await_own)
            for dx in steps_x:
                def await_edge(dx=dx):
                    edge_first(dx.back(), 0, m).wait_recv()
                when(dx.ok, await_edge)
            for dy in steps_y:
                @functools.partial(when, beside(dy))
                def await_beside(dy=dy):
                    halo_first(dy.back(), m).wait_recv()
                    for dx in steps_x:
                        def await_corner(dx=dx):
                            corner_first(dy.back(), dx.back(), m).wait_recv()
                        when(dx.ok, await_corner)

        place = lane_of((by, bx)) % 4

        def cut(full):
            value = full[0:lines]
            for k in range(1, ranks):
                value = jnp.where(mine == k, full[part * k : part * k + lines], value)
            return value

        def gather(m):
            rims = [jnp.where(place < 2, x1[slot, 0, m], x1[slot, 1, m]) for slot in range(3)]
            border = cut(jnp.concatenate([rims[1][by - 2 : by], rims[0], rims[2][0:2]], axis=0))
            below = my[0, rows_of(m, bz * 2), :]
            above = my[1, rows_of(m, bz * 2), :]
            block = m1[rows_of(m, bz * by), :]
            for z in range(bz):
                value = cut(
                    jnp.concatenate(
                        [below[2 * z : 2 * z + 2], block[z * by : (z + 1) * by], above[2 * z : 2 * z + 2]],
                        axis=0,
                    )
                )
                beyond = pltpu.roll(border, (bx - 2 - 4 * z) % bx, 1)
                where = pl.ds(aligned((m * bz + z + 1) * lines, lines), lines)
                store_shifts(shifted, where, value, beyond)

        spare = jnp.ones((lines, bx), F32)

        def gates(z, slot):
            pre = mxu(first_left, window_of(shifted, aligned(z * lines, lines), 3 * lines, spare))
            ready[0, slot] = mask * jnp.tanh(pre[0 : 16 * rows])
            ready[1, slot] = jax.nn.sigmoid(pre[16 * rows :])

        def advance(z, slot, hidden):
            hidden = hidden + ready[1, slot] * (ready[0, slot] - hidden)
            product[z + 1] = mxu(second_left, right_rows(*stacked_shifts(hidden, part)))
            return hidden

        def reach(m, first, count, hidden):
            arrive(m)
            gather(m)
            for slot in range(count):
                gates(first + slot, slot)
            for slot in range(count):
                hidden = advance(first + slot, slot, hidden)
            return hidden

        def later(i, hidden):
            return reach(i + 1, (i + 1) * bz - 1, bz, hidden)

        hidden = reach(0, 0, bz - 1, jnp.zeros((16 * rows, 2 * bx), F32))
        hidden = times(gz - 2, later, hidden)
        reach(gz - 1, depth - bz - 1, bz + 1, hidden)

        def back(z, hidden):
            pre = product[z, 0:32] + product[z + 1, 32:64] + product[z + 2, 64:96]
            cand = jnp.tanh(pre[0:16])
            change = jax.nn.sigmoid(pre[16:32] + second_bias)
            hidden = hidden + change * (cand - hidden)
            fix[pl.ds(z + 2, 1), :] = jnp.sum(head * hidden, axis=0, keepdims=True)
            return hidden

        times(depth, back, jnp.zeros((16, part * bx), F32), True)
        lane = lane_of((fix.shape[0], bx))
        border = jnp.zeros((fix.shape[0], bx), F32)
        for j in range(part):
            lanes = slice(j * bx, (j + 1) * bx)
            centre = shifted[1, pl.ds(lines + j + 2, depth, stride=lines), :]
            fix[2 : 2 + depth, lanes] = fix[2 : 2 + depth, lanes] + centre
            turned = pltpu.roll(fix[:, lanes], 4 * j + 2, 1)
            border = jnp.where((lane >= 4 * j) & (lane < 4 * j + 4), turned, border)
        for target in range(gz):
            packed[target] = fix[bz * target : bz * target + bz + 4, :]
            packed_rim[target] = border[bz * target : bz * target + bz + 4]
        late(lambda copy: copy.start())
        own_ref[mine] = packed[me]
        late(lambda copy: copy.wait_send())

    for k in range(ranks):
        def await_own(k=k):
            own_last(k, 0).wait_recv()
        pl.when(mine != k)(await_own)
    for dy in steps_y:
        def await_beside(dy=dy):
            halo_last(dy.back(), 0).wait_recv()
        when(dy.ok, await_beside)
    for dx in steps_x:
        def await_rims(dx=dx):
            for k in range(ranks):
                edge_last(dx.back(), k, 0).wait_recv()
        when(dx.ok, await_rims)
        for dy in steps_y:
            def await_corner(dy=dy, dx=dx):
                corner_last(dy.back(), dx.back(), 0).wait_recv()
            when(both(dy.ok, dx.ok), await_corner)
    place = lane_of((bz + 4, bx)) % 4
    for line in range(by + 4):
        if line < 2:
            slot, j = ranks, part - 2 + line
        elif line < by + 2:
            slot, j = (line - 2) // part, (line - 2) % part
        else:
            slot, j = ranks + 1, line - by - 2
        beyond = jnp.where(place < 2, x3[slot, 0], x3[slot, 1])
        edge_ref[line] = pltpu.roll(beyond, (bx - 2 - 4 * j) % bx, 1)


def segment_kernel(
    sizes, own_ref, beside_ref, edge_ref, in_left_ref, out_left_ref, out_bias_ref,
    clean_any, out_any, shifted, ready, product, result, clean, sems,
):
    gz, gy, gx = sizes
    ranks = own_ref.shape[0]
    lines, planes, bx = edge_ref.shape
    by, bz = lines - 4, planes - 4
    part = by // ranks
    me = lax.axis_index("gz")
    at_y = lax.axis_index("gy")
    at_x = lax.axis_index("gx")

    def middle_of(line):
        if 2 <= line < by + 2:
            k, j = divmod(line - 2, part)
            return own_ref[k, :, j * bx : (j + 1) * bx]
        index, j = (0, line) if line < 2 else (1, line - by - 2)
        return beside_ref[index, :, j * bx : (j + 1) * bx]

    for line in range(lines):
        store_shifts(shifted, slice(line * planes, (line + 1) * planes), middle_of(line), edge_ref[line])
    in_left = in_left_ref[...]
    out_left = out_left_ref[...]
    out_bias = out_bias_ref[:, 0:1]
    shape = (16 * (bz + 2), 2 * bx)
    lane, plane = lane_of(shape), row_of(shape) // 16
    outside = ((me == 0) & (plane == 0)) | ((me == gz - 1) & (plane == bz + 1))
    outside = outside | ((at_x == 0) & (lane == 2 * bx - 1)) | ((at_x == gx - 1) & (lane == bx))
    mask = jnp.where(outside, 0.0, 1.0).astype(F32)
    spare = jnp.ones((planes, bx), F32)
    for y in range(by + 2):
        grown = jnp.maximum(mxu(in_left, window_of(shifted, y * planes, 3 * planes, spare)), 0.0) * mask
        if y == 0:
            grown = grown * jnp.where(at_y > 0, 1.0, 0.0).astype(F32)
        if y == by + 1:
            grown = grown * jnp.where(at_y < gy - 1, 1.0, 0.0).astype(F32)
        ready[y] = grown
    for z in range(bz):
        for y in range(by):
            clean[z, y : y + 1, :] = middle_of(2 + y)[2 + z : 3 + z]
    first = pltpu.make_async_copy(clean, clean_any, sems.at[0])
    first.start()
    for y in range(by + 2):
        high, low = stacked_shifts(ready[y], bz)
        double = mxu(out_left, high)
        product[y] = double[0:48] + double[48:96] + mxu(out_left[0:48], low)
        if y >= 2:
            total = product[y - 2, 0:16] + product[y - 1, 16:32] + product[y, 32:48] + out_bias
            for z in range(bz):
                result[pl.ds(z * by + y - 2, 16, stride=bz * by), :] = total[:, z * bx : (z + 1) * bx]
    second = pltpu.make_async_copy(result.at[0 : 16 * bz * by, :], out_any, sems.at[1])
    second.start()
    first.wait()
    second.wait()


def body(sizes, noisy, first_weight, first_bias, second_weight, second_bias, head_weight,
         seg_weight_in, seg_bias_in, seg_weight_out, seg_bias_out):
    gz, gy, gx = sizes
    bz, by, bx = noisy.shape
    ranks = by // 4
    part = by // ranks
    lines = part + 4
    depth = gz * bz
    args = [
        noisy.reshape(bz * by, bx),
        first_weight.transpose(2, 1, 0),
        first_bias.reshape(1, -1),
        second_weight.transpose(2, 1, 0),
        second_bias.reshape(1, -1),
        head_weight.reshape(1, -1),
        seg_weight_in,
        seg_bias_in.reshape(1, -1),
        seg_weight_out,
        seg_bias_out.reshape(1, -1),
    ]
    vmem = pl.BlockSpec(memory_space=pltpu.VMEM)
    dma = pltpu.SemaphoreType.DMA
    rest = pl.BlockSpec(memory_space=pl.ANY)

    def room(*shape):
        return pltpu.VMEM(shape, F32)

    stages = [
        room(*(a.shape if i not in (1, 6) else (a.shape[0], a.shape[2]))) for i, a in enumerate(args)
    ]
    handed = pl.pallas_call(
        functools.partial(layers_kernel, sizes, ranks, bz, by, bx),
        out_shape=[
            room(ranks, bz + 4, part * bx),
            room(2, bz + 4, 2 * bx),
            room(by + 4, bz + 4, bx),
            pltpu.VMEM((16 * (bz + 2), 30 * (bz + 4)), BF16),
            pltpu.VMEM((96, 144), BF16),
            room(16, LANES),
        ],
        in_specs=[rest] * len(args),
        out_specs=[vmem] * 6,
        scratch_shapes=stages
        + [
            dma((len(args),)),
            room(depth * by, bx),
            room(2, depth * 2, bx),
            room(3, 2, gz, by, bx),
            room(2, bz * 2, bx),
            room(by, bx),
            dma((6, max(ranks, 2))),
            dma((9, gz)),
            room(6, (depth + 2) * lines, bx),
            room(2, bz + 1, 16 * (part + 2), 2 * bx),
            room(depth + 2, 96, part * bx),
            room(depth + 16, part * bx),
            room(gz, bz + 4, part * bx),
            room(gz, bz + 4, bx),
            room(ranks + 2, 2, bz + 4, bx),
            dma((gz,)),
            dma((ranks,)),
            dma((2, gz)),
            dma((2,)),
            dma((2, gz)),
            dma((2, 2, gz)),
            dma((ranks + 2, 2)),
        ],
        compiler_params=pltpu.CompilerParams(
            collective_id=0, has_side_effects=True, vmem_limit_bytes=GRANT
        ),
        name="layers",
    )(*(pltpu.with_memory_space_constraint(a, pltpu.HBM) for a in args))
    clean, features = pl.pallas_call(
        functools.partial(segment_kernel, sizes),
        out_shape=[
            jax.ShapeDtypeStruct((bz, by, bx), F32),
            jax.ShapeDtypeStruct((16 * bz * by, bx), F32),
        ],
        in_specs=[vmem] * 6,
        out_specs=[rest] * 2,
        scratch_shapes=[
            room(6, (by + 4) * (bz + 4), bx),
            room(by + 2, 16 * (bz + 2), 2 * bx),
            room(by + 2, 48, bz * bx),
            room(17 * bz * by, bx),
            room(bz, by, bx),
            dma((2,)),
        ],
        compiler_params=pltpu.CompilerParams(vmem_limit_bytes=GRANT),
        name="segment",
    )(*handed)
    return clean, features.reshape(16, bz, by, bx)


def solution(mesh):
    sizes = (mesh.shape["gz"], mesh.shape["gy"], mesh.shape["gx"])
    in_specs = (P(("win", "gz"), "gy", "gx"), P(), P(), P(), P(), P(), P(), P(), P(), P())
    out_specs = (P(("win", "gz"), "gy", "gx"), P(None, ("win", "gz"), "gy", "gx"))
    return jax.shard_map(
        functools.partial(body, sizes), mesh=mesh, in_specs=in_specs, out_specs=out_specs, check_vma=False
    )
```

```python
import functools

import jax
import jax.numpy as jnp
from jax import lax
from jax.experimental import pallas as pl
from jax.experimental.pallas import tpu as pltpu
from jax.sharding import PartitionSpec as P

LANES = 128
GRANT = 48 << 20
F32 = jnp.float32
BF16 = jnp.bfloat16
MESH = pl.DeviceIdType.MESH


def split(value):
    high = value.astype(BF16)
    return high, (value - high.astype(F32)).astype(BF16)


def left_rows(weight):
    high, low = split(weight)
    return jnp.concatenate([high, high, low], axis=1)


def right_rows(high, low):
    return jnp.concatenate([high, low, high], axis=0)


def mxu(left, right):
    return jnp.dot(left, right, preferred_element_type=F32)


def lane_of(shape):
    return lax.broadcasted_iota(jnp.int32, shape, len(shape) - 1)


def row_of(shape):
    return lax.broadcasted_iota(jnp.int32, shape, 0)


def column(row_ref):
    count = row_ref.shape[1]
    shape = (count, count)
    spread = jnp.broadcast_to(row_ref[...], shape)
    return jnp.sum(jnp.where(row_of(shape) == lane_of(shape), spread, 0.0), axis=1, keepdims=True)


def times(count, step, carry, backward=False):
    if count <= 16:
        for i in range(count):
            carry = step(count - 1 - i if backward else i, carry)
        return carry
    return lax.fori_loop(0, count, lambda i, c: step(count - 1 - i if backward else i, c), carry)


class Step:
    def __init__(self, step, side, ok):
        self.step, self.side, self.ok = step, side, ok

    def back(self):
        return Step(-self.step, 1 - self.side, self.ok)


def steps_along(at, count):
    if count == 1:
        return []
    if count == 2:
        return [Step(1 - 2 * at, 1 - at, None)]
    return [Step(-1, 0, at > 0), Step(1, 1, at < count - 1)]


STAY = Step(0, 0, None)


def aligned(start, unit):
    return start if isinstance(start, int) else pl.multiple_of(start, unit)


def matches(left, right):
    return jnp.where(left == right, 1.0, 0.0).astype(BF16)


def tap_parts(tap):
    plane = (tap >= 9).astype(jnp.int32) + (tap >= 18).astype(jnp.int32)
    rest = tap - 9 * plane
    line = (rest >= 3).astype(jnp.int32) + (rest >= 6).astype(jnp.int32)
    return plane, line, rest - 3 * line


def banded_rows(weight, bias, count, over_planes):
    outs, taps = weight.shape
    size = count + 2
    block = 10 * size
    shape = (taps, 3 * block)
    plane, line, step = tap_parts(row_of(shape))
    slow, fast = (line, plane) if over_planes else (plane, line)
    start = size * (3 * step + slow) + fast
    col = lane_of(shape)
    high, low = split(weight)
    shape = (outs, 3 * block)
    steady = jnp.zeros(shape, F32)
    for piece in range(3):
        piece_of = bias.astype(BF16).astype(F32)
        steady = jnp.where(lane_of(shape) == 9 * size + piece, piece_of, steady)
        bias = bias - piece_of
    parts = []
    for at in range(count):
        first = matches(col, start + at) + matches(col, start + at + block)
        last = matches(col, start + at + 2 * block)
        parts.append((mxu(high, first) + mxu(low, last) + steady).astype(BF16))
    return parts


def second_rows(turned, ins):
    return left_rows(
        jnp.concatenate(
            [
                jnp.concatenate(
                    [
                        turned[ins * (9 * a + 3 * b + c) : ins * (9 * a + 3 * b + c + 1)]
                        for c in range(3)
                        for b in range(3)
                    ],
                    axis=0,
                ).T
                for a in range(3)
            ],
            axis=0,
        )
    )


def last_rows(weight):
    outs, ins, taps = weight.shape
    shape = (taps, taps * ins)
    plane, line, step = tap_parts(row_of(shape))
    place = matches(3 * (3 * line + step) + plane, lane_of(shape) // ins)
    shape = (outs * ins, taps * ins)
    keep = (row_of(shape) % ins) == (lane_of(shape) % ins)
    shape = (outs, outs * ins)
    collect = matches(row_of(shape), lane_of(shape) // ins)
    parts = []
    for part in split(weight.reshape(outs * ins, taps)):
        grown = jnp.where(keep, mxu(part, place), 0.0).astype(BF16)
        parts.append(mxu(collect, grown).astype(BF16))
    third = taps * ins // 3
    high, low = (
        jnp.concatenate([p[:, third * b : third * (b + 1)] for b in range(3)], axis=0) for p in parts
    )
    return jnp.concatenate([high, low], axis=0)


def window_of(shifted, start, count, spare):
    halves = [
        jnp.concatenate([shifted[s, pl.ds(start, count), :] for s in three] + [spare], axis=0)
        for three in (range(3), range(3, 6))
    ]
    return right_rows(*split(jnp.concatenate(halves, axis=1)))


def store_shifts(shifted, where, value, beyond):
    size = value.shape[1]
    lane = lane_of(value.shape)
    shifted[0, where, :] = pltpu.roll(jnp.where(lane == size - 1, beyond, value), 1, 1)
    shifted[1, where, :] = value
    shifted[2, where, :] = pltpu.roll(jnp.where(lane == 0, beyond, value), size - 1, 1)
    shifted[3, where, :] = pltpu.roll(jnp.where(lane == size - 2, beyond, value), 1, 1)
    shifted[4, where, :] = beyond
    shifted[5, where, :] = pltpu.roll(jnp.where(lane == 1, beyond, value), size - 1, 1)


def stacked_shifts(field, count):
    size = field.shape[1] // 2
    inner, outer = field[:, 0:size], field[:, size:]
    lane = lane_of(inner.shape)
    fields = (
        pltpu.roll(jnp.where(lane == size - 1, outer, inner), 1, 1),
        inner,
        pltpu.roll(jnp.where(lane == 0, outer, inner), size - 1, 1),
    )
    return tuple(
        jnp.concatenate(
            [jnp.concatenate([v[16 * j : 16 * j + 48] for j in range(count)], axis=1) for v in values],
            axis=0,
        )
        for values in zip(*(split(f) for f in fields))
    )


def layers_kernel(
    sizes, ranks, bz, by, bx,
    noisy_any, w1_any, b1_any, w2_any, b2_any, head_any, w3_any, b3_any, w4_any, b4_any,
    own_ref, beside_ref, edge_ref, in_left_ref, out_left_ref, out_bias_ref,
    noisy_ref, w1_ref, b1_ref, w2_ref, b2_ref, head_ref, w3_ref, b3_ref, w4_ref, b4_ref, load_sem,
    m1, my, x1, halo, rim, send1, recv1,
    shifted, ready, product, settled, fix, packed, packed_rim,
    x3, own_send, own_recv, beside_send, beside_recv, edge_send, corner_send, edge_recv,
):
    gz, gy, gx = sizes
    depth = gz * bz
    part = by // ranks
    lines = part + 4
    rows = part + 2
    me = lax.axis_index("gz")
    at_y = lax.axis_index("gy")
    at_x = lax.axis_index("gx")
    works = me < ranks
    turned_round = 1 - lax.rem(at_y, 2)
    mine = me + turned_round * (ranks - 1 - 2 * me)
    steps_y = steps_along(at_y, gy)
    steps_x = steps_along(at_x, gx)

    def both(first, second):
        return second if first is None else first if second is None else first & second

    def when(ok, action):
        if ok is None:
            action()
        else:
            pl.when(ok)(action)

    def device(z, dy, dx):
        return {
            "win": lax.axis_index("win"),
            "gz": z,
            "gy": lax.rem(at_y + dy.step + gy, gy),
            "gx": lax.rem(at_x + dx.step + gx, gx),
        }

    def peer(k):
        return lax.rem(me + k, gz)

    def rank_towards(dy):
        return (1 - dy.side) * (ranks - 1)

    def beside(dy):
        return both(mine == rank_towards(dy.back()), dy.ok)

    def home_towards(dy):
        rank = rank_towards(dy)
        return rank + (1 - turned_round) * (ranks - 1 - 2 * rank)

    loads = [
        pltpu.make_async_copy(source, target, load_sem.at[i])
        for i, (source, target) in enumerate(
            (
                (noisy_any, noisy_ref),
                (w1_any.at[:, 0, :], w1_ref),
                (w2_any, w2_ref),
                (w3_any.at[:, 0, :], w3_ref),
                (w4_any, w4_ref),
                (b1_any, b1_ref),
                (b2_any, b2_ref),
                (head_any, head_ref),
                (b3_any, b3_ref),
                (b4_any, b4_ref),
            )
        )
    ]
    loads[0].start()
    barrier = pltpu.get_barrier_semaphore()

    def greet(dy, dx):
        for k in range(gz - 1, 0 if dy is STAY and dx is STAY else -1, -1):
            pl.semaphore_signal(barrier, inc=1, device_id=device(peer(k), dy, dx), device_id_type=MESH)

    for dy in steps_y:
        @functools.partial(when, beside(dy))
        def greet_beside(dy=dy):
            for dx in [STAY] + steps_x:
                when(dx.ok, functools.partial(greet, dy, dx))

    @pl.when(works)
    def greet_along():
        for dx in [STAY] + steps_x:
            when(dx.ok, functools.partial(greet, STAY, dx))

    for load in loads[1:]:
        load.start()

    loads[0].wait()
    for index, first in ((0, 0), (1, by - 2)):
        for z in range(bz):
            halo[index, 2 * z : 2 * z + 2, :] = noisy_ref[z * by + first : z * by + first + 2, :]
    lane = lane_of((by, bx))
    corner = jnp.zeros((by, bx), F32)
    for z in range(bz):
        turned = pltpu.roll(noisy_ref[z * by : (z + 1) * by, :], 4 * z + 2, 1)
        corner = jnp.where((lane >= 4 * z) & (lane < 4 * z + 4), turned, corner)
    rim[...] = corner

    count_y = (at_y > 0).astype(jnp.int32) + (at_y < gy - 1).astype(jnp.int32)
    count_x = (at_x > 0).astype(jnp.int32) + (at_x < gx - 1).astype(jnp.int32)
    pl.semaphore_wait(
        barrier, ranks - works.astype(jnp.int32) + count_y + count_x * ranks + count_y * count_x
    )

    def rows_of(z, count):
        return pl.ds(aligned(z * count, count), count)

    def own_first(k, source):
        return pltpu.make_async_remote_copy(
            src_ref=noisy_ref,
            dst_ref=m1.at[rows_of(source, bz * by), :],
            send_sem=send1.at[0, k],
            recv_sem=recv1.at[0, source],
            device_id=device(k, STAY, STAY),
            device_id_type=MESH,
        )

    def halo_first(dy, source):
        return pltpu.make_async_remote_copy(
            src_ref=halo.at[dy.side],
            dst_ref=my.at[1 - dy.side, rows_of(source, bz * 2), :],
            send_sem=send1.at[1, dy.side],
            recv_sem=recv1.at[2 - dy.side, source],
            device_id=device(home_towards(dy), dy, STAY),
            device_id_type=MESH,
        )

    def edge_first(dx, k, source):
        return pltpu.make_async_remote_copy(
            src_ref=rim,
            dst_ref=x1.at[0, 1 - dx.side, source],
            send_sem=send1.at[2 + dx.side, k],
            recv_sem=recv1.at[4 - dx.side, source],
            device_id=device(k, STAY, dx),
            device_id_type=MESH,
        )

    def corner_first(dy, dx, source):
        return pltpu.make_async_remote_copy(
            src_ref=rim,
            dst_ref=x1.at[2 - dy.side, 1 - dx.side, source],
            send_sem=send1.at[4 + dy.side, dx.side],
            recv_sem=recv1.at[8 - 2 * dy.side - dx.side, source],
            device_id=device(home_towards(dy), dy, dx),
            device_id_type=MESH,
        )

    early = []
    for dy in steps_y:
        early.append((dy.ok, functools.partial(halo_first, dy)))
        for dx in steps_x:
            early.append((both(dy.ok, dx.ok), functools.partial(corner_first, dy, dx)))
    for k in range(ranks):
        early.append((me != k, functools.partial(own_first, k)))
        for dx in steps_x:
            early.append((dx.ok, functools.partial(edge_first, dx, k)))
    for ok, make in early:
        when(ok, lambda make=make: make(me).start())

    for load in loads[1:]:
        load.wait()
    for index, ok in ((0, at_y == 0), (1, at_y == gy - 1)):
        def no_row(index=index):
            my[index] = jnp.zeros(my.shape[1:], F32)
            x1[1 + index] = jnp.zeros(x1.shape[1:], F32)
            beside_ref[index] = jnp.zeros(beside_ref.shape[1:], F32)
            x3[ranks + index] = jnp.zeros(x3.shape[1:], F32)
        pl.when(ok)(no_row)
    for index, ok in ((0, at_x == 0), (1, at_x == gx - 1)):
        def no_side(index=index):
            for slot in range(3):
                x1[slot, index] = jnp.zeros(x1.shape[2:], F32)
            for slot in range(ranks + 2):
                x3[slot, index] = jnp.zeros(x3.shape[2:], F32)
        pl.when(ok)(no_side)
    in_left_ref[...] = jnp.concatenate(
        banded_rows(w3_ref[...], column(b3_ref), bz + 2, True), axis=0
    )
    out_left_ref[...] = last_rows(w4_ref[...])
    out_bias_ref[...] = jnp.broadcast_to(column(b4_ref), out_bias_ref.shape)

    def own_last(k, target):
        return pltpu.make_async_remote_copy(
            src_ref=packed.at[target],
            dst_ref=own_ref.at[k],
            send_sem=own_send.at[target],
            recv_sem=own_recv.at[k],
            device_id=device(target, STAY, STAY),
            device_id_type=MESH,
        )

    def halo_last(dy, target):
        start = aligned(dy.side * ((part - 2) * bx), LANES)
        return pltpu.make_async_remote_copy(
            src_ref=packed.at[target, :, pl.ds(start, 2 * bx)],
            dst_ref=beside_ref.at[1 - dy.side],
            send_sem=beside_send.at[dy.side, target],
            recv_sem=beside_recv.at[1 - dy.side],
            device_id=device(target, dy, STAY),
            device_id_type=MESH,
        )

    def edge_last(dx, k, target):
        return pltpu.make_async_remote_copy(
            src_ref=packed_rim.at[target],
            dst_ref=x3.at[k, 1 - dx.side],
            send_sem=edge_send.at[dx.side, target],
            recv_sem=edge_recv.at[k, 1 - dx.side],
            device_id=device(target, STAY, dx),
            device_id_type=MESH,
        )

    def corner_last(dy, dx, target):
        return pltpu.make_async_remote_copy(
            src_ref=packed_rim.at[target],
            dst_ref=x3.at[ranks + 1 - dy.side, 1 - dx.side],
            send_sem=corner_send.at[dy.side, dx.side, target],
            recv_sem=edge_recv.at[ranks + 1 - dy.side, 1 - dx.side],
            device_id=device(target, dy, dx),
            device_id_type=MESH,
        )

    def late(act, pack=lambda targets: None):
        def to_beside(dy, targets):
            for target in targets:
                act(halo_last(dy, target))
                for dx in steps_x:
                    when(dx.ok, lambda: act(corner_last(dy, dx, target)))

        def to_own(target):
            act(own_last(mine, target))

        def to_edge(target):
            for dx in steps_x:
                when(dx.ok, lambda: act(edge_last(dx, mine, target)))

        pack(range(ranks))
        for dy in steps_y:
            when(beside(dy), functools.partial(to_beside, dy, range(ranks)))
        for k in range(1, ranks):
            to_own(lax.rem(me + k, ranks))
        for target in range(ranks):
            to_edge(target)
        pack(range(ranks, gz))
        for target in range(ranks, gz):
            to_own(target)
            to_edge(target)
        for dy in steps_y:
            when(beside(dy), functools.partial(to_beside, dy, range(ranks, gz)))

    for ok, make in early:
        when(ok, lambda make=make: make(me).wait_send())

    @pl.when(works)
    def layers():
        gate_bias = jnp.concatenate([jnp.zeros((16, 1), F32), column(b1_ref)], axis=0)
        parts = banded_rows(w1_ref[...].T, gate_bias, rows, False)
        first_left = jnp.concatenate([p[:16] for p in parts] + [p[16:] for p in parts], axis=0)
        second_left = second_rows(w2_ref[...].reshape(-1, w2_ref.shape[2]), w2_ref.shape[1])
        second_bias = column(b2_ref)
        head = column(head_ref)
        shape = (16 * rows, 2 * bx)
        lane, row = lane_of(shape), row_of(shape)
        place_y = at_y * by + mine * part + row // 16 - 1
        outside = (place_y < 0) | (place_y >= gy * by)
        outside = outside | ((at_x == 0) & (lane == 2 * bx - 1)) | ((at_x == gx - 1) & (lane == bx))
        mask = jnp.where(outside, 0.0, 1.0).astype(F32)
        for s in range(6):
            for plane in (0, depth + 1):
                shifted[s, plane * lines : (plane + 1) * lines, :] = jnp.zeros((lines, bx), F32)
        for plane in (0, depth + 1):
            product[plane] = jnp.zeros(product.shape[1:], F32)
        fix[...] = jnp.zeros(fix.shape, F32)
        m1[rows_of(me, bz * by), :] = noisy_ref[...]

        def arrive(m):
            def await_own():
                own_first(0, m).wait_recv()
            pl.when(me != m)(await_own)
            for dx in steps_x:
                def await_edge(dx=dx):
                    edge_first(dx.back(), 0, m).wait_recv()
                when(dx.ok, await_edge)
            for dy in steps_y:
                @functools.partial(when, beside(dy))
                def await_beside(dy=dy):
                    halo_first(dy.back(), m).wait_recv()
                    for dx in steps_x:
                        def await_corner(dx=dx):
                            corner_first(dy.back(), dx.back(), m).wait_recv()
                        when(dx.ok, await_corner)

        place = lane_of((by, bx)) % 4

        def cut(full):
            value = full[0:lines]
            for k in range(1, ranks):
                value = jnp.where(mine == k, full[part * k : part * k + lines], value)
            return value

        def gather(m):
            rims = [jnp.where(place < 2, x1[slot, 0, m], x1[slot, 1, m]) for slot in range(3)]
            border = cut(jnp.concatenate([rims[1][by - 2 : by], rims[0], rims[2][0:2]], axis=0))
            below = my[0, rows_of(m, bz * 2), :]
            above = my[1, rows_of(m, bz * 2), :]
            block = m1[rows_of(m, bz * by), :]
            for z in range(bz):
                value = cut(
                    jnp.concatenate(
                        [below[2 * z : 2 * z + 2], block[z * by : (z + 1) * by], above[2 * z : 2 * z + 2]],
                        axis=0,
                    )
                )
                beyond = pltpu.roll(border, (bx - 2 - 4 * z) % bx, 1)
                where = pl.ds(aligned((m * bz + z + 1) * lines, lines), lines)
                store_shifts(shifted, where, value, beyond)

        spare = jnp.ones((lines, bx), F32)

        def gates(z, slot):
            pre = mxu(first_left, window_of(shifted, aligned(z * lines, lines), 3 * lines, spare))
            ready[0, slot] = mask * jnp.tanh(pre[0 : 16 * rows])
            ready[1, slot] = jax.nn.sigmoid(pre[16 * rows :])

        def advance(z, slot, hidden):
            hidden = hidden + ready[1, slot] * (ready[0, slot] - hidden)
            product[z + 1] = mxu(second_left, right_rows(*stacked_shifts(hidden, part)))
            return hidden

        def settle(z):
            pre = product[z, 0:32] + product[z + 1, 32:64] + product[z + 2, 64:96]
            settled[0, z] = jnp.tanh(pre[0:16])
            settled[1, z] = jax.nn.sigmoid(pre[16:32] + second_bias)

        def reach(m, first, count, hidden, start=0):
            arrive(m)
            gather(m)
            for slot in range(count):
                gates(first + slot, slot)
            for slot in range(count):
                hidden = advance(first + slot, slot, hidden)
                if slot >= start:
                    settle(first + slot - 1)
            return hidden

        def later(i, hidden):
            return reach(i + 1, (i + 1) * bz - 1, bz, hidden)

        hidden = reach(0, 0, bz - 1, jnp.zeros((16 * rows, 2 * bx), F32), 1)
        hidden = times(gz - 2, later, hidden)
        reach(gz - 1, depth - bz - 1, bz + 1, hidden)
        settle(depth - 1)

        def back(z, hidden):
            hidden = hidden + settled[1, z] * (settled[0, z] - hidden)
            fix[pl.ds(z + 2, 1), :] = jnp.sum(head * hidden, axis=0, keepdims=True)
            return hidden

        times(depth, back, jnp.zeros((16, part * bx), F32), True)
        lane = lane_of((fix.shape[0], bx))
        border = jnp.zeros((fix.shape[0], bx), F32)
        for j in range(part):
            lanes = slice(j * bx, (j + 1) * bx)
            centre = shifted[1, pl.ds(lines + j + 2, depth, stride=lines), :]
            fix[2 : 2 + depth, lanes] = fix[2 : 2 + depth, lanes] + centre
            turned = pltpu.roll(fix[:, lanes], 4 * j + 2, 1)
            border = jnp.where((lane >= 4 * j) & (lane < 4 * j + 4), turned, border)
        def pack(targets):
            for target in targets:
                packed[target] = fix[bz * target : bz * target + bz + 4, :]
                packed_rim[target] = border[bz * target : bz * target + bz + 4]

        late(lambda copy: copy.start(), pack)
        own_ref[mine] = packed[me]
        late(lambda copy: copy.wait_send())

    for k in range(ranks):
        def await_own(k=k):
            own_last(k, 0).wait_recv()
        pl.when(mine != k)(await_own)
    for dy in steps_y:
        def await_beside(dy=dy):
            halo_last(dy.back(), 0).wait_recv()
        when(dy.ok, await_beside)
    for dx in steps_x:
        def await_rims(dx=dx):
            for k in range(ranks):
                edge_last(dx.back(), k, 0).wait_recv()
        when(dx.ok, await_rims)
        for dy in steps_y:
            def await_corner(dy=dy, dx=dx):
                corner_last(dy.back(), dx.back(), 0).wait_recv()
            when(both(dy.ok, dx.ok), await_corner)
    place = lane_of((bz + 4, bx)) % 4
    for line in range(by + 4):
        if line < 2:
            slot, j = ranks, part - 2 + line
        elif line < by + 2:
            slot, j = (line - 2) // part, (line - 2) % part
        else:
            slot, j = ranks + 1, line - by - 2
        beyond = jnp.where(place < 2, x3[slot, 0], x3[slot, 1])
        edge_ref[line] = pltpu.roll(beyond, (bx - 2 - 4 * j) % bx, 1)


def segment_kernel(
    sizes, own_ref, beside_ref, edge_ref, in_left_ref, out_left_ref, out_bias_ref,
    clean_any, out_any, shifted, ready, product, result, clean, sems,
):
    gz, gy, gx = sizes
    ranks = own_ref.shape[0]
    lines, planes, bx = edge_ref.shape
    by, bz = lines - 4, planes - 4
    part = by // ranks
    me = lax.axis_index("gz")
    at_y = lax.axis_index("gy")
    at_x = lax.axis_index("gx")

    def middle_of(line):
        if 2 <= line < by + 2:
            k, j = divmod(line - 2, part)
            return own_ref[k, :, j * bx : (j + 1) * bx]
        index, j = (0, line) if line < 2 else (1, line - by - 2)
        return beside_ref[index, :, j * bx : (j + 1) * bx]

    for line in range(lines):
        store_shifts(shifted, slice(line * planes, (line + 1) * planes), middle_of(line), edge_ref[line])
    in_left = in_left_ref[...]
    out_left = out_left_ref[...]
    out_bias = out_bias_ref[:, 0:1]
    shape = (16 * (bz + 2), 2 * bx)
    lane, plane = lane_of(shape), row_of(shape) // 16
    outside = ((me == 0) & (plane == 0)) | ((me == gz - 1) & (plane == bz + 1))
    outside = outside | ((at_x == 0) & (lane == 2 * bx - 1)) | ((at_x == gx - 1) & (lane == bx))
    mask = jnp.where(outside, 0.0, 1.0).astype(F32)
    spare = jnp.ones((planes, bx), F32)
    for y in range(by + 2):
        grown = jnp.maximum(mxu(in_left, window_of(shifted, y * planes, 3 * planes, spare)), 0.0) * mask
        if y == 0:
            grown = grown * jnp.where(at_y > 0, 1.0, 0.0).astype(F32)
        if y == by + 1:
            grown = grown * jnp.where(at_y < gy - 1, 1.0, 0.0).astype(F32)
        ready[y] = grown
    for z in range(bz):
        for y in range(by):
            clean[z, y : y + 1, :] = middle_of(2 + y)[2 + z : 3 + z]
    first = pltpu.make_async_copy(clean, clean_any, sems.at[0])
    first.start()
    for y in range(by + 2):
        high, low = stacked_shifts(ready[y], bz)
        double = mxu(out_left, high)
        product[y] = double[0:48] + double[48:96] + mxu(out_left[0:48], low)
        if y >= 2:
            total = product[y - 2, 0:16] + product[y - 1, 16:32] + product[y, 32:48] + out_bias
            for z in range(bz):
                result[pl.ds(z * by + y - 2, 16, stride=bz * by), :] = total[:, z * bx : (z + 1) * bx]
    second = pltpu.make_async_copy(result.at[0 : 16 * bz * by, :], out_any, sems.at[1])
    second.start()
    first.wait()
    second.wait()


def body(sizes, noisy, first_weight, first_bias, second_weight, second_bias, head_weight,
         seg_weight_in, seg_bias_in, seg_weight_out, seg_bias_out):
    gz, gy, gx = sizes
    bz, by, bx = noisy.shape
    ranks = by // 4
    part = by // ranks
    lines = part + 4
    depth = gz * bz
    args = [
        noisy.reshape(bz * by, bx),
        first_weight.transpose(2, 1, 0),
        first_bias.reshape(1, -1),
        second_weight.transpose(2, 1, 0),
        second_bias.reshape(1, -1),
        head_weight.reshape(1, -1),
        seg_weight_in,
        seg_bias_in.reshape(1, -1),
        seg_weight_out,
        seg_bias_out.reshape(1, -1),
    ]
    vmem = pl.BlockSpec(memory_space=pltpu.VMEM)
    dma = pltpu.SemaphoreType.DMA
    rest = pl.BlockSpec(memory_space=pl.ANY)

    def room(*shape):
        return pltpu.VMEM(shape, F32)

    stages = [
        room(*(a.shape if i not in (1, 6) else (a.shape[0], a.shape[2]))) for i, a in enumerate(args)
    ]
    handed = pl.pallas_call(
        functools.partial(layers_kernel, sizes, ranks, bz, by, bx),
        out_shape=[
            room(ranks, bz + 4, part * bx),
            room(2, bz + 4, 2 * bx),
            room(by + 4, bz + 4, bx),
            pltpu.VMEM((16 * (bz + 2), 30 * (bz + 4)), BF16),
            pltpu.VMEM((96, 144), BF16),
            room(16, LANES),
        ],
        in_specs=[rest] * len(args),
        out_specs=[vmem] * 6,
        scratch_shapes=stages
        + [
            dma((len(args),)),
            room(depth * by, bx),
            room(2, depth * 2, bx),
            room(3, 2, gz, by, bx),
            room(2, bz * 2, bx),
            room(by, bx),
            dma((6, max(ranks, 2))),
            dma((9, gz)),
            room(6, (depth + 2) * lines, bx),
            room(2, bz + 1, 16 * (part + 2), 2 * bx),
            room(depth + 2, 96, part * bx),
            room(2, depth, 16, part * bx),
            room(depth + 16, part * bx),
            room(gz, bz + 4, part * bx),
            room(gz, bz + 4, bx),
            room(ranks + 2, 2, bz + 4, bx),
            dma((gz,)),
            dma((ranks,)),
            dma((2, gz)),
            dma((2,)),
            dma((2, gz)),
            dma((2, 2, gz)),
            dma((ranks + 2, 2)),
        ],
        compiler_params=pltpu.CompilerParams(
            collective_id=0, has_side_effects=True, vmem_limit_bytes=GRANT
        ),
        name="layers",
    )(*(pltpu.with_memory_space_constraint(a, pltpu.HBM) for a in args))
    clean, features = pl.pallas_call(
        functools.partial(segment_kernel, sizes),
        out_shape=[
            jax.ShapeDtypeStruct((bz, by, bx), F32),
            jax.ShapeDtypeStruct((16 * bz * by, bx), F32),
        ],
        in_specs=[vmem] * 6,
        out_specs=[rest] * 2,
        scratch_shapes=[
            room(6, (by + 4) * (bz + 4), bx),
            room(by + 2, 16 * (bz + 2), 2 * bx),
            room(by + 2, 48, bz * bx),
            room(17 * bz * by, bx),
            room(bz, by, bx),
            dma((2,)),
        ],
        compiler_params=pltpu.CompilerParams(vmem_limit_bytes=GRANT),
        name="segment",
    )(*handed)
    return clean, features.reshape(16, bz, by, bx)


def solution(mesh):
    sizes = (mesh.shape["gz"], mesh.shape["gy"], mesh.shape["gx"])
    in_specs = (P(("win", "gz"), "gy", "gx"), P(), P(), P(), P(), P(), P(), P(), P(), P())
    out_specs = (P(("win", "gz"), "gy", "gx"), P(None, ("win", "gz"), "gy", "gx"))
    return jax.shard_map(
        functools.partial(body, sizes), mesh=mesh, in_specs=in_specs, out_specs=out_specs, check_vma=False
    )
```

```python
import functools

import jax
import jax.numpy as jnp
from jax import lax
from jax.experimental import pallas as pl
from jax.experimental.pallas import tpu as pltpu
from jax.sharding import PartitionSpec as P

LANES = 128
GRANT = 48 << 20
F32 = jnp.float32
BF16 = jnp.bfloat16
MESH = pl.DeviceIdType.MESH


def split(value):
    high = value.astype(BF16)
    return high, (value - high.astype(F32)).astype(BF16)


def left_rows(weight):
    high, low = split(weight)
    return jnp.concatenate([high, high, low], axis=1)


def right_rows(high, low):
    return jnp.concatenate([high, low, high], axis=0)


def mxu(left, right):
    return jnp.dot(left, right, preferred_element_type=F32)


def lane_of(shape):
    return lax.broadcasted_iota(jnp.int32, shape, len(shape) - 1)


def row_of(shape):
    return lax.broadcasted_iota(jnp.int32, shape, 0)


def column(row_ref):
    count = row_ref.shape[1]
    shape = (count, count)
    spread = jnp.broadcast_to(row_ref[...], shape)
    return jnp.sum(jnp.where(row_of(shape) == lane_of(shape), spread, 0.0), axis=1, keepdims=True)


def times(count, step, carry, backward=False):
    if count <= 16:
        for i in range(count):
            carry = step(count - 1 - i if backward else i, carry)
        return carry
    return lax.fori_loop(0, count, lambda i, c: step(count - 1 - i if backward else i, c), carry)


class Step:
    def __init__(self, step, side, ok):
        self.step, self.side, self.ok = step, side, ok

    def back(self):
        return Step(-self.step, 1 - self.side, self.ok)


def steps_along(at, count):
    if count == 1:
        return []
    if count == 2:
        return [Step(1 - 2 * at, 1 - at, None)]
    return [Step(-1, 0, at > 0), Step(1, 1, at < count - 1)]


STAY = Step(0, 0, None)


def aligned(start, unit):
    return start if isinstance(start, int) else pl.multiple_of(start, unit)


def matches(left, right):
    return jnp.where(left == right, 1.0, 0.0).astype(BF16)


def tap_parts(tap):
    plane = (tap >= 9).astype(jnp.int32) + (tap >= 18).astype(jnp.int32)
    rest = tap - 9 * plane
    line = (rest >= 3).astype(jnp.int32) + (rest >= 6).astype(jnp.int32)
    return plane, line, rest - 3 * line


def banded_rows(weight, bias, count, over_planes):
    outs, taps = weight.shape
    size = count + 2
    block = 10 * size
    shape = (taps, 3 * block)
    plane, line, step = tap_parts(row_of(shape))
    slow, fast = (line, plane) if over_planes else (plane, line)
    start = size * (3 * step + slow) + fast
    col = lane_of(shape)
    high, low = split(weight)
    shape = (outs, 3 * block)
    steady = jnp.zeros(shape, F32)
    for piece in range(3):
        piece_of = bias.astype(BF16).astype(F32)
        steady = jnp.where(lane_of(shape) == 9 * size + piece, piece_of, steady)
        bias = bias - piece_of
    parts = []
    for at in range(count):
        first = matches(col, start + at) + matches(col, start + at + block)
        last = matches(col, start + at + 2 * block)
        parts.append((mxu(high, first) + mxu(low, last) + steady).astype(BF16))
    return parts


def second_rows(turned, ins):
    return left_rows(
        jnp.concatenate(
            [
                jnp.concatenate(
                    [
                        turned[ins * (9 * a + 3 * b + c) : ins * (9 * a + 3 * b + c + 1)]
                        for c in range(3)
                        for b in range(3)
                    ],
                    axis=0,
                ).T
                for a in range(3)
            ],
            axis=0,
        )
    )


def last_rows(weight):
    outs, ins, taps = weight.shape
    shape = (taps, taps * ins)
    plane, line, step = tap_parts(row_of(shape))
    place = matches(3 * (3 * line + step) + plane, lane_of(shape) // ins)
    shape = (outs * ins, taps * ins)
    keep = (row_of(shape) % ins) == (lane_of(shape) % ins)
    shape = (outs, outs * ins)
    collect = matches(row_of(shape), lane_of(shape) // ins)
    parts = []
    for part in split(weight.reshape(outs * ins, taps)):
        grown = jnp.where(keep, mxu(part, place), 0.0).astype(BF16)
        parts.append(mxu(collect, grown).astype(BF16))
    third = taps * ins // 3
    high, low = (
        jnp.concatenate([p[:, third * b : third * (b + 1)] for b in range(3)], axis=0) for p in parts
    )
    return jnp.concatenate([high, low], axis=0)


def window_of(shifted, start, count, spare):
    halves = [
        jnp.concatenate([shifted[s, pl.ds(start, count), :] for s in three] + [spare], axis=0)
        for three in (range(3), range(3, 6))
    ]
    return right_rows(*split(jnp.concatenate(halves, axis=1)))


def store_shifts(shifted, where, value, beyond):
    size = value.shape[1]
    lane = lane_of(value.shape)
    shifted[0, where, :] = pltpu.roll(jnp.where(lane == size - 1, beyond, value), 1, 1)
    shifted[1, where, :] = value
    shifted[2, where, :] = pltpu.roll(jnp.where(lane == 0, beyond, value), size - 1, 1)
    shifted[3, where, :] = pltpu.roll(jnp.where(lane == size - 2, beyond, value), 1, 1)
    shifted[4, where, :] = beyond
    shifted[5, where, :] = pltpu.roll(jnp.where(lane == 1, beyond, value), size - 1, 1)


def stacked_shifts(field, count):
    size = field.shape[1] // 2
    inner, outer = field[:, 0:size], field[:, size:]
    lane = lane_of(inner.shape)
    fields = (
        pltpu.roll(jnp.where(lane == size - 1, outer, inner), 1, 1),
        inner,
        pltpu.roll(jnp.where(lane == 0, outer, inner), size - 1, 1),
    )
    return tuple(
        jnp.concatenate(
            [jnp.concatenate([v[16 * j : 16 * j + 48] for j in range(count)], axis=1) for v in values],
            axis=0,
        )
        for values in zip(*(split(f) for f in fields))
    )


def layers_kernel(
    sizes, ranks, bz, by, bx,
    noisy_any, w1_any, b1_any, w2_any, b2_any, head_any, w3_any, b3_any, w4_any, b4_any,
    own_ref, beside_ref, edge_ref, in_left_ref, out_left_ref, out_bias_ref,
    noisy_ref, w1_ref, b1_ref, w2_ref, b2_ref, head_ref, w3_ref, b3_ref, w4_ref, b4_ref, load_sem,
    m1, my, x1, halo, rim, send1, recv1,
    shifted, ready, product, settled, fix, packed, packed_rim,
    x3, own_send, own_recv, beside_send, beside_recv, edge_send, corner_send, edge_recv,
):
    gz, gy, gx = sizes
    depth = gz * bz
    part = by // ranks
    lines = part + 4
    rows = part + 2
    me = lax.axis_index("gz")
    at_y = lax.axis_index("gy")
    at_x = lax.axis_index("gx")
    works = me < ranks
    turned_round = 1 - lax.rem(at_y, 2)
    mine = me + turned_round * (ranks - 1 - 2 * me)
    steps_y = steps_along(at_y, gy)
    steps_x = steps_along(at_x, gx)

    def both(first, second):
        return second if first is None else first if second is None else first & second

    def when(ok, action):
        if ok is None:
            action()
        else:
            pl.when(ok)(action)

    def device(z, dy, dx):
        return {
            "win": lax.axis_index("win"),
            "gz": z,
            "gy": lax.rem(at_y + dy.step + gy, gy),
            "gx": lax.rem(at_x + dx.step + gx, gx),
        }

    def peer(k):
        return lax.rem(me + k, gz)

    def rank_towards(dy):
        return (1 - dy.side) * (ranks - 1)

    def beside(dy):
        return both(mine == rank_towards(dy.back()), dy.ok)

    def home_towards(dy):
        rank = rank_towards(dy)
        return rank + (1 - turned_round) * (ranks - 1 - 2 * rank)

    loads = [
        pltpu.make_async_copy(source, target, load_sem.at[i])
        for i, (source, target) in enumerate(
            (
                (noisy_any, noisy_ref),
                (w1_any.at[:, 0, :], w1_ref),
                (w2_any, w2_ref),
                (w3_any.at[:, 0, :], w3_ref),
                (w4_any, w4_ref),
                (b1_any, b1_ref),
                (b2_any, b2_ref),
                (head_any, head_ref),
                (b3_any, b3_ref),
                (b4_any, b4_ref),
            )
        )
    ]
    loads[0].start()
    barrier = pltpu.get_barrier_semaphore()

    def greet(dy, dx):
        for k in range(gz - 1, 0 if dy is STAY and dx is STAY else -1, -1):
            pl.semaphore_signal(barrier, inc=1, device_id=device(peer(k), dy, dx), device_id_type=MESH)

    for dy in steps_y:
        @functools.partial(when, beside(dy))
        def greet_beside(dy=dy):
            for dx in [STAY] + steps_x:
                when(dx.ok, functools.partial(greet, dy, dx))

    @pl.when(works)
    def greet_along():
        for dx in [STAY] + steps_x:
            when(dx.ok, functools.partial(greet, STAY, dx))

    for load in loads[1:]:
        load.start()

    loads[0].wait()
    for index, first in ((0, 0), (1, by - 2)):
        for z in range(bz):
            halo[index, 2 * z : 2 * z + 2, :] = noisy_ref[z * by + first : z * by + first + 2, :]
    lane = lane_of((by, bx))
    corner = jnp.zeros((by, bx), F32)
    for z in range(bz):
        turned = pltpu.roll(noisy_ref[z * by : (z + 1) * by, :], 4 * z + 2, 1)
        corner = jnp.where((lane >= 4 * z) & (lane < 4 * z + 4), turned, corner)
    rim[...] = corner

    count_y = (at_y > 0).astype(jnp.int32) + (at_y < gy - 1).astype(jnp.int32)
    count_x = (at_x > 0).astype(jnp.int32) + (at_x < gx - 1).astype(jnp.int32)
    pl.semaphore_wait(
        barrier, ranks - works.astype(jnp.int32) + count_y + count_x * ranks + count_y * count_x
    )

    def rows_of(z, count):
        return pl.ds(aligned(z * count, count), count)

    def own_first(k, source):
        return pltpu.make_async_remote_copy(
            src_ref=noisy_ref,
            dst_ref=m1.at[rows_of(source, bz * by), :],
            send_sem=send1.at[0, k],
            recv_sem=recv1.at[0, source],
            device_id=device(k, STAY, STAY),
            device_id_type=MESH,
        )

    def halo_first(dy, source):
        return pltpu.make_async_remote_copy(
            src_ref=halo.at[dy.side],
            dst_ref=my.at[1 - dy.side, rows_of(source, bz * 2), :],
            send_sem=send1.at[1, dy.side],
            recv_sem=recv1.at[2 - dy.side, source],
            device_id=device(home_towards(dy), dy, STAY),
            device_id_type=MESH,
        )

    def edge_first(dx, k, source):
        return pltpu.make_async_remote_copy(
            src_ref=rim,
            dst_ref=x1.at[0, 1 - dx.side, source],
            send_sem=send1.at[2 + dx.side, k],
            recv_sem=recv1.at[4 - dx.side, source],
            device_id=device(k, STAY, dx),
            device_id_type=MESH,
        )

    def corner_first(dy, dx, source):
        return pltpu.make_async_remote_copy(
            src_ref=rim,
            dst_ref=x1.at[2 - dy.side, 1 - dx.side, source],
            send_sem=send1.at[4 + dy.side, dx.side],
            recv_sem=recv1.at[8 - 2 * dy.side - dx.side, source],
            device_id=device(home_towards(dy), dy, dx),
            device_id_type=MESH,
        )

    early = []
    for dy in steps_y:
        early.append((dy.ok, functools.partial(halo_first, dy)))
        for dx in steps_x:
            early.append((both(dy.ok, dx.ok), functools.partial(corner_first, dy, dx)))
    for k in range(ranks):
        early.append((me != k, functools.partial(own_first, k)))
        for dx in steps_x:
            early.append((dx.ok, functools.partial(edge_first, dx, k)))
    for ok, make in early:
        when(ok, lambda make=make: make(me).start())

    for load in loads[1:]:
        load.wait()
    for index, ok in ((0, at_y == 0), (1, at_y == gy - 1)):
        def no_row(index=index):
            my[index] = jnp.zeros(my.shape[1:], F32)
            x1[1 + index] = jnp.zeros(x1.shape[1:], F32)
            beside_ref[index] = jnp.zeros(beside_ref.shape[1:], F32)
            x3[ranks + index] = jnp.zeros(x3.shape[1:], F32)
        pl.when(ok)(no_row)
    for index, ok in ((0, at_x == 0), (1, at_x == gx - 1)):
        def no_side(index=index):
            for slot in range(3):
                x1[slot, index] = jnp.zeros(x1.shape[2:], F32)
            for slot in range(ranks + 2):
                x3[slot, index] = jnp.zeros(x3.shape[2:], F32)
        pl.when(ok)(no_side)
    in_left_ref[...] = jnp.concatenate(
        banded_rows(w3_ref[...], column(b3_ref), bz + 2, True), axis=0
    )
    out_left_ref[...] = last_rows(w4_ref[...])
    out_bias_ref[...] = jnp.broadcast_to(column(b4_ref), out_bias_ref.shape)

    def own_last(k, target):
        return pltpu.make_async_remote_copy(
            src_ref=packed.at[target],
            dst_ref=own_ref.at[k],
            send_sem=own_send.at[target],
            recv_sem=own_recv.at[k],
            device_id=device(target, STAY, STAY),
            device_id_type=MESH,
        )

    def halo_last(dy, target):
        start = aligned(dy.side * ((part - 2) * bx), LANES)
        return pltpu.make_async_remote_copy(
            src_ref=packed.at[target, :, pl.ds(start, 2 * bx)],
            dst_ref=beside_ref.at[1 - dy.side],
            send_sem=beside_send.at[dy.side, target],
            recv_sem=beside_recv.at[1 - dy.side],
            device_id=device(target, dy, STAY),
            device_id_type=MESH,
        )

    def edge_last(dx, k, target):
        return pltpu.make_async_remote_copy(
            src_ref=packed_rim.at[target],
            dst_ref=x3.at[k, 1 - dx.side],
            send_sem=edge_send.at[dx.side, target],
            recv_sem=edge_recv.at[k, 1 - dx.side],
            device_id=device(target, STAY, dx),
            device_id_type=MESH,
        )

    def corner_last(dy, dx, target):
        return pltpu.make_async_remote_copy(
            src_ref=packed_rim.at[target],
            dst_ref=x3.at[ranks + 1 - dy.side, 1 - dx.side],
            send_sem=corner_send.at[dy.side, dx.side, target],
            recv_sem=edge_recv.at[ranks + 1 - dy.side, 1 - dx.side],
            device_id=device(target, dy, dx),
            device_id_type=MESH,
        )

    def late(act, pack=lambda targets: None):
        def to_beside(dy, targets):
            for target in targets:
                act(halo_last(dy, target))
                for dx in steps_x:
                    when(dx.ok, lambda: act(corner_last(dy, dx, target)))

        def to_own(target):
            act(own_last(mine, target))

        def to_edge(target):
            for dx in steps_x:
                when(dx.ok, lambda: act(edge_last(dx, mine, target)))

        pack(range(ranks))
        for dy in steps_y:
            when(beside(dy), functools.partial(to_beside, dy, range(ranks)))
        for k in range(1, ranks):
            to_own(lax.rem(me + k, ranks))
        for target in range(ranks):
            to_edge(target)
        pack(range(ranks, gz))
        for target in range(ranks, gz):
            to_own(target)
            to_edge(target)
        for dy in steps_y:
            when(beside(dy), functools.partial(to_beside, dy, range(ranks, gz)))

    for ok, make in early:
        when(ok, lambda make=make: make(me).wait_send())

    @pl.when(works)
    def layers():
        gate_bias = jnp.concatenate([jnp.zeros((16, 1), F32), column(b1_ref)], axis=0)
        parts = banded_rows(w1_ref[...].T, gate_bias, rows, False)
        first_left = jnp.concatenate([p[:16] for p in parts] + [p[16:] for p in parts], axis=0)
        second_left = second_rows(w2_ref[...].reshape(-1, w2_ref.shape[2]), w2_ref.shape[1])
        second_bias = column(b2_ref)
        head = column(head_ref)
        shape = (16 * rows, 2 * bx)
        lane, row = lane_of(shape), row_of(shape)
        place_y = at_y * by + mine * part + row // 16 - 1
        outside = (place_y < 0) | (place_y >= gy * by)
        outside = outside | ((at_x == 0) & (lane == 2 * bx - 1)) | ((at_x == gx - 1) & (lane == bx))
        mask = jnp.where(outside, 0.0, 1.0).astype(F32)
        for s in range(6):
            for plane in (0, depth + 1):
                shifted[s, plane * lines : (plane + 1) * lines, :] = jnp.zeros((lines, bx), F32)
        for plane in (0, depth + 1):
            product[plane] = jnp.zeros(product.shape[1:], F32)
        fix[...] = jnp.zeros(fix.shape, F32)
        m1[rows_of(me, bz * by), :] = noisy_ref[...]

        def arrive(m):
            def await_own():
                own_first(0, m).wait_recv()
            pl.when(me != m)(await_own)
            for dx in steps_x:
                def await_edge(dx=dx):
                    edge_first(dx.back(), 0, m).wait_recv()
                when(dx.ok, await_edge)
            for dy in steps_y:
                @functools.partial(when, beside(dy))
                def await_beside(dy=dy):
                    halo_first(dy.back(), m).wait_recv()
                    for dx in steps_x:
                        def await_corner(dx=dx):
                            corner_first(dy.back(), dx.back(), m).wait_recv()
                        when(dx.ok, await_corner)

        place = lane_of((by, bx)) % 4

        def cut(full):
            value = full[0:lines]
            for k in range(1, ranks):
                value = jnp.where(mine == k, full[part * k : part * k + lines], value)
            return value

        def gather(m):
            rims = [jnp.where(place < 2, x1[slot, 0, m], x1[slot, 1, m]) for slot in range(3)]
            border = cut(jnp.concatenate([rims[1][by - 2 : by], rims[0], rims[2][0:2]], axis=0))
            below = my[0, rows_of(m, bz * 2), :]
            above = my[1, rows_of(m, bz * 2), :]
            block = m1[rows_of(m, bz * by), :]
            for z in range(bz):
                value = cut(
                    jnp.concatenate(
                        [below[2 * z : 2 * z + 2], block[z * by : (z + 1) * by], above[2 * z : 2 * z + 2]],
                        axis=0,
                    )
                )
                beyond = pltpu.roll(border, (bx - 2 - 4 * z) % bx, 1)
                where = pl.ds(aligned((m * bz + z + 1) * lines, lines), lines)
                store_shifts(shifted, where, value, beyond)

        spare = jnp.ones((lines, bx), F32)

        def gates(z, slot):
            pre = mxu(first_left, window_of(shifted, aligned(z * lines, lines), 3 * lines, spare))
            ready[0, slot] = mask * jnp.tanh(pre[0 : 16 * rows])
            ready[1, slot] = jax.nn.sigmoid(pre[16 * rows :])

        def advance(z, slot, hidden):
            hidden = hidden + ready[1, slot] * (ready[0, slot] - hidden)
            product[z + 1] = mxu(second_left, right_rows(*stacked_shifts(hidden, part)))
            return hidden

        def settle(z):
            pre = product[z, 0:32] + product[z + 1, 32:64] + product[z + 2, 64:96]
            settled[0, z] = jnp.tanh(pre[0:16])
            settled[1, z] = jax.nn.sigmoid(pre[16:32] + second_bias)

        def reach(m, first, count, hidden, start=0):
            arrive(m)
            gather(m)
            for slot in range(count):
                gates(first + slot, slot)
            for slot in range(count):
                hidden = advance(first + slot, slot, hidden)
                if slot >= start:
                    settle(first + slot - 1)
            return hidden

        def later(i, hidden):
            return reach(i + 1, (i + 1) * bz - 1, bz, hidden)

        hidden = reach(0, 0, bz - 1, jnp.zeros((16 * rows, 2 * bx), F32), 1)
        hidden = times(gz - 2, later, hidden)
        reach(gz - 1, depth - bz - 1, bz + 1, hidden)
        settle(depth - 1)

        def back(z, hidden):
            hidden = hidden + settled[1, z] * (settled[0, z] - hidden)
            fix[pl.ds(z + 2, 1), :] = jnp.sum(head * hidden, axis=0, keepdims=True)
            return hidden

        times(depth, back, jnp.zeros((16, part * bx), F32), True)
        lane = lane_of((fix.shape[0], bx))
        border = jnp.zeros((fix.shape[0], bx), F32)
        for j in range(part):
            lanes = slice(j * bx, (j + 1) * bx)
            centre = shifted[1, pl.ds(lines + j + 2, depth, stride=lines), :]
            fix[2 : 2 + depth, lanes] = fix[2 : 2 + depth, lanes] + centre
            turned = pltpu.roll(fix[:, lanes], 4 * j + 2, 1)
            border = jnp.where((lane >= 4 * j) & (lane < 4 * j + 4), turned, border)
        def pack(targets):
            for target in targets:
                packed[target] = fix[bz * target : bz * target + bz + 4, :]
                packed_rim[target] = border[bz * target : bz * target + bz + 4]

        late(lambda copy: copy.start(), pack)
        own_ref[mine] = packed[me]
        late(lambda copy: copy.wait_send())

    for k in range(ranks):
        def await_own(k=k):
            own_last(k, 0).wait_recv()
        pl.when(mine != k)(await_own)
    for dy in steps_y:
        def await_beside(dy=dy):
            halo_last(dy.back(), 0).wait_recv()
        when(dy.ok, await_beside)
    for dx in steps_x:
        def await_rims(dx=dx):
            for k in range(ranks):
                edge_last(dx.back(), k, 0).wait_recv()
        when(dx.ok, await_rims)
        for dy in steps_y:
            def await_corner(dy=dy, dx=dx):
                corner_last(dy.back(), dx.back(), 0).wait_recv()
            when(both(dy.ok, dx.ok), await_corner)
    place = lane_of((bz + 4, bx)) % 4
    for line in range(by + 4):
        if line < 2:
            slot, j = ranks, part - 2 + line
        elif line < by + 2:
            slot, j = (line - 2) // part, (line - 2) % part
        else:
            slot, j = ranks + 1, line - by - 2
        beyond = jnp.where(place < 2, x3[slot, 0], x3[slot, 1])
        edge_ref[line] = pltpu.roll(beyond, (bx - 2 - 4 * j) % bx, 1)


def segment_kernel(
    sizes, own_ref, beside_ref, edge_ref, in_left_ref, out_left_ref, out_bias_ref,
    clean_any, out_any, shifted, ready, product, result, clean, sems,
):
    gz, gy, gx = sizes
    ranks = own_ref.shape[0]
    lines, planes, bx = edge_ref.shape
    by, bz = lines - 4, planes - 4
    part = by // ranks
    me = lax.axis_index("gz")
    at_y = lax.axis_index("gy")
    at_x = lax.axis_index("gx")

    def middle_of(line):
        if 2 <= line < by + 2:
            k, j = divmod(line - 2, part)
            return own_ref[k, :, j * bx : (j + 1) * bx]
        index, j = (0, line) if line < 2 else (1, line - by - 2)
        return beside_ref[index, :, j * bx : (j + 1) * bx]

    for line in range(lines):
        store_shifts(shifted, slice(line * planes, (line + 1) * planes), middle_of(line), edge_ref[line])
    in_left = in_left_ref[...]
    out_left = out_left_ref[...]
    out_bias = out_bias_ref[:, 0:1]
    shape = (16 * (bz + 2), 2 * bx)
    lane, plane = lane_of(shape), row_of(shape) // 16
    outside = ((me == 0) & (plane == 0)) | ((me == gz - 1) & (plane == bz + 1))
    outside = outside | ((at_x == 0) & (lane == 2 * bx - 1)) | ((at_x == gx - 1) & (lane == bx))
    mask = jnp.where(outside, 0.0, 1.0).astype(F32)
    spare = jnp.ones((planes, bx), F32)
    for y in range(by + 2):
        grown = jnp.maximum(mxu(in_left, window_of(shifted, y * planes, 3 * planes, spare)), 0.0) * mask
        if y == 0:
            grown = grown * jnp.where(at_y > 0, 1.0, 0.0).astype(F32)
        if y == by + 1:
            grown = grown * jnp.where(at_y < gy - 1, 1.0, 0.0).astype(F32)
        ready[y] = grown
    for z in range(bz):
        for y in range(by):
            clean[z, y : y + 1, :] = middle_of(2 + y)[2 + z : 3 + z]
    first = pltpu.make_async_copy(clean, clean_any, sems.at[0])
    first.start()
    totals = []
    for y in range(by + 2):
        high, low = stacked_shifts(ready[y], bz)
        double = mxu(out_left, high)
        product[y] = double[0:48] + double[48:96] + mxu(out_left[0:48], low)
        if y >= 2:
            totals.append(product[y - 2, 0:16] + product[y - 1, 16:32] + product[y, 32:48] + out_bias)
    for z in range(bz):
        stack = jnp.stack([total[:, z * bx : (z + 1) * bx] for total in totals], axis=0)
        turned = jnp.transpose(stack, (1, 0, 2))
        for o in range(16):
            row = (o * bz + z) * by
            result[row : row + by, :] = turned[o]
    second = pltpu.make_async_copy(result, out_any, sems.at[1])
    second.start()
    first.wait()
    second.wait()


def body(sizes, noisy, first_weight, first_bias, second_weight, second_bias, head_weight,
         seg_weight_in, seg_bias_in, seg_weight_out, seg_bias_out):
    gz, gy, gx = sizes
    bz, by, bx = noisy.shape
    ranks = by // 4
    part = by // ranks
    lines = part + 4
    depth = gz * bz
    args = [
        noisy.reshape(bz * by, bx),
        first_weight.transpose(2, 1, 0),
        first_bias.reshape(1, -1),
        second_weight.transpose(2, 1, 0),
        second_bias.reshape(1, -1),
        head_weight.reshape(1, -1),
        seg_weight_in,
        seg_bias_in.reshape(1, -1),
        seg_weight_out,
        seg_bias_out.reshape(1, -1),
    ]
    vmem = pl.BlockSpec(memory_space=pltpu.VMEM)
    dma = pltpu.SemaphoreType.DMA
    rest = pl.BlockSpec(memory_space=pl.ANY)

    def room(*shape):
        return pltpu.VMEM(shape, F32)

    stages = [
        room(*(a.shape if i not in (1, 6) else (a.shape[0], a.shape[2]))) for i, a in enumerate(args)
    ]
    handed = pl.pallas_call(
        functools.partial(layers_kernel, sizes, ranks, bz, by, bx),
        out_shape=[
            room(ranks, bz + 4, part * bx),
            room(2, bz + 4, 2 * bx),
            room(by + 4, bz + 4, bx),
            pltpu.VMEM((16 * (bz + 2), 30 * (bz + 4)), BF16),
            pltpu.VMEM((96, 144), BF16),
            room(16, LANES),
        ],
        in_specs=[rest] * len(args),
        out_specs=[vmem] * 6,
        scratch_shapes=stages
        + [
            dma((len(args),)),
            room(depth * by, bx),
            room(2, depth * 2, bx),
            room(3, 2, gz, by, bx),
            room(2, bz * 2, bx),
            room(by, bx),
            dma((6, max(ranks, 2))),
            dma((9, gz)),
            room(6, (depth + 2) * lines, bx),
            room(2, bz + 1, 16 * (part + 2), 2 * bx),
            room(depth + 2, 96, part * bx),
            room(2, depth, 16, part * bx),
            room(depth + 16, part * bx),
            room(gz, bz + 4, part * bx),
            room(gz, bz + 4, bx),
            room(ranks + 2, 2, bz + 4, bx),
            dma((gz,)),
            dma((ranks,)),
            dma((2, gz)),
            dma((2,)),
            dma((2, gz)),
            dma((2, 2, gz)),
            dma((ranks + 2, 2)),
        ],
        compiler_params=pltpu.CompilerParams(
            collective_id=0, has_side_effects=True, vmem_limit_bytes=GRANT
        ),
        name="layers",
    )(*(pltpu.with_memory_space_constraint(a, pltpu.HBM) for a in args))
    clean, features = pl.pallas_call(
        functools.partial(segment_kernel, sizes),
        out_shape=[
            jax.ShapeDtypeStruct((bz, by, bx), F32),
            jax.ShapeDtypeStruct((16 * bz * by, bx), F32),
        ],
        in_specs=[vmem] * 6,
        out_specs=[rest] * 2,
        scratch_shapes=[
            room(6, (by + 4) * (bz + 4), bx),
            room(by + 2, 16 * (bz + 2), 2 * bx),
            room(by + 2, 48, bz * bx),
            room(16 * bz * by, bx),
            room(bz, by, bx),
            dma((2,)),
        ],
        compiler_params=pltpu.CompilerParams(vmem_limit_bytes=GRANT),
        name="segment",
    )(*handed)
    return clean, features.reshape(16, bz, by, bx)


def solution(mesh):
    sizes = (mesh.shape["gz"], mesh.shape["gy"], mesh.shape["gx"])
    in_specs = (P(("win", "gz"), "gy", "gx"), P(), P(), P(), P(), P(), P(), P(), P(), P())
    out_specs = (P(("win", "gz"), "gy", "gx"), P(None, ("win", "gz"), "gy", "gx"))
    return jax.shard_map(
        functools.partial(body, sizes), mesh=mesh, in_specs=in_specs, out_specs=out_specs, check_vma=False
    )
```

```python
import functools

import jax
import jax.numpy as jnp
from jax import lax
from jax.experimental import pallas as pl
from jax.experimental.pallas import tpu as pltpu
from jax.sharding import PartitionSpec as P

LANES = 128
GRANT = 48 << 20
F32 = jnp.float32
BF16 = jnp.bfloat16
MESH = pl.DeviceIdType.MESH


def split(value):
    high = value.astype(BF16)
    return high, (value - high.astype(F32)).astype(BF16)


def left_rows(weight):
    high, low = split(weight)
    return jnp.concatenate([high, high, low], axis=1)


def right_rows(high, low):
    return jnp.concatenate([high, low, high], axis=0)


def mxu(left, right):
    return jnp.dot(left, right, preferred_element_type=F32)


def lane_of(shape):
    return lax.broadcasted_iota(jnp.int32, shape, len(shape) - 1)


def row_of(shape):
    return lax.broadcasted_iota(jnp.int32, shape, 0)


def column(row_ref):
    count = row_ref.shape[1]
    shape = (count, count)
    spread = jnp.broadcast_to(row_ref[...], shape)
    return jnp.sum(jnp.where(row_of(shape) == lane_of(shape), spread, 0.0), axis=1, keepdims=True)


def times(count, step, carry, backward=False):
    if count <= 16:
        for i in range(count):
            carry = step(count - 1 - i if backward else i, carry)
        return carry
    return lax.fori_loop(0, count, lambda i, c: step(count - 1 - i if backward else i, c), carry)


class Step:
    def __init__(self, step, side, ok):
        self.step, self.side, self.ok = step, side, ok

    def back(self):
        return Step(-self.step, 1 - self.side, self.ok)


def steps_along(at, count):
    if count == 1:
        return []
    if count == 2:
        return [Step(1 - 2 * at, 1 - at, None)]
    return [Step(-1, 0, at > 0), Step(1, 1, at < count - 1)]


STAY = Step(0, 0, None)


def aligned(start, unit):
    return start if isinstance(start, int) else pl.multiple_of(start, unit)


def matches(left, right):
    return jnp.where(left == right, 1.0, 0.0).astype(BF16)


def tap_parts(tap):
    plane = (tap >= 9).astype(jnp.int32) + (tap >= 18).astype(jnp.int32)
    rest = tap - 9 * plane
    line = (rest >= 3).astype(jnp.int32) + (rest >= 6).astype(jnp.int32)
    return plane, line, rest - 3 * line


def banded_rows(weight, bias, count, over_planes):
    outs, taps = weight.shape
    size = count + 2
    block = 10 * size
    shape = (taps, 3 * block)
    plane, line, step = tap_parts(row_of(shape))
    slow, fast = (line, plane) if over_planes else (plane, line)
    start = size * (3 * step + slow) + fast
    col = lane_of(shape)
    high, low = split(weight)
    shape = (outs, 3 * block)
    steady = jnp.zeros(shape, F32)
    for piece in range(3):
        piece_of = bias.astype(BF16).astype(F32)
        steady = jnp.where(lane_of(shape) == 9 * size + piece, piece_of, steady)
        bias = bias - piece_of
    parts = []
    for at in range(count):
        first = matches(col, start + at) + matches(col, start + at + block)
        last = matches(col, start + at + 2 * block)
        parts.append((mxu(high, first) + mxu(low, last) + steady).astype(BF16))
    return parts


def second_rows(turned, ins):
    return left_rows(
        jnp.concatenate(
            [
                jnp.concatenate(
                    [
                        turned[ins * (9 * a + 3 * b + c) : ins * (9 * a + 3 * b + c + 1)]
                        for c in range(3)
                        for b in range(3)
                    ],
                    axis=0,
                ).T
                for a in range(3)
            ],
            axis=0,
        )
    )


def last_rows(weight):
    outs, ins, taps = weight.shape
    shape = (taps, taps * ins)
    plane, line, step = tap_parts(row_of(shape))
    place = matches(3 * (3 * line + step) + plane, lane_of(shape) // ins)
    shape = (outs * ins, taps * ins)
    keep = (row_of(shape) % ins) == (lane_of(shape) % ins)
    shape = (outs, outs * ins)
    collect = matches(row_of(shape), lane_of(shape) // ins)
    parts = []
    for part in split(weight.reshape(outs * ins, taps)):
        grown = jnp.where(keep, mxu(part, place), 0.0).astype(BF16)
        parts.append(mxu(collect, grown).astype(BF16))
    third = taps * ins // 3
    high, low = (
        jnp.concatenate([p[:, third * b : third * (b + 1)] for b in range(3)], axis=0) for p in parts
    )
    return jnp.concatenate([high, low], axis=0)


def window_of(shifted, start, count, spare):
    halves = [
        jnp.concatenate([shifted[s, pl.ds(start, count), :] for s in three] + [spare], axis=0)
        for three in (range(3), range(3, 6))
    ]
    return right_rows(*split(jnp.concatenate(halves, axis=1)))


def store_shifts(shifted, where, value, beyond):
    size = value.shape[1]
    lane = lane_of(value.shape)
    shifted[0, where, :] = pltpu.roll(jnp.where(lane == size - 1, beyond, value), 1, 1)
    shifted[1, where, :] = value
    shifted[2, where, :] = pltpu.roll(jnp.where(lane == 0, beyond, value), size - 1, 1)
    shifted[3, where, :] = pltpu.roll(jnp.where(lane == size - 2, beyond, value), 1, 1)
    shifted[4, where, :] = beyond
    shifted[5, where, :] = pltpu.roll(jnp.where(lane == 1, beyond, value), size - 1, 1)


def stacked_shifts(field, count):
    size = field.shape[1] // 2
    inner, outer = field[:, 0:size], field[:, size:]
    lane = lane_of(inner.shape)
    fields = (
        pltpu.roll(jnp.where(lane == size - 1, outer, inner), 1, 1),
        inner,
        pltpu.roll(jnp.where(lane == 0, outer, inner), size - 1, 1),
    )
    return tuple(
        jnp.concatenate(
            [jnp.concatenate([v[16 * j : 16 * j + 48] for j in range(count)], axis=1) for v in values],
            axis=0,
        )
        for values in zip(*(split(f) for f in fields))
    )


def layers_kernel(
    sizes, ranks, bz, by, bx,
    noisy_any, w1_any, b1_any, w2_any, b2_any, head_any, w3_any, b3_any, w4_any, b4_any,
    own_ref, beside_ref, edge_ref, in_left_ref, out_left_ref, out_bias_ref,
    noisy_ref, w1_ref, b1_ref, w2_ref, b2_ref, head_ref, w3_ref, b3_ref, w4_ref, b4_ref, load_sem,
    m1, my, x1, halo, rim, send1, recv1,
    shifted, ready, product, settled, fix, packed, packed_rim,
    x3, own_send, own_recv, beside_send, beside_recv, edge_send, corner_send, edge_recv,
):
    gz, gy, gx = sizes
    depth = gz * bz
    part = by // ranks
    lines = part + 4
    rows = part + 2
    me = lax.axis_index("gz")
    at_y = lax.axis_index("gy")
    at_x = lax.axis_index("gx")
    works = me < ranks
    turned_round = 1 - lax.rem(at_y, 2)
    mine = me + turned_round * (ranks - 1 - 2 * me)
    steps_y = steps_along(at_y, gy)
    steps_x = steps_along(at_x, gx)

    def both(first, second):
        return second if first is None else first if second is None else first & second

    def when(ok, action):
        if ok is None:
            action()
        else:
            pl.when(ok)(action)

    def device(z, dy, dx):
        return {
            "win": lax.axis_index("win"),
            "gz": z,
            "gy": lax.rem(at_y + dy.step + gy, gy),
            "gx": lax.rem(at_x + dx.step + gx, gx),
        }

    def peer(k):
        return lax.rem(me + k, gz)

    def rank_towards(dy):
        return (1 - dy.side) * (ranks - 1)

    def beside(dy):
        return both(mine == rank_towards(dy.back()), dy.ok)

    def home_towards(dy):
        rank = rank_towards(dy)
        return rank + (1 - turned_round) * (ranks - 1 - 2 * rank)

    loads = [
        pltpu.make_async_copy(source, target, load_sem.at[i])
        for i, (source, target) in enumerate(
            (
                (noisy_any, noisy_ref),
                (w1_any.at[:, 0, :], w1_ref),
                (w2_any, w2_ref),
                (w3_any.at[:, 0, :], w3_ref),
                (w4_any, w4_ref),
                (b1_any, b1_ref),
                (b2_any, b2_ref),
                (head_any, head_ref),
                (b3_any, b3_ref),
                (b4_any, b4_ref),
            )
        )
    ]
    loads[0].start()
    barrier = pltpu.get_barrier_semaphore()

    def greet(dy, dx):
        for k in range(gz - 1, 0 if dy is STAY and dx is STAY else -1, -1):
            pl.semaphore_signal(barrier, inc=1, device_id=device(peer(k), dy, dx), device_id_type=MESH)

    for dy in steps_y:
        @functools.partial(when, beside(dy))
        def greet_beside(dy=dy):
            for dx in [STAY] + steps_x:
                when(dx.ok, functools.partial(greet, dy, dx))

    @pl.when(works)
    def greet_along():
        for dx in [STAY] + steps_x:
            when(dx.ok, functools.partial(greet, STAY, dx))


    loads[0].wait()
    for index, first in ((0, 0), (1, by - 2)):
        for z in range(bz):
            halo[index, 2 * z : 2 * z + 2, :] = noisy_ref[z * by + first : z * by + first + 2, :]
    lane = lane_of((by, bx))
    corner = jnp.zeros((by, bx), F32)
    for z in range(bz):
        turned = pltpu.roll(noisy_ref[z * by : (z + 1) * by, :], 4 * z + 2, 1)
        corner = jnp.where((lane >= 4 * z) & (lane < 4 * z + 4), turned, corner)
    rim[...] = corner

    count_y = (at_y > 0).astype(jnp.int32) + (at_y < gy - 1).astype(jnp.int32)
    count_x = (at_x > 0).astype(jnp.int32) + (at_x < gx - 1).astype(jnp.int32)
    pl.semaphore_wait(
        barrier, ranks - works.astype(jnp.int32) + count_y + count_x * ranks + count_y * count_x
    )

    def rows_of(z, count):
        return pl.ds(aligned(z * count, count), count)

    def own_first(k, source):
        return pltpu.make_async_remote_copy(
            src_ref=noisy_ref,
            dst_ref=m1.at[rows_of(source, bz * by), :],
            send_sem=send1.at[0, k],
            recv_sem=recv1.at[0, source],
            device_id=device(k, STAY, STAY),
            device_id_type=MESH,
        )

    def halo_first(dy, source):
        return pltpu.make_async_remote_copy(
            src_ref=halo.at[dy.side],
            dst_ref=my.at[1 - dy.side, rows_of(source, bz * 2), :],
            send_sem=send1.at[1, dy.side],
            recv_sem=recv1.at[2 - dy.side, source],
            device_id=device(home_towards(dy), dy, STAY),
            device_id_type=MESH,
        )

    def edge_first(dx, k, source):
        return pltpu.make_async_remote_copy(
            src_ref=rim,
            dst_ref=x1.at[0, 1 - dx.side, source],
            send_sem=send1.at[2 + dx.side, k],
            recv_sem=recv1.at[4 - dx.side, source],
            device_id=device(k, STAY, dx),
            device_id_type=MESH,
        )

    def corner_first(dy, dx, source):
        return pltpu.make_async_remote_copy(
            src_ref=rim,
            dst_ref=x1.at[2 - dy.side, 1 - dx.side, source],
            send_sem=send1.at[4 + dy.side, dx.side],
            recv_sem=recv1.at[8 - 2 * dy.side - dx.side, source],
            device_id=device(home_towards(dy), dy, dx),
            device_id_type=MESH,
        )

    early = []
    for dy in steps_y:
        early.append((dy.ok, functools.partial(halo_first, dy)))
        for dx in steps_x:
            early.append((both(dy.ok, dx.ok), functools.partial(corner_first, dy, dx)))
    for k in range(ranks):
        early.append((me != k, functools.partial(own_first, k)))
        for dx in steps_x:
            early.append((dx.ok, functools.partial(edge_first, dx, k)))
    for ok, make in early:
        when(ok, lambda make=make: make(me).start())
    for load in loads[1:]:
        load.start()

    for load in loads[1:]:
        load.wait()
    for index, ok in ((0, at_y == 0), (1, at_y == gy - 1)):
        def no_row(index=index):
            my[index] = jnp.zeros(my.shape[1:], F32)
            x1[1 + index] = jnp.zeros(x1.shape[1:], F32)
            beside_ref[index] = jnp.zeros(beside_ref.shape[1:], F32)
            x3[ranks + index] = jnp.zeros(x3.shape[1:], F32)
        pl.when(ok)(no_row)
    for index, ok in ((0, at_x == 0), (1, at_x == gx - 1)):
        def no_side(index=index):
            for slot in range(3):
                x1[slot, index] = jnp.zeros(x1.shape[2:], F32)
            for slot in range(ranks + 2):
                x3[slot, index] = jnp.zeros(x3.shape[2:], F32)
        pl.when(ok)(no_side)
    in_left_ref[...] = jnp.concatenate(
        banded_rows(w3_ref[...], column(b3_ref), bz + 2, True), axis=0
    )
    out_left_ref[...] = last_rows(w4_ref[...])
    out_bias_ref[...] = jnp.broadcast_to(column(b4_ref), out_bias_ref.shape)

    def own_last(k, target):
        return pltpu.make_async_remote_copy(
            src_ref=packed.at[target],
            dst_ref=own_ref.at[k],
            send_sem=own_send.at[target],
            recv_sem=own_recv.at[k],
            device_id=device(target, STAY, STAY),
            device_id_type=MESH,
        )

    def halo_last(dy, target):
        start = aligned(dy.side * ((part - 2) * bx), LANES)
        return pltpu.make_async_remote_copy(
            src_ref=packed.at[target, :, pl.ds(start, 2 * bx)],
            dst_ref=beside_ref.at[1 - dy.side],
            send_sem=beside_send.at[dy.side, target],
            recv_sem=beside_recv.at[1 - dy.side],
            device_id=device(target, dy, STAY),
            device_id_type=MESH,
        )

    def edge_last(dx, k, target):
        return pltpu.make_async_remote_copy(
            src_ref=packed_rim.at[target],
            dst_ref=x3.at[k, 1 - dx.side],
            send_sem=edge_send.at[dx.side, target],
            recv_sem=edge_recv.at[k, 1 - dx.side],
            device_id=device(target, STAY, dx),
            device_id_type=MESH,
        )

    def corner_last(dy, dx, target):
        return pltpu.make_async_remote_copy(
            src_ref=packed_rim.at[target],
            dst_ref=x3.at[ranks + 1 - dy.side, 1 - dx.side],
            send_sem=corner_send.at[dy.side, dx.side, target],
            recv_sem=edge_recv.at[ranks + 1 - dy.side, 1 - dx.side],
            device_id=device(target, dy, dx),
            device_id_type=MESH,
        )

    def late(act, pack=lambda targets: None):
        def to_beside(dy, targets):
            for target in targets:
                act(halo_last(dy, target))
                for dx in steps_x:
                    when(dx.ok, lambda: act(corner_last(dy, dx, target)))

        def to_own(target):
            act(own_last(mine, target))

        def to_edge(target):
            for dx in steps_x:
                when(dx.ok, lambda: act(edge_last(dx, mine, target)))

        pack(range(ranks))
        for dy in steps_y:
            when(beside(dy), functools.partial(to_beside, dy, range(ranks)))
        for k in range(1, ranks):
            to_own(lax.rem(me + k, ranks))
        for target in range(ranks):
            to_edge(target)
        pack(range(ranks, gz))
        for target in range(ranks, gz):
            to_own(target)
            to_edge(target)
        for dy in steps_y:
            when(beside(dy), functools.partial(to_beside, dy, range(ranks, gz)))

    for ok, make in early:
        when(ok, lambda make=make: make(me).wait_send())

    @pl.when(works)
    def layers():
        gate_bias = jnp.concatenate([jnp.zeros((16, 1), F32), column(b1_ref)], axis=0)
        parts = banded_rows(w1_ref[...].T, gate_bias, rows, False)
        first_left = jnp.concatenate([p[:16] for p in parts] + [p[16:] for p in parts], axis=0)
        second_left = second_rows(w2_ref[...].reshape(-1, w2_ref.shape[2]), w2_ref.shape[1])
        second_bias = column(b2_ref)
        head = column(head_ref)
        shape = (16 * rows, 2 * bx)
        lane, row = lane_of(shape), row_of(shape)
        place_y = at_y * by + mine * part + row // 16 - 1
        outside = (place_y < 0) | (place_y >= gy * by)
        outside = outside | ((at_x == 0) & (lane == 2 * bx - 1)) | ((at_x == gx - 1) & (lane == bx))
        mask = jnp.where(outside, 0.0, 1.0).astype(F32)
        for s in range(6):
            for plane in (0, depth + 1):
                shifted[s, plane * lines : (plane + 1) * lines, :] = jnp.zeros((lines, bx), F32)
        for plane in (0, depth + 1):
            product[plane] = jnp.zeros(product.shape[1:], F32)
        fix[...] = jnp.zeros(fix.shape, F32)
        m1[rows_of(me, bz * by), :] = noisy_ref[...]

        def arrive(m):
            def await_own():
                own_first(0, m).wait_recv()
            pl.when(me != m)(await_own)
            for dx in steps_x:
                def await_edge(dx=dx):
                    edge_first(dx.back(), 0, m).wait_recv()
                when(dx.ok, await_edge)
            for dy in steps_y:
                @functools.partial(when, beside(dy))
                def await_beside(dy=dy):
                    halo_first(dy.back(), m).wait_recv()
                    for dx in steps_x:
                        def await_corner(dx=dx):
                            corner_first(dy.back(), dx.back(), m).wait_recv()
                        when(dx.ok, await_corner)

        place = lane_of((by, bx)) % 4

        def cut(full):
            value = full[0:lines]
            for k in range(1, ranks):
                value = jnp.where(mine == k, full[part * k : part * k + lines], value)
            return value

        def gather(m):
            rims = [jnp.where(place < 2, x1[slot, 0, m], x1[slot, 1, m]) for slot in range(3)]
            border = cut(jnp.concatenate([rims[1][by - 2 : by], rims[0], rims[2][0:2]], axis=0))
            below = my[0, rows_of(m, bz * 2), :]
            above = my[1, rows_of(m, bz * 2), :]
            block = m1[rows_of(m, bz * by), :]
            for z in range(bz):
                value = cut(
                    jnp.concatenate(
                        [below[2 * z : 2 * z + 2], block[z * by : (z + 1) * by], above[2 * z : 2 * z + 2]],
                        axis=0,
                    )
                )
                beyond = pltpu.roll(border, (bx - 2 - 4 * z) % bx, 1)
                where = pl.ds(aligned((m * bz + z + 1) * lines, lines), lines)
                store_shifts(shifted, where, value, beyond)

        spare = jnp.ones((lines, bx), F32)

        def gates(z, slot):
            pre = mxu(first_left, window_of(shifted, aligned(z * lines, lines), 3 * lines, spare))
            ready[0, slot] = mask * jnp.tanh(pre[0 : 16 * rows])
            ready[1, slot] = jax.nn.sigmoid(pre[16 * rows :])

        def advance(z, slot, hidden):
            hidden = hidden + ready[1, slot] * (ready[0, slot] - hidden)
            product[z + 1] = mxu(second_left, right_rows(*stacked_shifts(hidden, part)))
            return hidden

        def settle(z):
            pre = product[z, 0:32] + product[z + 1, 32:64] + product[z + 2, 64:96]
            settled[0, z] = jnp.tanh(pre[0:16])
            settled[1, z] = jax.nn.sigmoid(pre[16:32] + second_bias)

        def reach(m, first, count, hidden, start=0):
            arrive(m)
            gather(m)
            for slot in range(count):
                gates(first + slot, slot)
            for slot in range(count):
                hidden = advance(first + slot, slot, hidden)
                if slot >= start:
                    settle(first + slot - 1)
            return hidden

        def later(i, hidden):
            return reach(i + 1, (i + 1) * bz - 1, bz, hidden)

        hidden = reach(0, 0, bz - 1, jnp.zeros((16 * rows, 2 * bx), F32), 1)
        hidden = times(gz - 2, later, hidden)
        reach(gz - 1, depth - bz - 1, bz + 1, hidden)
        settle(depth - 1)

        def back(z, hidden):
            hidden = hidden + settled[1, z] * (settled[0, z] - hidden)
            fix[pl.ds(z + 2, 1), :] = jnp.sum(head * hidden, axis=0, keepdims=True)
            return hidden

        times(depth, back, jnp.zeros((16, part * bx), F32), True)
        lane = lane_of((fix.shape[0], bx))
        border = jnp.zeros((fix.shape[0], bx), F32)
        for j in range(part):
            lanes = slice(j * bx, (j + 1) * bx)
            centre = shifted[1, pl.ds(lines + j + 2, depth, stride=lines), :]
            fix[2 : 2 + depth, lanes] = fix[2 : 2 + depth, lanes] + centre
            turned = pltpu.roll(fix[:, lanes], 4 * j + 2, 1)
            border = jnp.where((lane >= 4 * j) & (lane < 4 * j + 4), turned, border)
        def pack(targets):
            for target in targets:
                packed[target] = fix[bz * target : bz * target + bz + 4, :]
                packed_rim[target] = border[bz * target : bz * target + bz + 4]

        late(lambda copy: copy.start(), pack)
        own_ref[mine] = packed[me]
        late(lambda copy: copy.wait_send())

    for k in range(ranks):
        def await_own(k=k):
            own_last(k, 0).wait_recv()
        pl.when(mine != k)(await_own)
    for dy in steps_y:
        def await_beside(dy=dy):
            halo_last(dy.back(), 0).wait_recv()
        when(dy.ok, await_beside)
    for dx in steps_x:
        def await_rims(dx=dx):
            for k in range(ranks):
                edge_last(dx.back(), k, 0).wait_recv()
        when(dx.ok, await_rims)
        for dy in steps_y:
            def await_corner(dy=dy, dx=dx):
                corner_last(dy.back(), dx.back(), 0).wait_recv()
            when(both(dy.ok, dx.ok), await_corner)
    place = lane_of((bz + 4, bx)) % 4
    for line in range(by + 4):
        if line < 2:
            slot, j = ranks, part - 2 + line
        elif line < by + 2:
            slot, j = (line - 2) // part, (line - 2) % part
        else:
            slot, j = ranks + 1, line - by - 2
        beyond = jnp.where(place < 2, x3[slot, 0], x3[slot, 1])
        edge_ref[line] = pltpu.roll(beyond, (bx - 2 - 4 * j) % bx, 1)


def segment_kernel(
    sizes, own_ref, beside_ref, edge_ref, in_left_ref, out_left_ref, out_bias_ref,
    clean_any, out_any, shifted, ready, product, result, clean, sems,
):
    gz, gy, gx = sizes
    ranks = own_ref.shape[0]
    lines, planes, bx = edge_ref.shape
    by, bz = lines - 4, planes - 4
    part = by // ranks
    me = lax.axis_index("gz")
    at_y = lax.axis_index("gy")
    at_x = lax.axis_index("gx")

    def middle_of(line):
        if 2 <= line < by + 2:
            k, j = divmod(line - 2, part)
            return own_ref[k, :, j * bx : (j + 1) * bx]
        index, j = (0, line) if line < 2 else (1, line - by - 2)
        return beside_ref[index, :, j * bx : (j + 1) * bx]

    for line in range(lines):
        store_shifts(shifted, slice(line * planes, (line + 1) * planes), middle_of(line), edge_ref[line])
    in_left = in_left_ref[...]
    out_left = out_left_ref[...]
    out_bias = out_bias_ref[:, 0:1]
    shape = (16 * (bz + 2), 2 * bx)
    lane, plane = lane_of(shape), row_of(shape) // 16
    outside = ((me == 0) & (plane == 0)) | ((me == gz - 1) & (plane == bz + 1))
    outside = outside | ((at_x == 0) & (lane == 2 * bx - 1)) | ((at_x == gx - 1) & (lane == bx))
    mask = jnp.where(outside, 0.0, 1.0).astype(F32)
    spare = jnp.ones((planes, bx), F32)
    for y in range(by + 2):
        grown = jnp.maximum(mxu(in_left, window_of(shifted, y * planes, 3 * planes, spare)), 0.0) * mask
        if y == 0:
            grown = grown * jnp.where(at_y > 0, 1.0, 0.0).astype(F32)
        if y == by + 1:
            grown = grown * jnp.where(at_y < gy - 1, 1.0, 0.0).astype(F32)
        ready[y] = grown
    for z in range(bz):
        for y in range(by):
            clean[z, y : y + 1, :] = middle_of(2 + y)[2 + z : 3 + z]
    first = pltpu.make_async_copy(clean, clean_any, sems.at[0])
    first.start()
    for y in range(by + 2):
        high, low = stacked_shifts(ready[y], bz)
        double = mxu(out_left, high)
        product[y] = double[0:48] + double[48:96] + mxu(out_left[0:48], low)
        if y >= 2:
            total = product[y - 2, 0:16] + product[y - 1, 16:32] + product[y, 32:48] + out_bias
            for z in range(bz):
                result[pl.ds(z * by + y - 2, 16, stride=bz * by), :] = total[:, z * bx : (z + 1) * bx]
    second = pltpu.make_async_copy(result.at[0 : 16 * bz * by, :], out_any, sems.at[1])
    second.start()
    first.wait()
    second.wait()


def body(sizes, noisy, first_weight, first_bias, second_weight, second_bias, head_weight,
         seg_weight_in, seg_bias_in, seg_weight_out, seg_bias_out):
    gz, gy, gx = sizes
    bz, by, bx = noisy.shape
    ranks = by // 4
    part = by // ranks
    lines = part + 4
    depth = gz * bz
    args = [
        noisy.reshape(bz * by, bx),
        first_weight.transpose(2, 1, 0),
        first_bias.reshape(1, -1),
        second_weight.transpose(2, 1, 0),
        second_bias.reshape(1, -1),
        head_weight.reshape(1, -1),
        seg_weight_in,
        seg_bias_in.reshape(1, -1),
        seg_weight_out,
        seg_bias_out.reshape(1, -1),
    ]
    vmem = pl.BlockSpec(memory_space=pltpu.VMEM)
    dma = pltpu.SemaphoreType.DMA
    rest = pl.BlockSpec(memory_space=pl.ANY)

    def room(*shape):
        return pltpu.VMEM(shape, F32)

    stages = [
        room(*(a.shape if i not in (1, 6) else (a.shape[0], a.shape[2]))) for i, a in enumerate(args)
    ]
    handed = pl.pallas_call(
        functools.partial(layers_kernel, sizes, ranks, bz, by, bx),
        out_shape=[
            room(ranks, bz + 4, part * bx),
            room(2, bz + 4, 2 * bx),
            room(by + 4, bz + 4, bx),
            pltpu.VMEM((16 * (bz + 2), 30 * (bz + 4)), BF16),
            pltpu.VMEM((96, 144), BF16),
            room(16, LANES),
        ],
        in_specs=[rest] * len(args),
        out_specs=[vmem] * 6,
        scratch_shapes=stages
        + [
            dma((len(args),)),
            room(depth * by, bx),
            room(2, depth * 2, bx),
            room(3, 2, gz, by, bx),
            room(2, bz * 2, bx),
            room(by, bx),
            dma((6, max(ranks, 2))),
            dma((9, gz)),
            room(6, (depth + 2) * lines, bx),
            room(2, bz + 1, 16 * (part + 2), 2 * bx),
            room(depth + 2, 96, part * bx),
            room(2, depth, 16, part * bx),
            room(depth + 16, part * bx),
            room(gz, bz + 4, part * bx),
            room(gz, bz + 4, bx),
            room(ranks + 2, 2, bz + 4, bx),
            dma((gz,)),
            dma((ranks,)),
            dma((2, gz)),
            dma((2,)),
            dma((2, gz)),
            dma((2, 2, gz)),
            dma((ranks + 2, 2)),
        ],
        compiler_params=pltpu.CompilerParams(
            collective_id=0, has_side_effects=True, vmem_limit_bytes=GRANT
        ),
        name="layers",
    )(*(pltpu.with_memory_space_constraint(a, pltpu.HBM) for a in args))
    clean, features = pl.pallas_call(
        functools.partial(segment_kernel, sizes),
        out_shape=[
            jax.ShapeDtypeStruct((bz, by, bx), F32),
            jax.ShapeDtypeStruct((16 * bz * by, bx), F32),
        ],
        in_specs=[vmem] * 6,
        out_specs=[rest] * 2,
        scratch_shapes=[
            room(6, (by + 4) * (bz + 4), bx),
            room(by + 2, 16 * (bz + 2), 2 * bx),
            room(by + 2, 48, bz * bx),
            room(17 * bz * by, bx),
            room(bz, by, bx),
            dma((2,)),
        ],
        compiler_params=pltpu.CompilerParams(vmem_limit_bytes=GRANT),
        name="segment",
    )(*handed)
    return clean, features.reshape(16, bz, by, bx)


def solution(mesh):
    sizes = (mesh.shape["gz"], mesh.shape["gy"], mesh.shape["gx"])
    in_specs = (P(("win", "gz"), "gy", "gx"), P(), P(), P(), P(), P(), P(), P(), P(), P())
    out_specs = (P(("win", "gz"), "gy", "gx"), P(None, ("win", "gz"), "gy", "gx"))
    return jax.shard_map(
        functools.partial(body, sizes), mesh=mesh, in_specs=in_specs, out_specs=out_specs, check_vma=False
    )
```

```python
import functools

import jax
import jax.numpy as jnp
from jax import lax
from jax.experimental import pallas as pl
from jax.experimental.pallas import tpu as pltpu
from jax.sharding import PartitionSpec as P

LANES = 128
GRANT = 48 << 20
F32 = jnp.float32
BF16 = jnp.bfloat16
MESH = pl.DeviceIdType.MESH


def split(value):
    high = value.astype(BF16)
    return high, (value - high.astype(F32)).astype(BF16)


def left_rows(weight):
    high, low = split(weight)
    return jnp.concatenate([high, high, low], axis=1)


def right_rows(high, low):
    return jnp.concatenate([high, low, high], axis=0)


def mxu(left, right):
    return jnp.dot(left, right, preferred_element_type=F32)


def lane_of(shape):
    return lax.broadcasted_iota(jnp.int32, shape, len(shape) - 1)


def row_of(shape):
    return lax.broadcasted_iota(jnp.int32, shape, 0)


def column(row_ref):
    count = row_ref.shape[1]
    shape = (count, count)
    spread = jnp.broadcast_to(row_ref[...], shape)
    return jnp.sum(jnp.where(row_of(shape) == lane_of(shape), spread, 0.0), axis=1, keepdims=True)


def times(count, step, carry, backward=False):
    if count <= 16:
        for i in range(count):
            carry = step(count - 1 - i if backward else i, carry)
        return carry
    return lax.fori_loop(0, count, lambda i, c: step(count - 1 - i if backward else i, c), carry)


class Step:
    def __init__(self, step, side, ok):
        self.step, self.side, self.ok = step, side, ok

    def back(self):
        return Step(-self.step, 1 - self.side, self.ok)


def steps_along(at, count):
    if count == 1:
        return []
    if count == 2:
        return [Step(1 - 2 * at, 1 - at, None)]
    return [Step(-1, 0, at > 0), Step(1, 1, at < count - 1)]


STAY = Step(0, 0, None)


def aligned(start, unit):
    return start if isinstance(start, int) else pl.multiple_of(start, unit)


def matches(left, right):
    return jnp.where(left == right, 1.0, 0.0).astype(BF16)


def tap_parts(tap):
    plane = (tap >= 9).astype(jnp.int32) + (tap >= 18).astype(jnp.int32)
    rest = tap - 9 * plane
    line = (rest >= 3).astype(jnp.int32) + (rest >= 6).astype(jnp.int32)
    return plane, line, rest - 3 * line


def banded_rows(weight, bias, count, over_planes):
    outs, taps = weight.shape
    size = count + 2
    block = 10 * size
    shape = (taps, 3 * block)
    plane, line, step = tap_parts(row_of(shape))
    slow, fast = (line, plane) if over_planes else (plane, line)
    start = size * (3 * step + slow) + fast
    col = lane_of(shape)
    high, low = split(weight)
    shape = (outs, 3 * block)
    steady = jnp.zeros(shape, F32)
    for piece in range(3):
        piece_of = bias.astype(BF16).astype(F32)
        steady = jnp.where(lane_of(shape) == 9 * size + piece, piece_of, steady)
        bias = bias - piece_of
    parts = []
    for at in range(count):
        first = matches(col, start + at) + matches(col, start + at + block)
        last = matches(col, start + at + 2 * block)
        parts.append((mxu(high, first) + mxu(low, last) + steady).astype(BF16))
    return parts


def second_rows(turned, ins):
    return left_rows(
        jnp.concatenate(
            [
                jnp.concatenate(
                    [
                        turned[ins * (9 * a + 3 * b + c) : ins * (9 * a + 3 * b + c + 1)]
                        for c in range(3)
                        for b in range(3)
                    ],
                    axis=0,
                ).T
                for a in range(3)
            ],
            axis=0,
        )
    )


def last_rows(weight):
    outs, ins, taps = weight.shape
    shape = (taps, taps * ins)
    plane, line, step = tap_parts(row_of(shape))
    place = matches(3 * (3 * line + step) + plane, lane_of(shape) // ins)
    shape = (outs * ins, taps * ins)
    keep = (row_of(shape) % ins) == (lane_of(shape) % ins)
    shape = (outs, outs * ins)
    collect = matches(row_of(shape), lane_of(shape) // ins)
    parts = []
    for part in split(weight.reshape(outs * ins, taps)):
        grown = jnp.where(keep, mxu(part, place), 0.0).astype(BF16)
        parts.append(mxu(collect, grown).astype(BF16))
    third = taps * ins // 3
    high, low = (
        jnp.concatenate([p[:, third * b : third * (b + 1)] for b in range(3)], axis=0) for p in parts
    )
    return jnp.concatenate([high, low], axis=0)


def window_of(shifted, start, count, spare):
    halves = [
        jnp.concatenate([shifted[s, pl.ds(start, count), :] for s in three] + [spare], axis=0)
        for three in (range(3), range(3, 6))
    ]
    return right_rows(*split(jnp.concatenate(halves, axis=1)))


def store_shifts(shifted, where, value, beyond):
    size = value.shape[1]
    lane = lane_of(value.shape)
    shifted[0, where, :] = pltpu.roll(jnp.where(lane == size - 1, beyond, value), 1, 1)
    shifted[1, where, :] = value
    shifted[2, where, :] = pltpu.roll(jnp.where(lane == 0, beyond, value), size - 1, 1)
    shifted[3, where, :] = pltpu.roll(jnp.where(lane == size - 2, beyond, value), 1, 1)
    shifted[4, where, :] = beyond
    shifted[5, where, :] = pltpu.roll(jnp.where(lane == 1, beyond, value), size - 1, 1)


def stacked_shifts(field, count):
    size = field.shape[1] // 2
    inner, outer = field[:, 0:size], field[:, size:]
    lane = lane_of(inner.shape)
    fields = (
        pltpu.roll(jnp.where(lane == size - 1, outer, inner), 1, 1),
        inner,
        pltpu.roll(jnp.where(lane == 0, outer, inner), size - 1, 1),
    )
    return tuple(
        jnp.concatenate(
            [jnp.concatenate([v[16 * j : 16 * j + 48] for j in range(count)], axis=1) for v in values],
            axis=0,
        )
        for values in zip(*(split(f) for f in fields))
    )


def layers_kernel(
    sizes, ranks, bz, by, bx,
    noisy_any, w1_any, b1_any, w2_any, b2_any, head_any, w3_any, b3_any, w4_any, b4_any,
    own_ref, beside_ref, edge_ref, in_left_ref, out_left_ref, out_bias_ref,
    noisy_ref, w1_ref, b1_ref, w2_ref, b2_ref, head_ref, w3_ref, b3_ref, w4_ref, b4_ref, load_sem,
    m1, my, x1, halo, rim, send1, recv1,
    shifted, ready, product, settled, fix, packed, packed_rim,
    x3, own_send, own_recv, beside_send, beside_recv, edge_send, corner_send, edge_recv,
):
    gz, gy, gx = sizes
    depth = gz * bz
    part = by // ranks
    lines = part + 4
    rows = part + 2
    me = lax.axis_index("gz")
    at_y = lax.axis_index("gy")
    at_x = lax.axis_index("gx")
    works = me < ranks
    turned_round = 1 - lax.rem(at_y, 2)
    mine = me + turned_round * (ranks - 1 - 2 * me)
    steps_y = steps_along(at_y, gy)
    steps_x = steps_along(at_x, gx)

    def both(first, second):
        return second if first is None else first if second is None else first & second

    def when(ok, action):
        if ok is None:
            action()
        else:
            pl.when(ok)(action)

    def device(z, dy, dx):
        return {
            "win": lax.axis_index("win"),
            "gz": z,
            "gy": lax.rem(at_y + dy.step + gy, gy),
            "gx": lax.rem(at_x + dx.step + gx, gx),
        }

    def peer(k):
        return lax.rem(me + k, gz)

    def rank_towards(dy):
        return (1 - dy.side) * (ranks - 1)

    def beside(dy):
        return both(mine == rank_towards(dy.back()), dy.ok)

    def home_towards(dy):
        rank = rank_towards(dy)
        return rank + (1 - turned_round) * (ranks - 1 - 2 * rank)

    loads = [
        pltpu.make_async_copy(source, target, load_sem.at[i])
        for i, (source, target) in enumerate(
            (
                (noisy_any, noisy_ref),
                (w1_any.at[:, 0, :], w1_ref),
                (w2_any, w2_ref),
                (w3_any.at[:, 0, :], w3_ref),
                (w4_any, w4_ref),
                (b1_any, b1_ref),
                (b2_any, b2_ref),
                (head_any, head_ref),
                (b3_any, b3_ref),
                (b4_any, b4_ref),
            )
        )
    ]
    loads[0].start()
    barrier = pltpu.get_barrier_semaphore()

    def greet(dy, dx):
        for k in range(gz - 1, 0 if dy is STAY and dx is STAY else -1, -1):
            pl.semaphore_signal(barrier, inc=1, device_id=device(peer(k), dy, dx), device_id_type=MESH)

    for dy in steps_y:
        @functools.partial(when, beside(dy))
        def greet_beside(dy=dy):
            for dx in [STAY] + steps_x:
                when(dx.ok, functools.partial(greet, dy, dx))

    @pl.when(works)
    def greet_along():
        for dx in [STAY] + steps_x:
            when(dx.ok, functools.partial(greet, STAY, dx))

    for load in loads[1:]:
        load.start()

    loads[0].wait()
    for index, first in ((0, 0), (1, by - 2)):
        for z in range(bz):
            halo[index, 2 * z : 2 * z + 2, :] = noisy_ref[z * by + first : z * by + first + 2, :]
    lane = lane_of((by, bx))
    corner = jnp.zeros((by, bx), F32)
    for z in range(bz):
        turned = pltpu.roll(noisy_ref[z * by : (z + 1) * by, :], 4 * z + 2, 1)
        corner = jnp.where((lane >= 4 * z) & (lane < 4 * z + 4), turned, corner)
    rim[...] = corner

    count_y = (at_y > 0).astype(jnp.int32) + (at_y < gy - 1).astype(jnp.int32)
    count_x = (at_x > 0).astype(jnp.int32) + (at_x < gx - 1).astype(jnp.int32)
    pl.semaphore_wait(
        barrier, ranks - works.astype(jnp.int32) + count_y + count_x * ranks + count_y * count_x
    )

    def rows_of(z, count):
        return pl.ds(aligned(z * count, count), count)

    def own_first(k, source):
        return pltpu.make_async_remote_copy(
            src_ref=noisy_ref,
            dst_ref=m1.at[rows_of(source, bz * by), :],
            send_sem=send1.at[0, k],
            recv_sem=recv1.at[0, source],
            device_id=device(k, STAY, STAY),
            device_id_type=MESH,
        )

    def halo_first(dy, source):
        return pltpu.make_async_remote_copy(
            src_ref=halo.at[dy.side],
            dst_ref=my.at[1 - dy.side, rows_of(source, bz * 2), :],
            send_sem=send1.at[1, dy.side],
            recv_sem=recv1.at[2 - dy.side, source],
            device_id=device(home_towards(dy), dy, STAY),
            device_id_type=MESH,
        )

    def edge_first(dx, k, source):
        return pltpu.make_async_remote_copy(
            src_ref=rim,
            dst_ref=x1.at[0, 1 - dx.side, source],
            send_sem=send1.at[2 + dx.side, k],
            recv_sem=recv1.at[4 - dx.side, source],
            device_id=device(k, STAY, dx),
            device_id_type=MESH,
        )

    def corner_first(dy, dx, source):
        return pltpu.make_async_remote_copy(
            src_ref=rim,
            dst_ref=x1.at[2 - dy.side, 1 - dx.side, source],
            send_sem=send1.at[4 + dy.side, dx.side],
            recv_sem=recv1.at[8 - 2 * dy.side - dx.side, source],
            device_id=device(home_towards(dy), dy, dx),
            device_id_type=MESH,
        )

    early = []
    for dy in steps_y:
        early.append((dy.ok, functools.partial(halo_first, dy)))
        for dx in steps_x:
            early.append((both(dy.ok, dx.ok), functools.partial(corner_first, dy, dx)))
    for k in range(ranks):
        early.append((me != k, functools.partial(own_first, k)))
        for dx in steps_x:
            early.append((dx.ok, functools.partial(edge_first, dx, k)))
    for ok, make in early:
        when(ok, lambda make=make: make(me).start())

    for load in loads[1:]:
        load.wait()
    for index, ok in ((0, at_y == 0), (1, at_y == gy - 1)):
        def no_row(index=index):
            my[index] = jnp.zeros(my.shape[1:], F32)
            x1[1 + index] = jnp.zeros(x1.shape[1:], F32)
            beside_ref[index] = jnp.zeros(beside_ref.shape[1:], F32)
            x3[ranks + index] = jnp.zeros(x3.shape[1:], F32)
        pl.when(ok)(no_row)
    for index, ok in ((0, at_x == 0), (1, at_x == gx - 1)):
        def no_side(index=index):
            for slot in range(3):
                x1[slot, index] = jnp.zeros(x1.shape[2:], F32)
            for slot in range(ranks + 2):
                x3[slot, index] = jnp.zeros(x3.shape[2:], F32)
        pl.when(ok)(no_side)
    in_left_ref[...] = jnp.concatenate(
        banded_rows(w3_ref[...], column(b3_ref), bz + 2, True), axis=0
    )
    out_left_ref[...] = last_rows(w4_ref[...])
    out_bias_ref[...] = jnp.broadcast_to(column(b4_ref), out_bias_ref.shape)

    def own_last(k, target):
        return pltpu.make_async_remote_copy(
            src_ref=packed.at[target],
            dst_ref=own_ref.at[k],
            send_sem=own_send.at[target],
            recv_sem=own_recv.at[k],
            device_id=device(target, STAY, STAY),
            device_id_type=MESH,
        )

    def halo_last(dy, target):
        start = aligned(dy.side * ((part - 2) * bx), LANES)
        return pltpu.make_async_remote_copy(
            src_ref=packed.at[target, :, pl.ds(start, 2 * bx)],
            dst_ref=beside_ref.at[1 - dy.side],
            send_sem=beside_send.at[dy.side, target],
            recv_sem=beside_recv.at[1 - dy.side],
            device_id=device(target, dy, STAY),
            device_id_type=MESH,
        )

    def edge_last(dx, k, target):
        return pltpu.make_async_remote_copy(
            src_ref=packed_rim.at[target],
            dst_ref=x3.at[k, 1 - dx.side],
            send_sem=edge_send.at[dx.side, target],
            recv_sem=edge_recv.at[k, 1 - dx.side],
            device_id=device(target, STAY, dx),
            device_id_type=MESH,
        )

    def corner_last(dy, dx, target):
        return pltpu.make_async_remote_copy(
            src_ref=packed_rim.at[target],
            dst_ref=x3.at[ranks + 1 - dy.side, 1 - dx.side],
            send_sem=corner_send.at[dy.side, dx.side, target],
            recv_sem=edge_recv.at[ranks + 1 - dy.side, 1 - dx.side],
            device_id=device(target, dy, dx),
            device_id_type=MESH,
        )

    def late(act, pack=lambda targets: None):
        def to_beside(dy, targets):
            for target in targets:
                act(halo_last(dy, target))
                for dx in steps_x:
                    when(dx.ok, lambda: act(corner_last(dy, dx, target)))

        def to_own(target):
            act(own_last(mine, target))

        def to_edge(target):
            for dx in steps_x:
                when(dx.ok, lambda: act(edge_last(dx, mine, target)))

        pack(range(ranks))
        for dy in steps_y:
            when(beside(dy), functools.partial(to_beside, dy, range(ranks)))
        for k in range(1, ranks):
            to_own(lax.rem(me + k, ranks))
        for target in range(ranks):
            to_edge(target)
        pack(range(ranks, gz))
        for target in range(ranks, gz):
            to_own(target)
            to_edge(target)
        for dy in steps_y:
            when(beside(dy), functools.partial(to_beside, dy, range(ranks, gz)))

    for ok, make in early:
        when(ok, lambda make=make: make(me).wait_send())

    @pl.when(works)
    def layers():
        gate_bias = jnp.concatenate([jnp.zeros((16, 1), F32), column(b1_ref)], axis=0)
        parts = banded_rows(w1_ref[...].T, gate_bias, rows, False)
        first_left = jnp.concatenate([p[:16] for p in parts] + [p[16:] for p in parts], axis=0)
        second_left = second_rows(w2_ref[...].reshape(-1, w2_ref.shape[2]), w2_ref.shape[1])
        second_bias = column(b2_ref)
        head = column(head_ref)
        shape = (16 * rows, 2 * bx)
        lane, row = lane_of(shape), row_of(shape)
        place_y = at_y * by + mine * part + row // 16 - 1
        outside = (place_y < 0) | (place_y >= gy * by)
        outside = outside | ((at_x == 0) & (lane == 2 * bx - 1)) | ((at_x == gx - 1) & (lane == bx))
        mask = jnp.where(outside, 0.0, 1.0).astype(F32)
        for s in range(6):
            for plane in (0, depth + 1):
                shifted[s, plane * lines : (plane + 1) * lines, :] = jnp.zeros((lines, bx), F32)
        for plane in (0, depth + 1):
            product[plane] = jnp.zeros(product.shape[1:], F32)
        fix[...] = jnp.zeros(fix.shape, F32)
        m1[rows_of(me, bz * by), :] = noisy_ref[...]

        def arrive(m):
            def await_own():
                own_first(0, m).wait_recv()
            pl.when(me != m)(await_own)
            for dx in steps_x:
                def await_edge(dx=dx):
                    edge_first(dx.back(), 0, m).wait_recv()
                when(dx.ok, await_edge)
            for dy in steps_y:
                @functools.partial(when, beside(dy))
                def await_beside(dy=dy):
                    halo_first(dy.back(), m).wait_recv()
                    for dx in steps_x:
                        def await_corner(dx=dx):
                            corner_first(dy.back(), dx.back(), m).wait_recv()
                        when(dx.ok, await_corner)

        place = lane_of((by, bx)) % 4

        def cut(full):
            value = full[0:lines]
            for k in range(1, ranks):
                value = jnp.where(mine == k, full[part * k : part * k + lines], value)
            return value

        def gather(m):
            rims = [jnp.where(place < 2, x1[slot, 0, m], x1[slot, 1, m]) for slot in range(3)]
            border = cut(jnp.concatenate([rims[1][by - 2 : by], rims[0], rims[2][0:2]], axis=0))
            below = my[0, rows_of(m, bz * 2), :]
            above = my[1, rows_of(m, bz * 2), :]
            block = m1[rows_of(m, bz * by), :]
            for z in range(bz):
                value = cut(
                    jnp.concatenate(
                        [below[2 * z : 2 * z + 2], block[z * by : (z + 1) * by], above[2 * z : 2 * z + 2]],
                        axis=0,
                    )
                )
                beyond = pltpu.roll(border, (bx - 2 - 4 * z) % bx, 1)
                where = pl.ds(aligned((m * bz + z + 1) * lines, lines), lines)
                store_shifts(shifted, where, value, beyond)

        spare = jnp.ones((lines, bx), F32)

        def gates(z, slot):
            pre = mxu(first_left, window_of(shifted, aligned(z * lines, lines), 3 * lines, spare))
            ready[0, slot] = mask * jnp.tanh(pre[0 : 16 * rows])
            ready[1, slot] = jax.nn.sigmoid(pre[16 * rows :])

        def advance(slot, hidden):
            hidden = hidden + ready[1, slot] * (ready[0, slot] - hidden)
            ready[0, slot] = hidden
            return hidden

        def spread(z, slot):
            product[z + 1] = mxu(second_left, right_rows(*stacked_shifts(ready[0, slot], part)))

        def settle(z):
            pre = product[z, 0:32] + product[z + 1, 32:64] + product[z + 2, 64:96]
            settled[0, z] = jnp.tanh(pre[0:16])
            settled[1, z] = jax.nn.sigmoid(pre[16:32] + second_bias)

        def reach(m, first, count, hidden, start=0):
            arrive(m)
            gather(m)
            for slot in range(count):
                gates(first + slot, slot)
            for slot in range(count):
                hidden = advance(slot, hidden)
            for slot in range(count):
                spread(first + slot, slot)
                if slot >= start:
                    settle(first + slot - 1)
            return hidden

        def later(i, hidden):
            return reach(i + 1, (i + 1) * bz - 1, bz, hidden)

        hidden = reach(0, 0, bz - 1, jnp.zeros((16 * rows, 2 * bx), F32), 1)
        hidden = times(gz - 2, later, hidden)
        reach(gz - 1, depth - bz - 1, bz + 1, hidden)
        settle(depth - 1)

        def back(z, hidden):
            hidden = hidden + settled[1, z] * (settled[0, z] - hidden)
            fix[pl.ds(z + 2, 1), :] = jnp.sum(head * hidden, axis=0, keepdims=True)
            return hidden

        times(depth, back, jnp.zeros((16, part * bx), F32), True)
        lane = lane_of((fix.shape[0], bx))
        border = jnp.zeros((fix.shape[0], bx), F32)
        for j in range(part):
            lanes = slice(j * bx, (j + 1) * bx)
            centre = shifted[1, pl.ds(lines + j + 2, depth, stride=lines), :]
            fix[2 : 2 + depth, lanes] = fix[2 : 2 + depth, lanes] + centre
            turned = pltpu.roll(fix[:, lanes], 4 * j + 2, 1)
            border = jnp.where((lane >= 4 * j) & (lane < 4 * j + 4), turned, border)
        def pack(targets):
            for target in targets:
                packed[target] = fix[bz * target : bz * target + bz + 4, :]
                packed_rim[target] = border[bz * target : bz * target + bz + 4]

        late(lambda copy: copy.start(), pack)
        own_ref[mine] = packed[me]
        late(lambda copy: copy.wait_send())

    for k in range(ranks):
        def await_own(k=k):
            own_last(k, 0).wait_recv()
        pl.when(mine != k)(await_own)
    for dy in steps_y:
        def await_beside(dy=dy):
            halo_last(dy.back(), 0).wait_recv()
        when(dy.ok, await_beside)
    for dx in steps_x:
        def await_rims(dx=dx):
            for k in range(ranks):
                edge_last(dx.back(), k, 0).wait_recv()
        when(dx.ok, await_rims)
        for dy in steps_y:
            def await_corner(dy=dy, dx=dx):
                corner_last(dy.back(), dx.back(), 0).wait_recv()
            when(both(dy.ok, dx.ok), await_corner)
    place = lane_of((bz + 4, bx)) % 4
    for line in range(by + 4):
        if line < 2:
            slot, j = ranks, part - 2 + line
        elif line < by + 2:
            slot, j = (line - 2) // part, (line - 2) % part
        else:
            slot, j = ranks + 1, line - by - 2
        beyond = jnp.where(place < 2, x3[slot, 0], x3[slot, 1])
        edge_ref[line] = pltpu.roll(beyond, (bx - 2 - 4 * j) % bx, 1)


def segment_kernel(
    sizes, own_ref, beside_ref, edge_ref, in_left_ref, out_left_ref, out_bias_ref,
    clean_any, out_any, shifted, ready, product, result, clean, sems,
):
    gz, gy, gx = sizes
    ranks = own_ref.shape[0]
    lines, planes, bx = edge_ref.shape
    by, bz = lines - 4, planes - 4
    part = by // ranks
    me = lax.axis_index("gz")
    at_y = lax.axis_index("gy")
    at_x = lax.axis_index("gx")

    def middle_of(line):
        if 2 <= line < by + 2:
            k, j = divmod(line - 2, part)
            return own_ref[k, :, j * bx : (j + 1) * bx]
        index, j = (0, line) if line < 2 else (1, line - by - 2)
        return beside_ref[index, :, j * bx : (j + 1) * bx]

    for line in range(lines):
        store_shifts(shifted, slice(line * planes, (line + 1) * planes), middle_of(line), edge_ref[line])
    in_left = in_left_ref[...]
    out_left = out_left_ref[...]
    out_bias = out_bias_ref[:, 0:1]
    shape = (16 * (bz + 2), 2 * bx)
    lane, plane = lane_of(shape), row_of(shape) // 16
    outside = ((me == 0) & (plane == 0)) | ((me == gz - 1) & (plane == bz + 1))
    outside = outside | ((at_x == 0) & (lane == 2 * bx - 1)) | ((at_x == gx - 1) & (lane == bx))
    mask = jnp.where(outside, 0.0, 1.0).astype(F32)
    spare = jnp.ones((planes, bx), F32)
    for y in range(by + 2):
        grown = jnp.maximum(mxu(in_left, window_of(shifted, y * planes, 3 * planes, spare)), 0.0) * mask
        if y == 0:
            grown = grown * jnp.where(at_y > 0, 1.0, 0.0).astype(F32)
        if y == by + 1:
            grown = grown * jnp.where(at_y < gy - 1, 1.0, 0.0).astype(F32)
        ready[y] = grown
    for z in range(bz):
        for y in range(by):
            clean[z, y : y + 1, :] = middle_of(2 + y)[2 + z : 3 + z]
    first = pltpu.make_async_copy(clean, clean_any, sems.at[0])
    first.start()
    for y in range(by + 2):
        high, low = stacked_shifts(ready[y], bz)
        double = mxu(out_left, high)
        product[y] = double[0:48] + double[48:96] + mxu(out_left[0:48], low)
        if y >= 2:
            total = product[y - 2, 0:16] + product[y - 1, 16:32] + product[y, 32:48] + out_bias
            for z in range(bz):
                result[pl.ds(z * by + y - 2, 16, stride=bz * by), :] = total[:, z * bx : (z + 1) * bx]
    second = pltpu.make_async_copy(result.at[0 : 16 * bz * by, :], out_any, sems.at[1])
    second.start()
    first.wait()
    second.wait()


def body(sizes, noisy, first_weight, first_bias, second_weight, second_bias, head_weight,
         seg_weight_in, seg_bias_in, seg_weight_out, seg_bias_out):
    gz, gy, gx = sizes
    bz, by, bx = noisy.shape
    ranks = by // 4
    part = by // ranks
    lines = part + 4
    depth = gz * bz
    args = [
        noisy.reshape(bz * by, bx),
        first_weight.transpose(2, 1, 0),
        first_bias.reshape(1, -1),
        second_weight.transpose(2, 1, 0),
        second_bias.reshape(1, -1),
        head_weight.reshape(1, -1),
        seg_weight_in,
        seg_bias_in.reshape(1, -1),
        seg_weight_out,
        seg_bias_out.reshape(1, -1),
    ]
    vmem = pl.BlockSpec(memory_space=pltpu.VMEM)
    dma = pltpu.SemaphoreType.DMA
    rest = pl.BlockSpec(memory_space=pl.ANY)

    def room(*shape):
        return pltpu.VMEM(shape, F32)

    stages = [
        room(*(a.shape if i not in (1, 6) else (a.shape[0], a.shape[2]))) for i, a in enumerate(args)
    ]
    handed = pl.pallas_call(
        functools.partial(layers_kernel, sizes, ranks, bz, by, bx),
        out_shape=[
            room(ranks, bz + 4, part * bx),
            room(2, bz + 4, 2 * bx),
            room(by + 4, bz + 4, bx),
            pltpu.VMEM((16 * (bz + 2), 30 * (bz + 4)), BF16),
            pltpu.VMEM((96, 144), BF16),
            room(16, LANES),
        ],
        in_specs=[rest] * len(args),
        out_specs=[vmem] * 6,
        scratch_shapes=stages
        + [
            dma((len(args),)),
            room(depth * by, bx),
            room(2, depth * 2, bx),
            room(3, 2, gz, by, bx),
            room(2, bz * 2, bx),
            room(by, bx),
            dma((6, max(ranks, 2))),
            dma((9, gz)),
            room(6, (depth + 2) * lines, bx),
            room(2, bz + 1, 16 * (part + 2), 2 * bx),
            room(depth + 2, 96, part * bx),
            room(2, depth, 16, part * bx),
            room(depth + 16, part * bx),
            room(gz, bz + 4, part * bx),
            room(gz, bz + 4, bx),
            room(ranks + 2, 2, bz + 4, bx),
            dma((gz,)),
            dma((ranks,)),
            dma((2, gz)),
            dma((2,)),
            dma((2, gz)),
            dma((2, 2, gz)),
            dma((ranks + 2, 2)),
        ],
        compiler_params=pltpu.CompilerParams(
            collective_id=0, has_side_effects=True, vmem_limit_bytes=GRANT
        ),
        name="layers",
    )(*(pltpu.with_memory_space_constraint(a, pltpu.HBM) for a in args))
    clean, features = pl.pallas_call(
        functools.partial(segment_kernel, sizes),
        out_shape=[
            jax.ShapeDtypeStruct((bz, by, bx), F32),
            jax.ShapeDtypeStruct((16 * bz * by, bx), F32),
        ],
        in_specs=[vmem] * 6,
        out_specs=[rest] * 2,
        scratch_shapes=[
            room(6, (by + 4) * (bz + 4), bx),
            room(by + 2, 16 * (bz + 2), 2 * bx),
            room(by + 2, 48, bz * bx),
            room(17 * bz * by, bx),
            room(bz, by, bx),
            dma((2,)),
        ],
        compiler_params=pltpu.CompilerParams(vmem_limit_bytes=GRANT),
        name="segment",
    )(*handed)
    return clean, features.reshape(16, bz, by, bx)


def solution(mesh):
    sizes = (mesh.shape["gz"], mesh.shape["gy"], mesh.shape["gx"])
    in_specs = (P(("win", "gz"), "gy", "gx"), P(), P(), P(), P(), P(), P(), P(), P(), P())
    out_specs = (P(("win", "gz"), "gy", "gx"), P(None, ("win", "gz"), "gy", "gx"))
    return jax.shard_map(
        functools.partial(body, sizes), mesh=mesh, in_specs=in_specs, out_specs=out_specs, check_vma=False
    )
```
